32 devices in a mesh: dp: 8 (over z, x), mp: 4 (over y, core).
Axes of the slice: x: 2, y: 2, z: 4, core: 2. Of those that a mesh axis runs over, the one named last changes fastest.
Arguments:
- tokens: bfloat16 [16384, 768], P(('dp', 'mp')), may hold values from -6 to 6
- lengths: int32 [8, 16], P('dp'), may hold values from 1 to 1024, 2048 in all within a row
- w_qkv: bfloat16 [768, 3, 768], P(None, None, 'mp'), may hold values from -0.21875 to 0.21875
- w_out: bfloat16 [768, 768], P('mp'), may hold values from -0.875 to 0.875
- w_gate_up: bfloat16 [768, 2, 3072], P(None, None, 'mp'), may hold values from -0.21875 to 0.21875
- w_down: bfloat16 [3072, 768], P('mp'), may hold values from -0.109375 to 0.109375
- ln1_scale: float32 [768], replicated, may hold values from 0.5 to 1.5
- ln1_shift: float32 [768], replicated, may hold values from -2 to 2
- ln2_scale: float32 [768], replicated, may hold values from 0.5 to 1.5
- ln2_shift: float32 [768], replicated, may hold values from -2 to 2
- cotangent: bfloat16 [16384, 768], P(('dp', 'mp')), may hold values from -6 to 6
Outputs:
- output: bfloat16 [16384, 768], P(('dp', 'mp'))
- d_tokens: bfloat16 [16384, 768], P(('dp', 'mp'))
- grad_w_qkv: float32 [768, 3, 768], P(None, None, 'mp')
- grad_w_out: float32 [768, 768], P('mp')
- grad_w_gate_up: float32 [768, 2, 3072], P(None, None, 'mp')
- grad_w_down: float32 [3072, 768], P('mp')
- grad_ln1_scale: float32 [768], P('mp')
- grad_ln1_shift: float32 [768], P('mp')
- grad_ln2_scale: float32 [768], P('mp')
- grad_ln2_shift: float32 [768], P('mp')
The draws below stay inside these ranges and needn't reach their ends.
Inputs may be any that keep to these rules, and one draw needn't show every extreme that they name: The 16 lengths of each row sum to 2048, and each row's longest is exactly 1024.
All inputs are finite; a program needn't handle non-finite values.
Results may differ from the reference program's by a relative error of at most 0.024.
Values may be sent and summed in bfloat16 or wider, within the bound.
A program may use at most 192 MiB of HBM per device.

```python
import math
import jax
import jax.numpy as jnp
import numpy as np
from jax import lax

D = 768
HEADS = 12
HEAD_DIM = 64
FF = 3072
ROW_LEN = 2048
DOCS = 16
DOC_MOST = 1024
ROWS = 8
TOKENS = 16384


def shard_levels(stream_key, dims, pieces, smallest, top_value):
    level, own = 1.0, jax.random.fold_in(stream_key, 6)
    for dim, shards_of in pieces:
        draws = jnp.exp(jax.random.uniform(jax.random.fold_in(own, dim), (shards_of,), jnp.float32, smallest / len(pieces), top_value / len(pieces)))
        level = level * jnp.repeat(draws, dims[dim] // shards_of).reshape([-1 if axis == dim else 1 for axis in range(len(dims))])
    return level


def split_up(count, total, most, slope):
    weights = [(1 << 20) // math.isqrt(rank ** slope) + 1 for rank in range(2, count + 1)]
    rest, counts = total - most - (count - 1), [1] * (count - 1)
    while rest > 0:
        free = [i for i in range(count - 1) if counts[i] < most]
        pool, remaining = sum([weights[i] for i in free]), rest
        for i in free:
            more = min(most - counts[i], max(1, remaining * weights[i] // pool), rest)
            counts[i] = counts[i] + more
            rest = rest - more
    return np.array([most] + counts)


def uneven_parts(key, amount, total, reach, lean):
    if amount == 2:
        one = jax.random.randint(key, (), max(1, total - reach), min(reach, total - 1) + 1)
        return jnp.stack([one, total - one])
    sizes = jnp.asarray(split_up(amount, total, reach, lean), jnp.int32)
    twos = (amount - 1) // 2
    giver, sink = sizes[1:1 + 2 * twos:2], sizes[2:2 + 2 * twos:2]
    room = jnp.minimum(giver - 1, reach - sink)
    passed = jax.random.randint(jax.random.fold_in(key, 1), (twos,), 0, 1 << 20) % (room + 1)
    sizes = sizes.at[1:1 + 2 * twos:2].set(giver - passed).at[2:2 + 2 * twos:2].set(sink + passed)
    return sizes[jax.random.permutation(jax.random.fold_in(key, 2), amount)]


def bell_draw(stream_key, extent, deviation, most, shards=(), held_as=jnp.bfloat16):
    array = jax.random.normal(stream_key, extent, jnp.float32) * deviation
    if len(shards) > 0:
        array = shard_levels(stream_key, extent, shards, -0.22, 0.18) * array
    return jnp.clip(array, min=-most, max=most).astype(held_as)


def setup_inputs(seed: int = 0) -> dict:
    seeds = jax.random.split(jax.random.key(seed), 12)
    tokens = bell_draw(seeds[0], (TOKENS, D), 1.0, 6.0, ((0, 32),))
    lengths = jax.vmap(lambda own: uneven_parts(own, DOCS, ROW_LEN, DOC_MOST, 2))(jax.random.split(seeds[1], ROWS)).reshape((ROWS, DOCS)).astype(jnp.int32)
    w_qkv = bell_draw(seeds[2], (D, 3, D), D ** -0.5, 0.21875, ((2, 4),))
    w_out = bell_draw(seeds[3], (D, D), (D // 16) ** -0.5, 0.875, ((0, 4),))
    w_gate_up = bell_draw(seeds[4], (D, 2, FF), D ** -0.5, 0.21875, ((2, 4),))
    w_down = bell_draw(seeds[5], (FF, D), FF ** -0.5, 0.109375, ((0, 4),))
    ln1_scale = jnp.clip(1.0 + 0.1 * jax.random.normal(seeds[6], (D,), jnp.float32), 0.5, 1.5)
    ln1_shift = bell_draw(seeds[7], (D,), 0.3, 2.0, (), jnp.float32)
    ln2_scale = jnp.clip(1.0 + 0.1 * jax.random.normal(seeds[8], (D,), jnp.float32), 0.5, 1.5)
    ln2_shift = bell_draw(seeds[9], (D,), 0.3, 2.0, (), jnp.float32)
    cotangent = bell_draw(seeds[10], (TOKENS, D), 1.0, 6.0, ((0, 32),))
    return dict(tokens=tokens, lengths=lengths, w_qkv=w_qkv, w_out=w_out, w_gate_up=w_gate_up, w_down=w_down, ln1_scale=ln1_scale, ln1_shift=ln1_shift, ln2_scale=ln2_scale, ln2_shift=ln2_shift, cotangent=cotangent)


@jax.custom_vjp
def low(v):
    return lax.optimization_barrier(v.astype(jnp.bfloat16)).astype(jnp.float32)

@jax.custom_vjp
def low_back(v):
    return v

def low_keep(v):
    return (low(v), None)

def low_pass(kept, grad):
    return (grad,)

def back_keep(v):
    return (v, None)

def back_low(kept, grad):
    return (low(grad),)
low.defvjp(low_keep, low_pass)
low_back.defvjp(back_keep, back_low)
EPSILON = 1e-05
PRECISE = lax.Precision.HIGHEST

def layer_norm(values, scale, shift):
    centred = values - lax.optimization_barrier(jnp.mean(values, axis=-1, keepdims=True))
    spread = lax.optimization_barrier(jnp.mean(centred * centred, axis=-1, keepdims=True))
    return centred * lax.rsqrt(spread + EPSILON) * scale + shift

def doc_layout(lengths_row):
    places = jnp.arange(ROW_LEN, dtype=jnp.int32)
    doc_ends = jnp.cumsum(lengths_row).astype(jnp.int32)
    seg_ids = lax.optimization_barrier(jnp.sum((places[:, None] >= doc_ends[None, :]).astype(jnp.int32), axis=1)).astype(jnp.int32)
    doc_starts = (doc_ends - lengths_row).astype(jnp.int32)
    one_hot = seg_ids[:, None] == jnp.arange(lengths_row.shape[0], dtype=jnp.int32)[None, :]
    first_pos = lax.optimization_barrier(jnp.sum(jnp.where(one_hot, doc_starts[None, :], 0), axis=1)).astype(jnp.int32)
    return (seg_ids, (places - first_pos).astype(jnp.int32))

def rotary_tables(positions):
    angle_rate = jnp.exp(jnp.arange(HEAD_DIM // 2, dtype=jnp.float32) * (-2.0 * math.log(1000.0) / HEAD_DIM))
    angles = positions.astype(jnp.float32)[..., None] * angle_rate
    cosine = jnp.concatenate([jnp.cos(angles), jnp.cos(angles)], axis=-1)[..., None, :]
    sine_val = jnp.concatenate([jnp.sin(angles), jnp.sin(angles)], axis=-1)[..., None, :]
    return (cosine, sine_val)

def rotate(values, cosine, sine_val):
    half_dim = values.shape[-1] // 2
    turned = jnp.concatenate([-values[..., half_dim:], values[..., :half_dim]], axis=-1)
    return values * cosine + turned * sine_val

def row_forward(x_row, lengths_row, w_qkv, w_out, w_gate_up, w_down, ln1_scale, ln1_shift, ln2_scale, ln2_shift):
    seg_ids, positions = doc_layout(lengths_row)
    cosine, sine_val = rotary_tables(positions)
    projected = low_back(jnp.dot(x_row, w_qkv.reshape(D, 3 * D), precision=PRECISE))
    projected = projected.reshape(ROW_LEN, 3, HEADS, HEAD_DIM)
    queries = low(rotate(projected[:, 0], cosine, sine_val))
    keys_all = low(rotate(projected[:, 1], cosine, sine_val))
    values_all = low(projected[:, 2])
    block_rows = min(512, ROW_LEN)
    scale_qk = 1.0 / math.sqrt(HEAD_DIM)

    def attend(pair):
        q_block, q_seg = pair
        scores = low_back(jnp.einsum('qhd,khd->hqk', q_block, keys_all, precision=PRECISE) * scale_qk)
        scores = jnp.where((q_seg[:, None] == seg_ids[None, :])[None], scores, -1e+30)
        row_top = lax.optimization_barrier(jnp.max(scores, axis=-1, keepdims=True))
        exp_terms = jnp.exp(scores - row_top)
        attention = exp_terms / lax.optimization_barrier(jnp.sum(exp_terms, axis=-1, keepdims=True))
        return jnp.einsum('hqk,khd->qhd', low(attention), values_all, precision=PRECISE)
    attended = lax.map(jax.checkpoint(attend), (queries.reshape(ROW_LEN // block_rows, block_rows, HEADS, HEAD_DIM), seg_ids.reshape(ROW_LEN // block_rows, block_rows)))
    attended = low(low_back(attended.reshape(ROW_LEN, D)))
    branch = low_back(jnp.dot(attended, w_out, precision=PRECISE))
    normed = layer_norm(x_row + branch, ln1_scale, ln1_shift)
    gate_up = jnp.dot(low(normed), w_gate_up.reshape(D, 2 * FF), precision=PRECISE)
    gate_val = low_back(gate_up[:, :FF])
    up_val = low_back(gate_up[:, FF:])
    hidden = low(gate_val * jax.nn.sigmoid(gate_val) * up_val)
    mlp_out = low_back(jnp.dot(hidden, w_down, precision=PRECISE))
    return layer_norm(normed + mlp_out, ln2_scale, ln2_shift)

def reference(tokens, lengths, w_qkv, w_out, w_gate_up, w_down, ln1_scale, ln1_shift, ln2_scale, ln2_shift, cotangent):
    x_rows = tokens.astype(jnp.float32).reshape(ROWS, ROW_LEN, D)

    def whole(inputs, wq_all, wo_all, wgu_all, wd_all, scale_one, shift_one, scale_two, shift_two):

        def one_row(pair):
            return row_forward(pair[0], pair[1], wq_all, wo_all, wgu_all, wd_all, scale_one, shift_one, scale_two, shift_two)
        return lax.map(jax.checkpoint(one_row), (inputs, lengths))
    outputs, pullback = jax.vjp(whole, x_rows, w_qkv.astype(jnp.float32), w_out.astype(jnp.float32), w_gate_up.astype(jnp.float32), w_down.astype(jnp.float32), ln1_scale.astype(jnp.float32), ln1_shift.astype(jnp.float32), ln2_scale.astype(jnp.float32), ln2_shift.astype(jnp.float32))
    grads = pullback(cotangent.astype(jnp.float32).reshape(ROWS, ROW_LEN, D))
    return (outputs.reshape(TOKENS, D).astype(jnp.bfloat16), grads[0].reshape(TOKENS, D).astype(jnp.bfloat16), grads[1], grads[2], grads[3], grads[4], grads[5], grads[6], grads[7], grads[8])
```

```python
import functools
import math

import jax
import jax.numpy as jnp
from jax import lax
from jax.experimental import pallas as pl
from jax.experimental.pallas import tpu as pltpu
from jax.sharding import PartitionSpec as P

F32 = jnp.float32
BF16 = jnp.bfloat16
HEAD_DIM = 64
LANES = 128
EPSILON = 1e-05
BLOCK = 256
SEG_COL = 64
SHIFT_COL = 80
FAR = -(2.0**100)
LOG2E = math.log2(math.e)
NT = (((1,), (1,)), ((), ()))
TN = (((0,), (0,)), ((), ()))
NN = (((1,), (0,)), ((), ()))
VMEM_LIMIT = 58 << 20


def mm(a, b, dims=NN):
    return lax.dot_general(a, b, dims, preferred_element_type=F32)


def lane_iota(rows):
    return lax.broadcasted_iota(jnp.int32, (rows, LANES), 1)


def thirds(column):
    high = column.astype(BF16)
    rest = column - high.astype(F32)
    mid = rest.astype(BF16)
    low = (rest - mid.astype(F32)).astype(BF16)
    return high.astype(F32), mid.astype(F32), low.astype(F32)


def shift_columns(column, first, lanes):
    high, mid, low = thirds(column)
    terms = jnp.where(lanes == first, high, 0.0)
    terms = jnp.where(lanes == first + 1, mid, terms)
    return jnp.where(lanes == first + 2, low, terms)


def turn(values, lanes):
    width = values.shape[-1]
    left = pltpu.roll(values, width - 32, 1)
    right = pltpu.roll(values, 32, 1)
    return jnp.where((lanes & 63) < 32, left, right)


def qkv_kernel(place, x_ref, w_ref, cos_ref, sin_ref, bounds_ref, q_ref, k_ref, v_ref):
    rows = x_ref.shape[1]
    heads = q_ref.shape[0]
    width = heads * HEAD_DIM
    shard = place[0] ^ place[1 + pl.program_id(0)]
    tile = BLOCK
    lanes = lane_iota(tile)
    for part in range(rows // tile):
        piece = pl.ds(part * tile, tile)
        projected = mm(x_ref[0, piece, :], w_ref[...])
        cosine, sine = cos_ref[piece, :], sin_ref[piece, :]
        token = lax.broadcasted_iota(jnp.int32, (tile, LANES), 0) + (shard * rows + part * tile)
        inside = (token >= bounds_ref[0:1, :]) & (token < bounds_ref[1:2, :])
        slot = (lanes >= SEG_COL) & (lanes < SHIFT_COL)
        q_tail = jnp.where(slot & ~inside, FAR, 0.0)
        k_tail = jnp.where((slot & inside) | ((lanes >= SHIFT_COL) & (lanes < SHIFT_COL + 3)), 1.0, 0.0)
        v_tail = jnp.where((lanes >= HEAD_DIM) & (lanes < HEAD_DIM + 3), 1.0, 0.0)

        def head_of(column):
            start = column // LANES * LANES
            pair = projected[:, start : min(start + LANES, 3 * width)]
            if pair.shape[1] < LANES:
                pair = jnp.concatenate([pair, pair], axis=1)
            return pair if column % LANES == 0 else pltpu.roll(pair, HEAD_DIM, 1)

        for h in range(heads):
            q = head_of(h * HEAD_DIM)
            q = (q * cosine + turn(q, lanes) * sine) * (LOG2E / math.sqrt(HEAD_DIM))
            q_ref[h, piece, :] = jnp.where(lanes < HEAD_DIM, q, q_tail).astype(BF16)
            k = head_of(width + h * HEAD_DIM)
            k = k * cosine + turn(k, lanes) * sine
            k_ref[h, piece, :] = jnp.where(lanes < HEAD_DIM, k, k_tail).astype(BF16)
            v = head_of(2 * width + h * HEAD_DIM)
            v_ref[h, piece, :] = jnp.where(lanes < HEAD_DIM, v, v_tail).astype(BF16)


def project(x_slots, w_flat, cosine, sine, bounds, place, heads):
    count, rows, width = x_slots.shape
    tokens = count * rows
    out = jax.ShapeDtypeStruct((heads, tokens, LANES), BF16)
    whole = lambda *shape: pl.BlockSpec(shape, lambda s, place: (0,) * len(shape))
    by_shard = pl.BlockSpec((rows, LANES), lambda s, place: (place[0] ^ place[1 + s], 0))
    head_spec = pl.BlockSpec((heads, rows, LANES), lambda s, place: (0, place[0] ^ place[1 + s], 0))
    return pl.pallas_call(
        qkv_kernel,
        out_shape=(out, out, out),
        grid_spec=pltpu.PrefetchScalarGridSpec(
            num_scalar_prefetch=1,
            grid=(count,),
            in_specs=[
                pl.BlockSpec((1, rows, width), lambda s, place: (s, 0, 0)),
                whole(*w_flat.shape),
                by_shard,
                by_shard,
                whole(*bounds.shape),
            ],
            out_specs=[head_spec] * 3,
        ),
        compiler_params=pltpu.CompilerParams(vmem_limit_bytes=VMEM_LIMIT),
        cost_estimate=pl.CostEstimate(
            flops=2 * tokens * width * w_flat.shape[1],
            bytes_accessed=tokens * width * 2 + 3 * heads * tokens * LANES * 2,
            transcendentals=0,
        ),
        name="project",
    )(place, x_slots, w_flat, cosine, sine, bounds)


def attend_kernel(place, ranges, q_ref, k_ref, v_ref, o_ref, qb_ref, top_ref, acc_ref):
    heads = q_ref.shape[0]
    i = pl.program_id(0)
    blocks = pl.num_programs(0)
    first, last = ranges[i], ranges[blocks + i]
    lanes = lane_iota(BLOCK)
    top_ref[...] = jnp.full_like(top_ref, FAR)
    acc_ref[...] = jnp.zeros_like(acc_ref)

    def find_top(j, carry):
        rows = pl.ds(pl.multiple_of(j * BLOCK, BLOCK), BLOCK)
        for h in range(heads):
            s = mm(q_ref[h], k_ref[h, rows, :], NT)
            top_ref[h] = jnp.maximum(top_ref[h], jnp.maximum(s[:, :LANES], s[:, LANES:]))
        return carry

    lax.fori_loop(first, last + 1, find_top, 0)
    tops = []
    for h in range(heads):
        top = jnp.max(top_ref[h], axis=1, keepdims=True)
        tops.append(top)
        qb_ref[h] = q_ref[h] + shift_columns(-top, SHIFT_COL, lanes).astype(BF16)

    def add_up(j, carry):
        rows = pl.ds(pl.multiple_of(j * BLOCK, BLOCK), BLOCK)
        for h in range(heads):
            s = mm(qb_ref[h], k_ref[h, rows, :], NT)
            acc_ref[h] += mm(jnp.exp2(s).astype(BF16), v_ref[h, rows, :])
        return carry

    lax.fori_loop(first, last + 1, add_up, 0)
    for h in range(heads):
        total = acc_ref[h, :, HEAD_DIM : HEAD_DIM + 1]
        o_ref[0, :, h * HEAD_DIM : (h + 1) * HEAD_DIM] = (acc_ref[h, :, :HEAD_DIM] / total).astype(BF16)
        level = tops[h] + jnp.log2(total)
        qb_ref[h] = q_ref[h] + shift_columns(-level, SHIFT_COL, lanes).astype(BF16)


def slot_of(relative):
    return (relative >> 1) | ((relative & 1) << 1)


def attend(q, k, v, place, ranges, shards):
    heads, tokens, _ = q.shape
    blocks = tokens // BLOCK
    rows = tokens // shards
    per = rows // BLOCK
    whole = pl.BlockSpec((heads, tokens, LANES), lambda i, place, ranges: (0, 0, 0))
    mine = pl.BlockSpec((heads, BLOCK, LANES), lambda i, place, ranges: (0, i, 0))
    return pl.pallas_call(
        attend_kernel,
        out_shape=(
            jax.ShapeDtypeStruct((shards, rows, heads * HEAD_DIM), BF16),
            jax.ShapeDtypeStruct((heads, tokens, LANES), BF16),
        ),
        grid_spec=pltpu.PrefetchScalarGridSpec(
            num_scalar_prefetch=2,
            grid=(blocks,),
            in_specs=[mine, whole, whole],
            out_specs=[
                pl.BlockSpec(
                    (1, BLOCK, heads * HEAD_DIM),
                    lambda i, place, ranges: (slot_of((i // per) ^ place[0]), i % per, 0),
                ),
                mine,
            ],
            scratch_shapes=[pltpu.VMEM((heads, BLOCK, LANES), F32), pltpu.VMEM((heads, BLOCK, LANES), F32)],
        ),
        compiler_params=pltpu.CompilerParams(vmem_limit_bytes=VMEM_LIMIT),
        cost_estimate=pl.CostEstimate(
            flops=3 * heads * tokens * tokens * LANES,
            bytes_accessed=5 * heads * tokens * LANES * 2,
            transcendentals=heads * tokens * tokens // 2,
        ),
        name="attend",
    )(place, ranges, q, k, v)


def attend_back_kernel(
    place, ranges, qb_ref, k_ref, v_ref, att_ref, dh_ref, w_ref, cos_ref, sin_ref, out_ref, do_ref, dq_ref, dk_ref, dv_ref
):
    heads, tokens, _ = qb_ref.shape
    shards, rows, _ = att_ref.shape
    blocks = tokens // BLOCK
    per = rows // BLOCK
    width = heads * HEAD_DIM
    lanes = lane_iota(BLOCK)

    def place_of(i):
        return slot_of((i // per) ^ place[0]), pl.ds(pl.multiple_of((i % per) * BLOCK, BLOCK), BLOCK)

    def rows_of(i):
        return pl.ds(pl.multiple_of(i * BLOCK, BLOCK), BLOCK)

    def prepare(i, carry):
        slot, piece = place_of(i)
        d_att = mm(dh_ref[slot, piece, :], w_ref[...], NT)
        for h in range(heads):
            d_head = d_att[:, h * LANES : (h + 1) * LANES].astype(BF16).astype(F32)
            own = att_ref[slot, piece, h * HEAD_DIM : (h + 1) * HEAD_DIM].astype(F32)
            dot = jnp.sum(d_head[:, :HEAD_DIM] * own, axis=1, keepdims=True)
            do_ref[h, rows_of(i), :] = (d_head + shift_columns(-dot, HEAD_DIM, lanes)).astype(BF16)
        return carry

    lax.fori_loop(0, blocks, prepare, 0)
    dq_ref[...] = jnp.zeros_like(dq_ref)

    def rotate_back(values, where):
        return values * cos_ref[where, :] - turn(values, lanes) * sin_ref[where, :]

    def over_keys(j, carry):
        keys = rows_of(j)
        dk_ref[...] = jnp.zeros_like(dk_ref)
        dv_ref[...] = jnp.zeros_like(dv_ref)

        def over_queries(i, carry):
            queries = rows_of(i)
            for h in range(heads):
                k, q, d_out = k_ref[h, keys, :], qb_ref[h, queries, :], do_ref[h, queries, :]
                probs = jnp.exp2(mm(k, q, NT))
                d_scores = (probs * mm(v_ref[h, keys, :], d_out, NT)).astype(BF16)
                dv_ref[h] += mm(probs.astype(BF16), d_out)
                dk_ref[h] += mm(d_scores, q)
                dq_ref[h, queries, :] += mm(d_scores, k, TN)
            return carry

        lax.fori_loop(ranges[j], ranges[blocks + j] + 1, over_queries, 0)
        slot, piece = place_of(j)
        for h in range(heads):
            d_key = rotate_back(dk_ref[h] * (1.0 / LOG2E), keys)
            column = width + h * HEAD_DIM
            out_ref[slot, piece, column : column + HEAD_DIM] = d_key[:, :HEAD_DIM].astype(BF16)
            column = 2 * width + h * HEAD_DIM
            out_ref[slot, piece, column : column + HEAD_DIM] = dv_ref[h, :, :HEAD_DIM].astype(BF16)
        return carry

    lax.fori_loop(0, blocks, over_keys, 0)

    def finish(i, carry):
        slot, piece = place_of(i)
        for h in range(heads):
            d_query = rotate_back(dq_ref[h, rows_of(i), :] * (1.0 / math.sqrt(HEAD_DIM)), rows_of(i))
            out_ref[slot, piece, h * HEAD_DIM : (h + 1) * HEAD_DIM] = d_query[:, :HEAD_DIM].astype(BF16)
        return carry

    lax.fori_loop(0, blocks, finish, 0)


def attend_back(qb, k, v, att, dh_slots, w_out, cosine, sine, place, ranges):
    heads, tokens, _ = qb.shape
    shards, rows, _ = att.shape
    w_wide = jnp.pad(w_out.reshape(heads, HEAD_DIM, -1), ((0, 0), (0, LANES - HEAD_DIM), (0, 0)))
    w_wide = w_wide.reshape(heads * LANES, -1)
    vmem = pl.BlockSpec(memory_space=pltpu.VMEM)
    smem = pl.BlockSpec(memory_space=pltpu.SMEM)
    return pl.pallas_call(
        attend_back_kernel,
        out_shape=jax.ShapeDtypeStruct((shards, rows, 3 * heads * HEAD_DIM), BF16),
        in_specs=[smem, smem] + [vmem] * 8,
        out_specs=vmem,
        scratch_shapes=[
            pltpu.VMEM((heads, tokens, LANES), BF16),
            pltpu.VMEM((heads, tokens, LANES), F32),
            pltpu.VMEM((heads, BLOCK, LANES), F32),
            pltpu.VMEM((heads, BLOCK, LANES), F32),
        ],
        compiler_params=pltpu.CompilerParams(vmem_limit_bytes=VMEM_LIMIT),
        cost_estimate=pl.CostEstimate(
            flops=5 * heads * tokens * tokens * LANES,
            bytes_accessed=6 * heads * tokens * LANES * 2,
            transcendentals=heads * tokens * tokens // 2,
        ),
        name="attend_back",
    )(place, ranges, qb, k, v, att, dh_slots, w_wide, cosine, sine)


def doc_tables(lengths, tokens, blocks):
    ends = jnp.cumsum(lengths)
    starts = ends - lengths
    places = jnp.arange(tokens, dtype=jnp.int32)
    inside = (places[:, None] >= starts[None, :]) & (places[:, None] < ends[None, :])
    positions = places - jnp.sum(jnp.where(inside, starts[None, :], 0), axis=1)
    edge = jnp.arange(blocks, dtype=jnp.int32) * BLOCK
    touches = (starts[None, :] < edge[:, None] + BLOCK) & (ends[None, :] > edge[:, None])
    first = jnp.min(jnp.where(touches, starts[None, :], tokens), axis=1) // BLOCK
    last = (jnp.max(jnp.where(touches, ends[None, :], 0), axis=1) - 1) // BLOCK
    ranges = jnp.concatenate([first, last]).astype(jnp.int32)
    pad = (SEG_COL, LANES - SEG_COL - lengths.shape[0])
    bounds = jnp.stack([jnp.pad(starts, pad), jnp.pad(ends, pad)]).astype(jnp.int32)
    return positions, ranges, jnp.pad(bounds, ((0, 6), (0, 0)))


def rotary(positions):
    lane = jnp.arange(LANES, dtype=jnp.int32)
    rate = jnp.exp((lane & 31).astype(F32) * (-2.0 * math.log(1000.0) / HEAD_DIM))
    angles = positions.astype(F32)[:, None] * rate[None, :]
    sign = jnp.where((lane & 63) < 32, -1.0, 1.0)
    return jnp.cos(angles), jnp.sin(angles) * sign[None, :]


def reduce_over_dp(total, bits, me):
    size = lax.axis_size("dp")

    def exchange(values, bit):
        return lax.ppermute(values, "dp", [(i, i ^ (1 << bit)) for i in range(size)])

    for bit in bits:
        half = total.shape[0] // 2
        mine = (me >> bit) & 1
        give = lax.dynamic_slice_in_dim(total, (1 - mine) * half, half, 0).astype(BF16)
        keep = lax.dynamic_slice_in_dim(total, mine * half, half, 0)
        total = keep + exchange(give, bit).astype(F32)
    total = total.astype(BF16)
    for bit in reversed(bits):
        mine = (me >> bit) & 1
        other = exchange(total, bit)
        total = jnp.where(mine == 0, jnp.concatenate([total, other]), jnp.concatenate([other, total]))
    return total


def body(
    tokens, lengths, w_qkv, w_out, w_gate_up, w_down, ln1_scale, ln1_shift, ln2_scale, ln2_shift, cotangent
):
    rows, width = tokens.shape
    shards = lax.axis_size("mp")
    length = rows * shards
    local_cols = w_out.shape[0]
    heads = local_cols // HEAD_DIM
    hidden_cols = w_down.shape[0]
    m = lax.axis_index("mp")
    dp_bits = list(range(int(math.log2(lax.axis_size("dp")))))
    me = lax.axis_index("dp")

    def swap(values, distance):
        return lax.ppermute(values, "mp", [(i, i ^ distance) for i in range(shards)])

    across = lambda values: swap(values, 2)
    beside = lambda values: swap(values, 1)

    x_far = across(tokens)
    x_near = beside(tokens)
    x_last = beside(x_far)
    positions, ranges, bounds = doc_tables(lengths[0], length, length // BLOCK)
    cosine, sine = rotary(positions)
    place = jnp.stack([m.astype(jnp.int32)] + [jnp.int32(r) for r in (0, 2, 1, 3)])
    flat_qkv = w_qkv.reshape(width, 3 * local_cols)
    w_qkv_near = beside(flat_qkv)
    w_out_near = beside(w_out)
    flat_gate_up = w_gate_up.reshape(width, 2 * hidden_cols)
    w_gate_up_near = beside(flat_gate_up)
    w_down_near = beside(w_down)
    x_slots = jnp.stack([tokens, x_far, x_near, x_last])
    q, k, v = project(x_slots, flat_qkv, cosine, sine, bounds, place, heads)
    att, qb = attend(q, k, v, place, ranges, shards)
    att_near = beside(att[2:])

    def out_project(index):
        return mm(att[index], w_out) + mm(att_near[index], w_out_near)

    branch_far = across(out_project(1).astype(BF16))
    h = tokens.astype(F32) + out_project(0) + branch_far.astype(F32)
    h = h - jnp.mean(h, axis=-1, keepdims=True)
    r1 = lax.rsqrt(jnp.mean(h * h, axis=-1, keepdims=True) + EPSILON)
    h_hat = h * r1
    normed = h_hat * ln1_scale + ln1_shift
    normed_low = normed.astype(BF16)
    normed_far = across(normed_low)

    w_ins, w_downs = (flat_gate_up, w_gate_up_near), (w_down, w_down_near)

    def mlp(values):
        kept, partial = [], 0.0
        for w_in, w_back in zip(w_ins, w_downs):
            gate_up = mm(values, w_in)
            gate, up = gate_up[:, :hidden_cols], gate_up[:, hidden_cols:]
            hidden = (gate * jax.nn.sigmoid(gate) * up).astype(BF16)
            partial = partial + mm(hidden, w_back)
            kept.append((gate_up.astype(BF16), hidden))
        return partial, kept

    partial_own, kept_own = mlp(normed_low)
    partial_far, kept_far = mlp(normed_far)
    mlp_far = across(partial_far.astype(BF16))
    z = normed + partial_own + mlp_far.astype(F32)
    z = z - jnp.mean(z, axis=-1, keepdims=True)
    r2 = lax.rsqrt(jnp.mean(z * z, axis=-1, keepdims=True) + EPSILON)
    z_hat = z * r2
    output = (z_hat * ln2_scale + ln2_shift).astype(BF16)
    g = cotangent.astype(F32)
    e = g * ln2_scale
    dz = r2 * (e - jnp.mean(e, axis=-1, keepdims=True) - z_hat * jnp.mean(e * z_hat, axis=-1, keepdims=True))
    d_scale_two, d_shift_two = jnp.sum(g * z_hat, axis=0), jnp.sum(g, axis=0)
    dz_low = dz.astype(BF16)
    dz_far = across(dz_low)

    def mlp_back(d_out, kept):
        d_normed, d_ins = 0.0, []
        for (gate_up, hidden), w_in, w_back in zip(kept, w_ins, w_downs):
            gate, up = gate_up[:, :hidden_cols].astype(F32), gate_up[:, hidden_cols:].astype(F32)
            d_hidden = mm(d_out, w_back, NT)
            s = jax.nn.sigmoid(gate)
            d_gate = (d_hidden * up * s * (1.0 + gate * (1.0 - s))).astype(BF16)
            d_up = (d_hidden * gate * s).astype(BF16)
            d_in = jnp.concatenate([d_gate, d_up], axis=1)
            d_normed = d_normed + mm(d_in, w_in, NT)
            d_ins.append(d_in)
        return d_normed, d_ins

    d_own, d_ins_own = mlp_back(dz_low, kept_own)
    d_far, d_ins_far = mlp_back(dz_far, kept_far)
    d_normed_far = across(d_far.astype(BF16))

    def weight_grads(core):
        down = mm(kept_own[core][1], dz_low, TN) + mm(kept_far[core][1], dz_far, TN)
        gate_up = mm(normed_low, d_ins_own[core], TN) + mm(normed_far, d_ins_far[core], TN)
        return gate_up, down

    grad_gate_up, grad_down = weight_grads(1)
    grad_gate_up_near, grad_down_near = beside(grad_gate_up.astype(BF16)), beside(grad_down.astype(BF16))
    grad_gate_up, grad_down = weight_grads(0)
    grad_gate_up = grad_gate_up + grad_gate_up_near.astype(F32)
    grad_down = grad_down + grad_down_near.astype(F32)
    swapped = [dp_bits[1], dp_bits[0]] + dp_bits[2:] if len(dp_bits) > 1 else dp_bits
    half = width // 2
    grad_gate_up = jnp.concatenate(
        [reduce_over_dp(grad_gate_up[:half], dp_bits, me), reduce_over_dp(grad_gate_up[half:], swapped, me)]
    ).astype(F32)
    grad_down = jnp.concatenate(
        [
            reduce_over_dp(grad_down[: hidden_cols // 2], dp_bits, me),
            reduce_over_dp(grad_down[hidden_cols // 2 :], swapped, me),
        ]
    ).astype(F32)

    d_normed = dz + d_own + d_normed_far.astype(F32)
    e1 = d_normed * ln1_scale
    dh = r1 * (e1 - jnp.mean(e1, axis=-1, keepdims=True) - h_hat * jnp.mean(e1 * h_hat, axis=-1, keepdims=True))
    d_scale_one, d_shift_one = jnp.sum(d_normed * h_hat, axis=0), jnp.sum(d_normed, axis=0)
    dh_low = dh.astype(BF16)
    dh_far = across(dh_low)
    dh_near = beside(dh_low)
    dh_last = beside(dh_far)
    dh_slots = jnp.stack([dh_low, dh_far, dh_near, dh_last])
    d_qkv = attend_back(qb, k, v, att, dh_slots, w_out, cosine, sine, place, ranges)
    grad_out = mm(att.reshape(length, local_cols), dh_slots.reshape(length, width), TN)
    d_qkv_near = beside(d_qkv[2:])
    d_x_far = mm(d_qkv[1], flat_qkv, NT) + mm(d_qkv_near[1], w_qkv_near, NT)
    d_x_far = across(d_x_far.astype(BF16))
    d_x_own = mm(d_qkv[0], flat_qkv, NT) + mm(d_qkv_near[0], w_qkv_near, NT)
    grad_qkv = mm(x_slots.reshape(length, width), d_qkv.reshape(length, 3 * local_cols), TN)
    d_tokens = (dh + d_x_own + d_x_far.astype(F32)).astype(BF16)
    grad_qkv = jnp.concatenate(
        [reduce_over_dp(grad_qkv[:half], dp_bits, me), reduce_over_dp(grad_qkv[half:], swapped, me)]
    ).astype(F32)
    grad_out = reduce_over_dp(grad_out, swapped, me).astype(F32)
    norms = lax.psum(jnp.stack([d_scale_one, d_shift_one, d_scale_two, d_shift_two]), ("dp", "mp"))
    norms = lax.dynamic_slice_in_dim(norms, m * local_cols, local_cols, 1)
    return (
        output,
        d_tokens,
        grad_qkv.reshape(width, 3, local_cols),
        grad_out,
        grad_gate_up.reshape(width, 2, hidden_cols),
        grad_down,
        norms[0],
        norms[1],
        norms[2],
        norms[3],
    )


def solution(mesh):
    return jax.shard_map(
        body,
        mesh=mesh,
        in_specs=(
            P(("dp", "mp"), None),
            P("dp", None),
            P(None, None, "mp"),
            P("mp", None),
            P(None, None, "mp"),
            P("mp", None),
            P(),
            P(),
            P(),
            P(),
            P(("dp", "mp"), None),
        ),
        out_specs=(
            P(("dp", "mp"), None),
            P(("dp", "mp"), None),
            P(None, None, "mp"),
            P("mp", None),
            P(None, None, "mp"),
            P("mp", None),
            P("mp"),
            P("mp"),
            P("mp"),
            P("mp"),
        ),
        check_vma=False,
    )
```

```python
import functools
import math

import jax
import jax.numpy as jnp
from jax import lax
from jax.experimental import pallas as pl
from jax.experimental.pallas import tpu as pltpu
from jax.sharding import PartitionSpec as P

F32 = jnp.float32
BF16 = jnp.bfloat16
HEAD_DIM = 64
LANES = 128
EPSILON = 1e-05
BLOCK = 256
SEG_COL = 64
SHIFT_COL = 80
FAR = -(2.0**100)
LOG2E = math.log2(math.e)
NT = (((1,), (1,)), ((), ()))
TN = (((0,), (0,)), ((), ()))
NN = (((1,), (0,)), ((), ()))
VMEM_LIMIT = 58 << 20
MESH = pl.DeviceIdType.MESH


def mm(a, b, dims=NN):
    return lax.dot_general(a, b, dims, preferred_element_type=F32)


def lane_iota(rows):
    return lax.broadcasted_iota(jnp.int32, (rows, LANES), 1)


def thirds(column):
    high = column.astype(BF16)
    rest = column - high.astype(F32)
    mid = rest.astype(BF16)
    low = (rest - mid.astype(F32)).astype(BF16)
    return high.astype(F32), mid.astype(F32), low.astype(F32)


def shift_columns(column, first, lanes):
    high, mid, low = thirds(column)
    terms = jnp.where(lanes == first, high, 0.0)
    terms = jnp.where(lanes == first + 1, mid, terms)
    return jnp.where(lanes == first + 2, low, terms)


def turn(values, lanes):
    width = values.shape[-1]
    left = pltpu.roll(values, width - 32, 1)
    right = pltpu.roll(values, 32, 1)
    return jnp.where((lanes & 63) < 32, left, right)


def qkv_kernel(place, x_ref, w_ref, cos_ref, sin_ref, bounds_ref, q_ref, k_ref, v_ref):
    rows = x_ref.shape[1]
    heads = q_ref.shape[0]
    width = heads * HEAD_DIM
    shard = place[0] ^ place[1 + pl.program_id(0)]
    tile = BLOCK
    lanes = lane_iota(tile)
    for part in range(rows // tile):
        piece = pl.ds(part * tile, tile)
        projected = mm(x_ref[0, piece, :], w_ref[...])
        cosine, sine = cos_ref[piece, :], sin_ref[piece, :]
        token = lax.broadcasted_iota(jnp.int32, (tile, LANES), 0) + (shard * rows + part * tile)
        inside = (token >= bounds_ref[0:1, :]) & (token < bounds_ref[1:2, :])
        slot = (lanes >= SEG_COL) & (lanes < SHIFT_COL)
        q_tail = jnp.where(slot & ~inside, FAR, 0.0)
        k_tail = jnp.where((slot & inside) | ((lanes >= SHIFT_COL) & (lanes < SHIFT_COL + 3)), 1.0, 0.0)
        v_tail = jnp.where((lanes >= HEAD_DIM) & (lanes < HEAD_DIM + 3), 1.0, 0.0)

        def head_of(column):
            start = column // LANES * LANES
            pair = projected[:, start : min(start + LANES, 3 * width)]
            if pair.shape[1] < LANES:
                pair = jnp.concatenate([pair, pair], axis=1)
            return pair if column % LANES == 0 else pltpu.roll(pair, HEAD_DIM, 1)

        for h in range(heads):
            q = head_of(h * HEAD_DIM)
            q = (q * cosine + turn(q, lanes) * sine) * (LOG2E / math.sqrt(HEAD_DIM))
            q_ref[h, piece, :] = jnp.where(lanes < HEAD_DIM, q, q_tail).astype(BF16)
            k = head_of(width + h * HEAD_DIM)
            k = k * cosine + turn(k, lanes) * sine
            k_ref[h, piece, :] = jnp.where(lanes < HEAD_DIM, k, k_tail).astype(BF16)
            v = head_of(2 * width + h * HEAD_DIM)
            v_ref[h, piece, :] = jnp.where(lanes < HEAD_DIM, v, v_tail).astype(BF16)


def project(x_slots, w_flat, cosine, sine, bounds, place, heads):
    count, rows, width = x_slots.shape
    tokens = count * rows
    out = jax.ShapeDtypeStruct((heads, tokens, LANES), BF16)
    whole = lambda *shape: pl.BlockSpec(shape, lambda s, place: (0,) * len(shape))
    by_shard = pl.BlockSpec((rows, LANES), lambda s, place: (place[0] ^ place[1 + s], 0))
    head_spec = pl.BlockSpec((heads, rows, LANES), lambda s, place: (0, place[0] ^ place[1 + s], 0))
    return pl.pallas_call(
        qkv_kernel,
        out_shape=(out, out, out),
        grid_spec=pltpu.PrefetchScalarGridSpec(
            num_scalar_prefetch=1,
            grid=(count,),
            in_specs=[
                pl.BlockSpec((1, rows, width), lambda s, place: (s, 0, 0)),
                whole(*w_flat.shape),
                by_shard,
                by_shard,
                whole(*bounds.shape),
            ],
            out_specs=[head_spec] * 3,
        ),
        compiler_params=pltpu.CompilerParams(vmem_limit_bytes=VMEM_LIMIT),
        cost_estimate=pl.CostEstimate(
            flops=2 * tokens * width * w_flat.shape[1],
            bytes_accessed=tokens * width * 2 + 3 * heads * tokens * LANES * 2,
            transcendentals=0,
        ),
        name="project",
    )(place, x_slots, w_flat, cosine, sine, bounds)


def attend_kernel(place, ranges, q_ref, k_ref, v_ref, o_ref, qb_ref, top_ref, acc_ref):
    heads = q_ref.shape[0]
    i = pl.program_id(0)
    blocks = pl.num_programs(0)
    first, last = ranges[i], ranges[blocks + i]
    lanes = lane_iota(BLOCK)
    top_ref[...] = jnp.full_like(top_ref, FAR)
    acc_ref[...] = jnp.zeros_like(acc_ref)

    def find_top(j, carry):
        rows = pl.ds(pl.multiple_of(j * BLOCK, BLOCK), BLOCK)
        for h in range(heads):
            s = mm(q_ref[h], k_ref[h, rows, :], NT)
            top_ref[h] = jnp.maximum(top_ref[h], jnp.maximum(s[:, :LANES], s[:, LANES:]))
        return carry

    lax.fori_loop(first, last + 1, find_top, 0)
    tops = []
    for h in range(heads):
        top = jnp.max(top_ref[h], axis=1, keepdims=True)
        tops.append(top)
        qb_ref[h] = q_ref[h] + shift_columns(-top, SHIFT_COL, lanes).astype(BF16)

    def add_up(j, carry):
        rows = pl.ds(pl.multiple_of(j * BLOCK, BLOCK), BLOCK)
        for h in range(heads):
            s = mm(qb_ref[h], k_ref[h, rows, :], NT)
            acc_ref[h] += mm(jnp.exp2(s).astype(BF16), v_ref[h, rows, :])
        return carry

    lax.fori_loop(first, last + 1, add_up, 0)
    for h in range(heads):
        total = acc_ref[h, :, HEAD_DIM : HEAD_DIM + 1]
        o_ref[0, :, h * HEAD_DIM : (h + 1) * HEAD_DIM] = (acc_ref[h, :, :HEAD_DIM] / total).astype(BF16)
        level = tops[h] + jnp.log2(total)
        qb_ref[h] = q_ref[h] + shift_columns(-level, SHIFT_COL, lanes).astype(BF16)


def slot_of(relative):
    return (relative >> 1) | ((relative & 1) << 1)


def attend(q, k, v, place, ranges, shards):
    heads, tokens, _ = q.shape
    blocks = tokens // BLOCK
    rows = tokens // shards
    per = rows // BLOCK
    whole = pl.BlockSpec((heads, tokens, LANES), lambda i, place, ranges: (0, 0, 0))
    mine = pl.BlockSpec((heads, BLOCK, LANES), lambda i, place, ranges: (0, i, 0))
    return pl.pallas_call(
        attend_kernel,
        out_shape=(
            jax.ShapeDtypeStruct((shards, rows, heads * HEAD_DIM), BF16),
            jax.ShapeDtypeStruct((heads, tokens, LANES), BF16),
        ),
        grid_spec=pltpu.PrefetchScalarGridSpec(
            num_scalar_prefetch=2,
            grid=(blocks,),
            in_specs=[mine, whole, whole],
            out_specs=[
                pl.BlockSpec(
                    (1, BLOCK, heads * HEAD_DIM),
                    lambda i, place, ranges: (slot_of((i // per) ^ place[0]), i % per, 0),
                ),
                mine,
            ],
            scratch_shapes=[pltpu.VMEM((heads, BLOCK, LANES), F32), pltpu.VMEM((heads, BLOCK, LANES), F32)],
        ),
        compiler_params=pltpu.CompilerParams(vmem_limit_bytes=VMEM_LIMIT),
        cost_estimate=pl.CostEstimate(
            flops=3 * heads * tokens * tokens * LANES,
            bytes_accessed=5 * heads * tokens * LANES * 2,
            transcendentals=heads * tokens * tokens // 2,
        ),
        name="attend",
    )(place, ranges, q, k, v)


def attend_back_kernel(
    place, ranges, qb_ref, k_ref, v_ref, att_ref, dh_ref, w_ref, cos_ref, sin_ref, out_ref, do_ref, dq_ref, dk_ref, dv_ref
):
    heads, tokens, _ = qb_ref.shape
    shards, rows, _ = att_ref.shape
    blocks = tokens // BLOCK
    per = rows // BLOCK
    width = heads * HEAD_DIM
    lanes = lane_iota(BLOCK)

    def place_of(i):
        return slot_of((i // per) ^ place[0]), pl.ds(pl.multiple_of((i % per) * BLOCK, BLOCK), BLOCK)

    def rows_of(i):
        return pl.ds(pl.multiple_of(i * BLOCK, BLOCK), BLOCK)

    def prepare(i, carry):
        slot, piece = place_of(i)
        d_att = mm(dh_ref[slot, piece, :], w_ref[...], NT)
        for h in range(heads):
            d_head = d_att[:, h * LANES : (h + 1) * LANES].astype(BF16).astype(F32)
            own = att_ref[slot, piece, h * HEAD_DIM : (h + 1) * HEAD_DIM].astype(F32)
            dot = jnp.sum(d_head[:, :HEAD_DIM] * own, axis=1, keepdims=True)
            do_ref[h, rows_of(i), :] = (d_head + shift_columns(-dot, HEAD_DIM, lanes)).astype(BF16)
        return carry

    lax.fori_loop(0, blocks, prepare, 0)
    dq_ref[...] = jnp.zeros_like(dq_ref)

    def rotate_back(values, where):
        return values * cos_ref[where, :] - turn(values, lanes) * sin_ref[where, :]

    def over_keys(j, carry):
        keys = rows_of(j)
        dk_ref[...] = jnp.zeros_like(dk_ref)
        dv_ref[...] = jnp.zeros_like(dv_ref)

        def over_queries(i, carry):
            queries = rows_of(i)
            for h in range(heads):
                k, q, d_out = k_ref[h, keys, :], qb_ref[h, queries, :], do_ref[h, queries, :]
                probs = jnp.exp2(mm(k, q, NT))
                d_scores = (probs * mm(v_ref[h, keys, :], d_out, NT)).astype(BF16)
                dv_ref[h] += mm(probs.astype(BF16), d_out)
                dk_ref[h] += mm(d_scores, q)
                dq_ref[h, queries, :] += mm(d_scores, k, TN)
            return carry

        lax.fori_loop(ranges[j], ranges[blocks + j] + 1, over_queries, 0)
        slot, piece = place_of(j)
        for h in range(heads):
            d_key = rotate_back(dk_ref[h] * (1.0 / LOG2E), keys)
            column = width + h * HEAD_DIM
            out_ref[slot, piece, column : column + HEAD_DIM] = d_key[:, :HEAD_DIM].astype(BF16)
            column = 2 * width + h * HEAD_DIM
            out_ref[slot, piece, column : column + HEAD_DIM] = dv_ref[h, :, :HEAD_DIM].astype(BF16)
        return carry

    lax.fori_loop(0, blocks, over_keys, 0)

    def finish(i, carry):
        slot, piece = place_of(i)
        for h in range(heads):
            d_query = rotate_back(dq_ref[h, rows_of(i), :] * (1.0 / math.sqrt(HEAD_DIM)), rows_of(i))
            out_ref[slot, piece, h * HEAD_DIM : (h + 1) * HEAD_DIM] = d_query[:, :HEAD_DIM].astype(BF16)
        return carry

    lax.fori_loop(0, blocks, finish, 0)


def attend_back(qb, k, v, att, dh_slots, w_out, cosine, sine, place, ranges):
    heads, tokens, _ = qb.shape
    shards, rows, _ = att.shape
    w_wide = jnp.pad(w_out.reshape(heads, HEAD_DIM, -1), ((0, 0), (0, LANES - HEAD_DIM), (0, 0)))
    w_wide = w_wide.reshape(heads * LANES, -1)
    vmem = pl.BlockSpec(memory_space=pltpu.VMEM)
    smem = pl.BlockSpec(memory_space=pltpu.SMEM)
    return pl.pallas_call(
        attend_back_kernel,
        out_shape=jax.ShapeDtypeStruct((shards, rows, 3 * heads * HEAD_DIM), BF16),
        in_specs=[smem, smem] + [vmem] * 8,
        out_specs=vmem,
        scratch_shapes=[
            pltpu.VMEM((heads, tokens, LANES), BF16),
            pltpu.VMEM((heads, tokens, LANES), F32),
            pltpu.VMEM((heads, BLOCK, LANES), F32),
            pltpu.VMEM((heads, BLOCK, LANES), F32),
        ],
        compiler_params=pltpu.CompilerParams(vmem_limit_bytes=VMEM_LIMIT),
        cost_estimate=pl.CostEstimate(
            flops=5 * heads * tokens * tokens * LANES,
            bytes_accessed=6 * heads * tokens * LANES * 2,
            transcendentals=heads * tokens * tokens // 2,
        ),
        name="attend_back",
    )(place, ranges, qb, k, v, att, dh_slots, w_wide, cosine, sine)


def doc_tables(lengths, tokens, blocks):
    ends = jnp.cumsum(lengths)
    starts = ends - lengths
    places = jnp.arange(tokens, dtype=jnp.int32)
    inside = (places[:, None] >= starts[None, :]) & (places[:, None] < ends[None, :])
    positions = places - jnp.sum(jnp.where(inside, starts[None, :], 0), axis=1)
    edge = jnp.arange(blocks, dtype=jnp.int32) * BLOCK
    touches = (starts[None, :] < edge[:, None] + BLOCK) & (ends[None, :] > edge[:, None])
    first = jnp.min(jnp.where(touches, starts[None, :], tokens), axis=1) // BLOCK
    last = (jnp.max(jnp.where(touches, ends[None, :], 0), axis=1) - 1) // BLOCK
    ranges = jnp.concatenate([first, last]).astype(jnp.int32)
    pad = (SEG_COL, LANES - SEG_COL - lengths.shape[0])
    bounds = jnp.stack([jnp.pad(starts, pad), jnp.pad(ends, pad)]).astype(jnp.int32)
    return positions, ranges, jnp.pad(bounds, ((0, 6), (0, 0)))


def rotary(positions):
    lane = jnp.arange(LANES, dtype=jnp.int32)
    rate = jnp.exp((lane & 31).astype(F32) * (-2.0 * math.log(1000.0) / HEAD_DIM))
    angles = positions.astype(F32)[:, None] * rate[None, :]
    sign = jnp.where((lane & 63) < 32, -1.0, 1.0)
    return jnp.cos(angles), jnp.sin(angles) * sign[None, :]


def dp_orders(size):
    bits = list(range(size.bit_length() - 1))
    return [bits, bits[1::-1] + bits[2:]]


def piece_rows(rows, size):
    return -(-rows // (16 * size)) * 16


def peer_of(index, bit):
    mine = (index // (1 << bit)) % 2
    return index + (1 - 2 * mine) * (1 << bit), mine


def finish_kernel(
    size, x_ref, dq_ref, w_ref, w_near_ref, dh_ref, norms_ref,
    dx_ref, grad_ref, sums_ref,
    total, give, take, near, far_out, far_in, own, norm_in,
    near_sem, far_sem, give_sem, gather_sem, norm_sem,
):
    orders = dp_orders(size)
    rows = total.shape[1] // size
    cols = total.shape[2]
    half = x_ref.shape[2] // 2
    m, me = lax.axis_index("mp"), lax.axis_index("dp")
    core, far = peer_of(m, 0)[0], peer_of(m, 1)[0]
    stages = len(orders[0])

    barrier = pltpu.get_barrier_semaphore()
    partners = [{"mp": core}, {"mp": far}] + [{"dp": peer_of(me, bit)[0]} for bit in range(stages)]
    for partner in partners:
        pl.semaphore_signal(barrier, inc=1, device_id=partner, device_id_type=MESH)
    pl.semaphore_wait(barrier, len(partners))

    def send(source, target, sems, where, partner):
        copy = pltpu.make_async_remote_copy(
            source, target, sems.at[0, *where], sems.at[1, *where], device_id=partner, device_id_type=MESH
        )
        copy.start()
        return copy

    near_copy = send(dq_ref.at[pl.ds(2, 2)], near, near_sem, (), {"mp": core})
    sums_ref[...] = norms_ref[...]
    norm_partners = partners

    for chain in range(2):
        if total.shape[1] > half:
            total[chain, half:, :] = jnp.zeros((total.shape[1] - half, cols), F32)
        for part in range(0, half, LANES):
            at = chain * half + part
            piece = mm(x_ref[0, :, at : at + LANES], dq_ref[0], TN)
            for slot in range(1, x_ref.shape[0]):
                piece += mm(x_ref[slot, :, at : at + LANES], dq_ref[slot], TN)
            total[chain, part : part + LANES, :] = piece

    def scatter(stage, lows, count):
        half_count = count // 2
        copies, keeps = [], []
        for chain in range(2):
            partner, mine = peer_of(me, orders[chain][stage])
            out = pl.ds(pl.multiple_of((lows[chain] + (1 - mine) * half_count) * rows, 16), half_count * rows)
            keeps.append(lows[chain] + mine * half_count)
            spot = pl.ds(half_count * rows, half_count * rows)
            give[chain, spot, :] = total[chain, out, :].astype(BF16)
            copies.append(
                send(give.at[chain, spot], take.at[chain, spot], give_sem, (chain, stage), {"dp": partner})
            )
        return copies, keeps

    def absorb(copies, keeps, count):
        half_count = count // 2
        for chain in range(2):
            copies[chain].wait()
            keep = pl.ds(pl.multiple_of(keeps[chain] * rows, 16), half_count * rows)
            total[chain, keep, :] += take[chain, pl.ds(half_count * rows, half_count * rows), :].astype(F32)

    def norm_exchange(stage):
        return send(sums_ref, norm_in.at[stage], norm_sem, (stage,), norm_partners[stage])

    def norm_add(stage, copy):
        copy.wait()
        sums_ref[...] += norm_in[stage]

    lows, count = [0, 0], size
    copies, keeps = scatter(0, lows, count)
    norm_copy = norm_exchange(0)
    near_copy.wait()
    d_far = mm(dq_ref[1], w_ref[...], NT) + mm(near[1], w_near_ref[...], NT)
    far_out[...] = d_far.astype(BF16)
    far_copy = send(far_out, far_in, far_sem, (), {"mp": far})
    d_own = mm(dq_ref[0], w_ref[...], NT) + mm(near[0], w_near_ref[...], NT)
    own[...] = dh_ref[...] + d_own
    norm_add(0, norm_copy)
    norm_done = 1
    for stage in range(stages):
        norm_copy = norm_exchange(norm_done) if norm_done < len(partners) else None
        absorb(copies, keeps, count)
        lows, count = keeps, count // 2
        if stage + 1 < stages:
            copies, keeps = scatter(stage + 1, lows, count)
        if norm_copy is not None:
            norm_add(norm_done, norm_copy)
            norm_done += 1
    for chain in range(2):
        mine = pl.ds(pl.multiple_of(lows[chain] * rows, 16), rows)
        grad_ref[chain, mine, :] = total[chain, mine, :].astype(BF16)
    for stage in reversed(range(stages)):
        copies = []
        for chain in range(2):
            partner, mine = peer_of(me, orders[chain][stage])
            block = pl.ds(pl.multiple_of(lows[chain] * rows, 16), count * rows)
            spot = grad_ref.at[chain, block]
            copies.append(send(spot, spot, gather_sem, (chain, stage), {"dp": partner}))
            lows[chain] = lows[chain] - mine * count
        if norm_done < len(partners):
            norm_add(norm_done, norm_exchange(norm_done))
            norm_done += 1
        for copy in copies:
            copy.wait()
        count *= 2
    far_copy.wait()
    dx_ref[...] = (own[...] + far_in[...].astype(F32)).astype(BF16)
    while norm_done < len(partners):
        norm_add(norm_done, norm_exchange(norm_done))
        norm_done += 1


def finish(x_slots, d_qkv, w_qkv, w_near, dh, norms):
    size = lax.axis_size("dp")
    stages = size.bit_length() - 1
    slots, rows, width = x_slots.shape
    cols = d_qkv.shape[2]
    padded = piece_rows(width // 2, size) * size
    vmem = pl.BlockSpec(memory_space=pltpu.VMEM)
    dma = pltpu.SemaphoreType.DMA
    return pl.pallas_call(
        functools.partial(finish_kernel, size),
        out_shape=(
            jax.ShapeDtypeStruct((rows, width), BF16),
            jax.ShapeDtypeStruct((2, padded, cols), BF16),
            jax.ShapeDtypeStruct(norms.shape, F32),
        ),
        in_specs=[vmem] * 6,
        out_specs=[vmem] * 3,
        scratch_shapes=[
            pltpu.VMEM((2, padded, cols), F32),
            pltpu.VMEM((2, padded, cols), BF16),
            pltpu.VMEM((2, padded, cols), BF16),
            pltpu.VMEM((2, rows, cols), BF16),
            pltpu.VMEM((rows, width), BF16),
            pltpu.VMEM((rows, width), BF16),
            pltpu.VMEM((rows, width), F32),
            pltpu.VMEM((2 + stages,) + norms.shape, F32),
            dma((2,)),
            dma((2,)),
            dma((2, 2, stages)),
            dma((2, 2, stages)),
            dma((2, 2 + stages)),
        ],
        compiler_params=pltpu.CompilerParams(
            collective_id=1, has_side_effects=True, vmem_limit_bytes=VMEM_LIMIT
        ),
        cost_estimate=pl.CostEstimate(
            flops=6 * slots * rows * width * cols, bytes_accessed=12 * rows * width, transcendentals=0
        ),
        name="finish",
    )(x_slots, d_qkv, w_qkv, w_near, dh, norms)


def sum_over_dp(values):
    piece = lax.psum_scatter(values.astype(BF16), "dp", scatter_dimension=0, tiled=True)
    return lax.all_gather(piece, "dp", axis=0, tiled=True).astype(F32)


def body(
    tokens, lengths, w_qkv, w_out, w_gate_up, w_down, ln1_scale, ln1_shift, ln2_scale, ln2_shift, cotangent
):
    rows, width = tokens.shape
    shards = lax.axis_size("mp")
    length = rows * shards
    local_cols = w_out.shape[0]
    heads = local_cols // HEAD_DIM
    hidden_cols = w_down.shape[0]
    m = lax.axis_index("mp")

    def swap(values, distance):
        return lax.ppermute(values, "mp", [(i, i ^ distance) for i in range(shards)])

    across = lambda values: swap(values, 2)
    beside = lambda values: swap(values, 1)

    x_far = across(tokens)
    x_near = beside(tokens)
    x_last = beside(x_far)
    positions, ranges, bounds = doc_tables(lengths[0], length, length // BLOCK)
    cosine, sine = rotary(positions)
    place = jnp.stack([m.astype(jnp.int32)] + [jnp.int32(r) for r in (0, 2, 1, 3)])
    flat_qkv = w_qkv.reshape(width, 3 * local_cols)
    w_qkv_near = beside(flat_qkv)
    w_out_near = beside(w_out)
    flat_gate_up = w_gate_up.reshape(width, 2 * hidden_cols)
    w_gate_up_near = beside(flat_gate_up)
    w_down_near = beside(w_down)
    x_slots = jnp.stack([tokens, x_far, x_near, x_last])
    q, k, v = project(x_slots, flat_qkv, cosine, sine, bounds, place, heads)
    att, qb = attend(q, k, v, place, ranges, shards)
    att_near = beside(att[2:])

    def out_project(index):
        return mm(att[index], w_out) + mm(att_near[index], w_out_near)

    branch_far = across(out_project(1).astype(BF16))
    h = tokens.astype(F32) + out_project(0) + branch_far.astype(F32)
    h = h - jnp.mean(h, axis=-1, keepdims=True)
    r1 = lax.rsqrt(jnp.mean(h * h, axis=-1, keepdims=True) + EPSILON)
    h_hat = h * r1
    normed = h_hat * ln1_scale + ln1_shift
    normed_low = normed.astype(BF16)
    normed_far = across(normed_low)

    w_ins, w_downs = (flat_gate_up, w_gate_up_near), (w_down, w_down_near)

    def mlp(values):
        kept, partial = [], 0.0
        for w_in, w_back in zip(w_ins, w_downs):
            gate_up = mm(values, w_in)
            gate, up = gate_up[:, :hidden_cols], gate_up[:, hidden_cols:]
            hidden = (gate * jax.nn.sigmoid(gate) * up).astype(BF16)
            partial = partial + mm(hidden, w_back)
            kept.append((gate_up.astype(BF16), hidden))
        return partial, kept

    partial_own, kept_own = mlp(normed_low)
    partial_far, kept_far = mlp(normed_far)
    mlp_far = across(partial_far.astype(BF16))
    z = normed + partial_own + mlp_far.astype(F32)
    z = z - jnp.mean(z, axis=-1, keepdims=True)
    r2 = lax.rsqrt(jnp.mean(z * z, axis=-1, keepdims=True) + EPSILON)
    z_hat = z * r2
    output = (z_hat * ln2_scale + ln2_shift).astype(BF16)
    g = cotangent.astype(F32)
    e = g * ln2_scale
    dz = r2 * (e - jnp.mean(e, axis=-1, keepdims=True) - z_hat * jnp.mean(e * z_hat, axis=-1, keepdims=True))
    d_scale_two, d_shift_two = jnp.sum(g * z_hat, axis=0), jnp.sum(g, axis=0)
    dz_low = dz.astype(BF16)
    dz_far = across(dz_low)

    def mlp_back(d_out, kept):
        d_normed, d_ins = 0.0, []
        for (gate_up, hidden), w_in, w_back in zip(kept, w_ins, w_downs):
            gate, up = gate_up[:, :hidden_cols].astype(F32), gate_up[:, hidden_cols:].astype(F32)
            d_hidden = mm(d_out, w_back, NT)
            s = jax.nn.sigmoid(gate)
            d_gate = (d_hidden * up * s * (1.0 + gate * (1.0 - s))).astype(BF16)
            d_up = (d_hidden * gate * s).astype(BF16)
            d_in = jnp.concatenate([d_gate, d_up], axis=1)
            d_normed = d_normed + mm(d_in, w_in, NT)
            d_ins.append(d_in)
        return d_normed, d_ins

    d_own, d_ins_own = mlp_back(dz_low, kept_own)
    d_far, d_ins_far = mlp_back(dz_far, kept_far)
    d_normed_far = across(d_far.astype(BF16))

    def weight_grads(core):
        down = mm(kept_own[core][1], dz_low, TN) + mm(kept_far[core][1], dz_far, TN)
        gate_up = mm(normed_low, d_ins_own[core], TN) + mm(normed_far, d_ins_far[core], TN)
        return gate_up, down

    grad_gate_up, grad_down = weight_grads(1)
    grad_gate_up_near, grad_down_near = beside(grad_gate_up.astype(BF16)), beside(grad_down.astype(BF16))
    grad_gate_up, grad_down = weight_grads(0)
    grad_gate_up = grad_gate_up + grad_gate_up_near.astype(F32)
    grad_down = grad_down + grad_down_near.astype(F32)
    grad_gate_up = sum_over_dp(grad_gate_up)
    grad_down = sum_over_dp(grad_down)

    d_normed = dz + d_own + d_normed_far.astype(F32)
    e1 = d_normed * ln1_scale
    dh = r1 * (e1 - jnp.mean(e1, axis=-1, keepdims=True) - h_hat * jnp.mean(e1 * h_hat, axis=-1, keepdims=True))
    d_scale_one, d_shift_one = jnp.sum(d_normed * h_hat, axis=0), jnp.sum(d_normed, axis=0)
    dh_low = dh.astype(BF16)
    dh_far = across(dh_low)
    dh_near = beside(dh_low)
    dh_last = beside(dh_far)
    dh_slots = jnp.stack([dh_low, dh_far, dh_near, dh_last])
    d_qkv = attend_back(qb, k, v, att, dh_slots, w_out, cosine, sine, place, ranges)
    grad_out = mm(att.reshape(length, local_cols), dh_slots.reshape(length, width), TN)
    grad_out = sum_over_dp(grad_out)
    norms = jnp.stack([d_scale_one, d_shift_one, d_scale_two, d_shift_two])
    norms = jnp.concatenate([norms, jnp.zeros_like(norms)])
    d_tokens, grad_qkv, norms = finish(x_slots, d_qkv, flat_qkv, w_qkv_near, dh, norms)
    grad_qkv = grad_qkv[:, : width // 2].reshape(width, 3 * local_cols).astype(F32)
    norms = lax.dynamic_slice_in_dim(norms, m * local_cols, local_cols, 1)
    return (
        output,
        d_tokens,
        grad_qkv.reshape(width, 3, local_cols),
        grad_out,
        grad_gate_up.reshape(width, 2, hidden_cols),
        grad_down,
        norms[0],
        norms[1],
        norms[2],
        norms[3],
    )


def solution(mesh):
    return jax.shard_map(
        body,
        mesh=mesh,
        in_specs=(
            P(("dp", "mp"), None),
            P("dp", None),
            P(None, None, "mp"),
            P("mp", None),
            P(None, None, "mp"),
            P("mp", None),
            P(),
            P(),
            P(),
            P(),
            P(("dp", "mp"), None),
        ),
        out_specs=(
            P(("dp", "mp"), None),
            P(("dp", "mp"), None),
            P(None, None, "mp"),
            P("mp", None),
            P(None, None, "mp"),
            P("mp", None),
            P("mp"),
            P("mp"),
            P("mp"),
            P("mp"),
        ),
        check_vma=False,
    )
```

```python
import functools
import math

import jax
import jax.numpy as jnp
from jax import lax
from jax.experimental import pallas as pl
from jax.experimental.pallas import tpu as pltpu
from jax.sharding import PartitionSpec as P

F32 = jnp.float32
BF16 = jnp.bfloat16
HEAD_DIM = 64
LANES = 128
EPSILON = 1e-05
KEYS = 512
FAR = -(2.0**100)
LOG2E = math.log2(math.e)
NT = (((1,), (1,)), ((), ()))
TN = (((0,), (0,)), ((), ()))
NN = (((1,), (0,)), ((), ()))
VMEM_LIMIT = 58 << 20
WIDE_LIMIT = 62 << 20
MESH = pl.DeviceIdType.MESH


def mm(a, b, dims=NN):
    return lax.dot_general(a, b, dims, preferred_element_type=F32)


def thirds(row):
    high = row.astype(BF16).astype(F32)
    mid = (row - high).astype(BF16).astype(F32)
    low = row - high - mid
    return jnp.concatenate([high, mid, low, jnp.zeros((13, row.shape[1]), F32)], axis=0)


def slot_of(relative):
    return relative // 2 + 2 * (relative % 2)


def span(index, size):
    return pl.ds(pl.multiple_of(index * size, size), size)


def project_kernel(place, x_ref, w_ref, cos_ref, sin_ref, bounds_ref, q_ref, k_ref, v_ref, k_rows_ref):
    rows = x_ref.shape[1]
    heads = q_ref.shape[0]
    width = heads * HEAD_DIM
    shard = place[0] ^ place[1 + pl.program_id(0)]
    projected = mm(w_ref[...], x_ref[0], NT)
    cosine, sine = cos_ref[...], sin_ref[...]
    token = lax.broadcasted_iota(jnp.int32, (16, rows), 1) + shard * rows
    inside = (token >= bounds_ref[:, 0:1]) & (token < bounds_ref[:, 1:2])
    row = lax.broadcasted_iota(jnp.int32, (48, rows), 0)
    q_tail = jnp.concatenate([jnp.where(inside, 0.0, FAR), jnp.zeros((48 - 16 + 16, rows), F32)], axis=0)
    ones = jnp.where(row < 3, 1.0, 0.0)
    k_tail = jnp.concatenate([jnp.where(inside, 1.0, 0.0), ones], axis=0)
    v_tail = jnp.concatenate([ones, jnp.zeros((16, rows), F32)], axis=0)
    half = HEAD_DIM // 2

    def rotated(start):
        first, second = projected[start : start + half], projected[start + half : start + HEAD_DIM]
        return first * cosine - second * sine, second * cosine + first * sine

    scale = LOG2E / math.sqrt(HEAD_DIM)
    for h in range(heads):
        first, second = rotated(h * HEAD_DIM)
        q_ref[h] = jnp.concatenate([first * scale, second * scale, q_tail], axis=0).astype(BF16)
        first, second = rotated(width + h * HEAD_DIM)
        k = jnp.concatenate([first, second, k_tail], axis=0)
        k_ref[h] = k.astype(BF16)
        k_rows_ref[h] = k.T.astype(BF16)
        start = 2 * width + h * HEAD_DIM
        v_ref[h] = jnp.concatenate([projected[start : start + HEAD_DIM], v_tail], axis=0).astype(BF16)


def project(x_slots, w_turned, cosine, sine, bounds, place, heads):
    count, rows, width = x_slots.shape
    tokens = count * rows
    along = jax.ShapeDtypeStruct((heads, LANES, tokens), BF16)
    down = jax.ShapeDtypeStruct((heads, tokens, LANES), BF16)
    whole = lambda *shape: pl.BlockSpec(shape, lambda s, place: (0,) * len(shape))
    table = pl.BlockSpec((HEAD_DIM // 2, rows), lambda s, place: (0, place[0] ^ place[1 + s]))
    along_spec = pl.BlockSpec((heads, LANES, rows), lambda s, place: (0, 0, place[0] ^ place[1 + s]))
    down_spec = pl.BlockSpec((heads, rows, LANES), lambda s, place: (0, place[0] ^ place[1 + s], 0))
    return pl.pallas_call(
        project_kernel,
        out_shape=(along, along, along, down),
        grid_spec=pltpu.PrefetchScalarGridSpec(
            num_scalar_prefetch=1,
            grid=(count,),
            in_specs=[
                pl.BlockSpec((1, rows, width), lambda s, place: (s, 0, 0)),
                whole(*w_turned.shape),
                table,
                table,
                whole(*bounds.shape),
            ],
            out_specs=[along_spec] * 3 + [down_spec],
        ),
        compiler_params=pltpu.CompilerParams(vmem_limit_bytes=VMEM_LIMIT),
        cost_estimate=pl.CostEstimate(
            flops=2 * tokens * width * w_turned.shape[0],
            bytes_accessed=tokens * width * 2 + 4 * heads * tokens * LANES * 2,
            transcendentals=0,
        ),
        name="project",
    )(place, x_slots, w_turned, cosine, sine, bounds)


def attend_kernel(place, ranges, q_ref, k_ref, v_ref, o_ref, o_along_ref, q_rows_ref, top_ref, acc_ref):
    heads = q_ref.shape[0]
    i = pl.program_id(0)
    tiles = pl.num_programs(0)
    top_ref[...] = jnp.full_like(top_ref, FAR)
    acc_ref[...] = jnp.zeros_like(acc_ref)

    def over_keys(j, carry):
        for h in range(heads):
            s = mm(k_ref[h, span(j, KEYS), :], q_ref[h])
            old = top_ref[h, 0:1, :]
            top = jnp.maximum(old, jnp.max(s, axis=0, keepdims=True))
            probs = jnp.exp2(s - top).astype(BF16)
            top_ref[h, 0:1, :] = top
            acc_ref[h] = acc_ref[h] * jnp.exp2(old - top) + mm(v_ref[h, :80, span(j, KEYS)], probs)
        return carry

    lax.fori_loop(ranges[i], ranges[tiles + i] + 1, over_keys, 0)
    outs = []
    for h in range(heads):
        total = acc_ref[h, HEAD_DIM : HEAD_DIM + 1, :]
        outs.append(acc_ref[h, :HEAD_DIM, :] / total)
        level = top_ref[h, 0:1, :] + jnp.log2(total)
        query = q_ref[h].astype(F32)
        q_rows_ref[h] = jnp.concatenate([query[:80], thirds(-level), query[96:]], axis=0).T.astype(BF16)
    out = jnp.concatenate(outs, axis=0)
    o_along_ref[...] = out.astype(BF16)
    o_ref[0] = out.T.astype(BF16)


def attend(q, k_rows, v, place, ranges, shards):
    heads, _, tokens = q.shape
    rows = tokens // shards
    whole = lambda *shape: pl.BlockSpec(shape, lambda i, place, ranges: (0, 0, 0))
    return pl.pallas_call(
        attend_kernel,
        out_shape=(
            jax.ShapeDtypeStruct((shards, rows, heads * HEAD_DIM), BF16),
            jax.ShapeDtypeStruct((heads * HEAD_DIM, tokens), BF16),
            jax.ShapeDtypeStruct((heads, tokens, LANES), BF16),
        ),
        grid_spec=pltpu.PrefetchScalarGridSpec(
            num_scalar_prefetch=2,
            grid=(shards,),
            in_specs=[
                pl.BlockSpec((heads, LANES, rows), lambda i, place, ranges: (0, 0, i)),
                whole(heads, tokens, LANES),
                whole(heads, LANES, tokens),
            ],
            out_specs=[
                pl.BlockSpec(
                    (1, rows, heads * HEAD_DIM), lambda i, place, ranges: (slot_of(i ^ place[0]), 0, 0)
                ),
                pl.BlockSpec((heads * HEAD_DIM, rows), lambda i, place, ranges: (0, i)),
                pl.BlockSpec((heads, rows, LANES), lambda i, place, ranges: (0, i, 0)),
            ],
            scratch_shapes=[pltpu.VMEM((heads, 8, rows), F32), pltpu.VMEM((heads, 80, rows), F32)],
        ),
        compiler_params=pltpu.CompilerParams(vmem_limit_bytes=VMEM_LIMIT),
        cost_estimate=pl.CostEstimate(
            flops=2 * heads * tokens * tokens * LANES,
            bytes_accessed=5 * heads * tokens * LANES * 2,
            transcendentals=heads * tokens * tokens // 2,
        ),
        name="attend",
    )(place, ranges, q, k_rows, v)


def attend_back_kernel(
    place, ranges, q_rows_ref, q_ref, k_rows_ref, k_ref, v_ref, att_ref, dh_ref, w_ref, cos_ref, sin_ref,
    out_ref, do_ref, do_rows_ref, dq_ref, dk_ref, dv_ref,
):
    heads, _, tokens = q_ref.shape
    shards, rows, _ = dh_ref.shape
    width = heads * HEAD_DIM
    half = HEAD_DIM // 2
    tiles = tokens // KEYS
    per = rows // KEYS

    def prepare(i, carry):
        d_att = mm(w_ref[...], dh_ref[slot_of(i ^ place[0])], NT).astype(BF16)
        do_ref[:, span(i, rows)] = d_att
        products = d_att.astype(F32) * att_ref[:, span(i, rows)].astype(F32)
        for h in range(heads):
            own = slice(h * HEAD_DIM, (h + 1) * HEAD_DIM)
            dot = jnp.sum(products[own], axis=0, keepdims=True)
            wide = [d_att[own].astype(F32), thirds(-dot), jnp.zeros((LANES - HEAD_DIM - 16, rows), F32)]
            do_rows_ref[h, span(i, rows), :] = jnp.concatenate(wide, axis=0).T.astype(BF16)
        return carry

    lax.fori_loop(0, shards, prepare, 0)
    dq_ref[...] = jnp.zeros_like(dq_ref)

    def rotated_back(values, cosine, sine):
        first, second = values[:half], values[half:]
        return [first * cosine + second * sine, second * cosine - first * sine]

    def over_keys(j, carry):
        keys = span(j, KEYS)
        dk_ref[...] = jnp.zeros_like(dk_ref)
        dv_ref[...] = jnp.zeros_like(dv_ref)

        def over_queries(i, carry):
            queries = span(i, rows)
            for h in range(heads):
                k = k_ref[h, :, keys]
                probs = jnp.exp2(mm(q_rows_ref[h, queries, :], k))
                d_scores = (probs * mm(do_rows_ref[h, queries, :], v_ref[h, :, keys])).astype(BF16)
                dv_ref[h] += mm(do_ref[h * HEAD_DIM : (h + 1) * HEAD_DIM, queries], probs.astype(BF16))
                dk_ref[h] += mm(q_ref[h, :HEAD_DIM, queries], d_scores)
                dq_ref[h, :, queries] += mm(k[:HEAD_DIM], d_scores, NT)
            return carry

        lax.fori_loop(ranges[j], ranges[tiles + j] + 1, over_queries, 0)
        cosine, sine = cos_ref[:, keys] * (1.0 / LOG2E), sin_ref[:, keys] * (1.0 / LOG2E)
        pieces = []
        for h in range(heads):
            pieces += rotated_back(dk_ref[h], cosine, sine)
        pieces += [dv_ref[h] for h in range(heads)]
        slot = slot_of((j // per) ^ place[0])
        out_ref[slot, span(j % per, KEYS), width:] = jnp.concatenate(pieces, axis=0).T.astype(BF16)
        return carry

    lax.fori_loop(0, tiles, over_keys, 0)

    def finish(i, carry):
        scale = 1.0 / math.sqrt(HEAD_DIM)
        cosine, sine = cos_ref[:, span(i, rows)] * scale, sin_ref[:, span(i, rows)] * scale
        pieces = []
        for h in range(heads):
            pieces += rotated_back(dq_ref[h, :, span(i, rows)], cosine, sine)
        out_ref[slot_of(i ^ place[0]), :, :width] = jnp.concatenate(pieces, axis=0).T.astype(BF16)
        return carry

    lax.fori_loop(0, shards, finish, 0)


def attend_back(q_rows, q, k_rows, k, v, att_along, dh_slots, w_out, cosine, sine, place, ranges):
    heads, _, tokens = q.shape
    shards, rows, _ = dh_slots.shape
    vmem = pl.BlockSpec(memory_space=pltpu.VMEM)
    smem = pl.BlockSpec(memory_space=pltpu.SMEM)
    return pl.pallas_call(
        attend_back_kernel,
        out_shape=jax.ShapeDtypeStruct((shards, rows, 3 * heads * HEAD_DIM), BF16),
        in_specs=[smem, smem] + [vmem] * 10,
        out_specs=vmem,
        scratch_shapes=[
            pltpu.VMEM((heads * HEAD_DIM, tokens), BF16),
            pltpu.VMEM((heads, tokens, LANES), BF16),
            pltpu.VMEM((heads, HEAD_DIM, tokens), F32),
            pltpu.VMEM((heads, HEAD_DIM, KEYS), F32),
            pltpu.VMEM((heads, HEAD_DIM, KEYS), F32),
        ],
        compiler_params=pltpu.CompilerParams(vmem_limit_bytes=VMEM_LIMIT),
        cost_estimate=pl.CostEstimate(
            flops=4 * heads * tokens * tokens * LANES,
            bytes_accessed=6 * heads * tokens * LANES * 2,
            transcendentals=heads * tokens * tokens // 2,
        ),
        name="attend_back",
    )(place, ranges, q_rows, q, k_rows, k, v, att_along, dh_slots, w_out, cosine, sine)


def doc_tables(lengths, tokens, rows):
    ends = jnp.cumsum(lengths)
    starts = ends - lengths
    places = jnp.arange(tokens, dtype=jnp.int32)
    inside = (places[:, None] >= starts[None, :]) & (places[:, None] < ends[None, :])
    positions = places - jnp.sum(jnp.where(inside, starts[None, :], 0), axis=1)

    def shared(size, other):
        edge = jnp.arange(tokens // size, dtype=jnp.int32) * size
        touches = (starts[None, :] < edge[:, None] + size) & (ends[None, :] > edge[:, None])
        first = jnp.min(jnp.where(touches, starts[None, :], tokens), axis=1) // other
        last = (jnp.max(jnp.where(touches, ends[None, :], 0), axis=1) - 1) // other
        return jnp.concatenate([first, last]).astype(jnp.int32)

    bounds = jnp.stack([starts, ends], axis=1).astype(jnp.int32)
    return positions, shared(rows, KEYS), shared(KEYS, rows), bounds


def rotary(positions):
    rate = jnp.exp(jnp.arange(HEAD_DIM // 2, dtype=F32) * (-2.0 * math.log(1000.0) / HEAD_DIM))
    angles = rate[:, None] * positions.astype(F32)[None, :]
    return jnp.cos(angles), jnp.sin(angles)


def dp_orders(size):
    bits = list(range(size.bit_length() - 1))
    return [bits, bits[1::-1] + bits[2:]]


def halvings(size):
    return min(3, size.bit_length() - 1)


def peer_of(index, bit):
    mine = (index // (1 << bit)) % 2
    return index + (1 - 2 * mine) * (1 << bit), mine


def send(source, target, send_sem, recv_sem, partner):
    copy = pltpu.make_async_remote_copy(
        source, target, send_sem, recv_sem, device_id=partner, device_id_type=MESH
    )
    copy.start()
    return copy


def greet(partners):
    barrier = pltpu.get_barrier_semaphore()
    for partner in partners:
        pl.semaphore_signal(barrier, inc=1, device_id=partner, device_id_type=MESH)
    pl.semaphore_wait(barrier, len(partners))


ATT, BRANCH, NORMED, OUT, DOUT, DNORMED, DH, DH_NEAR, DH_LAST, GRAD_NEAR, GRAD_DP = range(11)


def middle_kernel(
    size, att_ref, wo_ref, wo_near_ref, tok_ref, cot_ref, ln_ref, win_hbm, win_near_hbm, wdn_hbm, wdn_near_hbm,
    out_ref, dh_ref, slots_ref, norms_ref, kept_hbm,
    win, wdn, near, outbox, inbox, low, hat, res, own, r1, gu, hid, dlow, total, give, take, take_dp, sums,
    sems, loads, stores,
):
    rows, width = tok_ref.shape
    hidden = wdn.shape[0] // 2
    half = width // 2
    chunk = rows // 2
    chunks = [slice(c * chunk, (c + 1) * chunk) for c in range(2)]
    m, me = lax.axis_index("mp"), lax.axis_index("dp")
    core, far = {"mp": peer_of(m, 0)[0]}, {"mp": peer_of(m, 1)[0]}
    firsts = [order[0] for order in dp_orders(size)]
    greet([core, far] + [{"dp": peer_of(me, bit)[0]} for bit in sorted(set(firsts))])

    def post(kind, c, source, target, partner):
        return send(source, target, sems.at[0, kind, c], sems.at[1, kind, c], partner)

    att_copy = post(ATT, 0, att_ref.at[pl.ds(2, 2)], near, core)
    fetches = []
    for n, (source, target) in enumerate(
        [
            (win_hbm, win.at[0]),
            (win_near_hbm, win.at[1]),
            (wdn_hbm, wdn.at[pl.ds(0, hidden)]),
            (wdn_near_hbm, wdn.at[pl.ds(hidden, hidden)]),
        ]
    ):
        fetches.append(pltpu.make_async_copy(source, target, loads.at[n]))
        fetches[-1].start()
    sums[...] = jnp.zeros_like(sums)
    scale_one, shift_one, scale_two, shift_two = (ln_ref[i : i + 1, :] for i in range(4))
    att_copy.wait()

    def branch(index, where):
        return mm(att_ref[index, where, :], wo_ref[...]) + mm(near[index, where, :], wo_near_ref[...])

    def exchange(kind, value_of):
        copies = []
        for c, where in enumerate(chunks):
            outbox[where, :] = value_of(where).astype(BF16)
            copies.append(post(kind, c, outbox.at[where], inbox.at[where], far))
        return copies

    branch_copies = exchange(BRANCH, lambda where: branch(1, where))
    for where in chunks:
        hat[where, :] = tok_ref[where, :].astype(F32) + branch(0, where)

    def by_parts(c, part):
        step = 64

        def run(i, carry):
            part(pl.ds(pl.multiple_of(c * chunk + i * step, step), step))
            return carry

        lax.fori_loop(0, chunk // step, run, 0)

    def mean(values):
        return jnp.sum(values, axis=-1, keepdims=True) * (1.0 / width)

    def add_up(index, values):
        sums[index] += jnp.sum(values.reshape(values.shape[0] // 8, 8, width), axis=0)

    def norm_one(where):
        h = hat[where, :] + inbox[where, :].astype(F32)
        h = h - mean(h)
        r = lax.rsqrt(mean(h * h) + EPSILON)
        h = h * r
        hat[where, :] = h
        r1[where, :] = jnp.broadcast_to(r, (r.shape[0], LANES))
        h = h * scale_one + shift_one
        res[where, :] = h
        low[0, where, :] = h.astype(BF16)

    normed_copies = []
    for c, where in enumerate(chunks):
        branch_copies[c].wait()
        by_parts(c, norm_one)
        normed_copies.append(post(NORMED, c, low.at[0, where], low.at[1, where], far))
    for fetch in fetches:
        fetch.wait()

    tile = hidden // 2

    def mlp(side, where):
        def columns(t, carry):
            k, at = t // 2, (t % 2) * tile
            x = low[side, where, :]
            gate_at = pl.ds(pl.multiple_of(at, LANES), tile)
            up_at = pl.ds(pl.multiple_of(hidden + at, LANES), tile)
            gate, up = mm(x, win[k, :, gate_at]), mm(x, win[k, :, up_at])
            gu[side, k, where, gate_at] = gate.astype(BF16)
            gu[side, k, where, up_at] = up.astype(BF16)
            value = gate * jax.nn.sigmoid(gate) * up
            hid[side, where, pl.ds(pl.multiple_of(k * hidden + at, LANES), tile)] = value.astype(BF16)
            return carry

        lax.fori_loop(0, 4, columns, 0)
        return mm(hid[side, where, :], wdn[...])

    def both_sides(copies_in, kind, compute):
        copies = []
        for c, where in enumerate(chunks):
            own[where, :] = compute(0, where)
            copies_in[c].wait()
            outbox[where, :] = compute(1, where).astype(BF16)
            copies.append(post(kind, c, outbox.at[where], inbox.at[where], far))
        return copies

    out_copies = both_sides(normed_copies, OUT, mlp)

    def norm_two(where):
        z = res[where, :] + own[where, :] + inbox[where, :].astype(F32)
        z = z - mean(z)
        r = lax.rsqrt(mean(z * z) + EPSILON)
        z = z * r
        out_ref[where, :] = (z * scale_two + shift_two).astype(BF16)
        g = cot_ref[where, :].astype(F32)
        add_up(2, g * z)
        add_up(3, g)
        e = g * scale_two
        dz = r * (e - mean(e) - z * mean(e * z))
        res[where, :] = dz
        dlow[0, where, :] = dz.astype(BF16)

    dout_copies = []
    for c, where in enumerate(chunks):
        out_copies[c].wait()
        by_parts(c, norm_two)
        dout_copies.append(post(DOUT, c, dlow.at[0, where], dlow.at[1, where], far))

    def mlp_back(side, where):
        def columns(t, carry):
            k, at = t // 2, (t % 2) * tile
            d_hidden = mm(
                dlow[side, where, :], wdn[pl.ds(pl.multiple_of(k * hidden + at, LANES), tile), :], NT
            )
            gate_at = pl.ds(pl.multiple_of(at, LANES), tile)
            up_at = pl.ds(pl.multiple_of(hidden + at, LANES), tile)
            gate, up = gu[side, k, where, gate_at].astype(F32), gu[side, k, where, up_at].astype(F32)
            s = jax.nn.sigmoid(gate)
            gu[side, k, where, gate_at] = (d_hidden * up * s * (1.0 + gate * (1.0 - s))).astype(BF16)
            gu[side, k, where, up_at] = (d_hidden * gate * s).astype(BF16)
            return carry

        lax.fori_loop(0, 4, columns, 0)
        return mm(gu[side, 0, where, :], win[0], NT) + mm(gu[side, 1, where, :], win[1], NT)

    dnormed_copies = both_sides(dout_copies, DNORMED, mlp_back)

    def weight_grads(k, target):
        def chain(r, carry):
            at = pl.ds(pl.multiple_of(r * half, LANES), half)
            for n, place in enumerate((slice(0, hidden), slice(hidden, 2 * hidden))):
                piece = mm(low[0, :, at], gu[0, k, :, place], TN) + mm(low[1, :, at], gu[1, k, :, place], TN)
                target[r, n * half : (n + 1) * half, :] = piece.astype(target.dtype)
            at = pl.ds(pl.multiple_of(k * hidden + r * half, LANES), half)
            piece = mm(hid[0, :, at], dlow[0], TN) + mm(hid[1, :, at], dlow[1], TN)
            target[r, 2 * half : 3 * half, :] = piece.astype(target.dtype)
            return carry

        lax.fori_loop(0, 2, chain, 0)

    weight_grads(1, give)
    grad_copies = [post(GRAD_NEAR, r, give.at[r], take.at[r], core) for r in range(2)]

    def norm_one_back(where):
        d = res[where, :] + own[where, :] + inbox[where, :].astype(F32)
        h = hat[where, :]
        add_up(0, d * h)
        add_up(1, d)
        e = d * scale_one
        dh = r1[where, 0:1] * (e - mean(e) - h * mean(e * h))
        dh_ref[where, :] = dh
        slots_ref[0, where, :] = dh.astype(BF16)

    dh_copies, last_copies = [], []

    def dh_chunk(c):
        where = chunks[c]
        dnormed_copies[c].wait()
        by_parts(c, norm_one_back)
        mine = slots_ref.at[0, where]
        dh_copies.append(post(DH, c, mine, slots_ref.at[1, where], far))
        last_copies.append(post(DH_NEAR, c, mine, slots_ref.at[2, where], core))

    dh_chunk(0)
    weight_grads(0, total)
    dh_chunk(1)
    size_rows = total.shape[1] // 2
    dp_copies, keeps = [], []
    for r in range(2):
        grad_copies[r].wait()
        total[r] += take[r].astype(F32)
        partner, mine = peer_of(me, firsts[r])
        away = pl.ds(pl.multiple_of((1 - mine) * size_rows, 16), size_rows)
        keeps.append(pl.ds(pl.multiple_of(mine * size_rows, 16), size_rows))
        give[r, :size_rows, :] = total[r, away, :].astype(BF16)
        dp_copies.append(post(GRAD_DP, r, give.at[r, pl.ds(0, size_rows)], take_dp.at[r], {"dp": partner}))
    for c, where in enumerate(chunks):
        dh_copies[c].wait()
        last_copies.append(post(DH_LAST, c, slots_ref.at[1, where], slots_ref.at[3, where], core))
    for i in range(4):
        norms_ref[i : i + 1, :] = jnp.sum(sums[i], axis=0, keepdims=True)
    norms_ref[4:8, :] = jnp.zeros((4, width), F32)
    writes = []
    for r in range(2):
        dp_copies[r].wait()
        total[r, keeps[r], :] += take_dp[r].astype(F32)
        writes.append(pltpu.make_async_copy(total.at[r, keeps[r]], kept_hbm.at[r], stores.at[r]))
        writes[-1].start()
    for copy in last_copies + writes:
        copy.wait()


def middle(att, w_out, w_out_near, tokens, cotangent, norms, w_in, w_in_near, w_down, w_down_near):
    size = lax.axis_size("dp")
    shards, rows, cols = att.shape
    width = tokens.shape[1]
    hidden = w_down.shape[0]
    chain = 3 * width // 2
    vmem = pl.BlockSpec(memory_space=pltpu.VMEM)
    hbm = pl.BlockSpec(memory_space=pl.ANY)
    dma = pltpu.SemaphoreType.DMA
    return pl.pallas_call(
        functools.partial(middle_kernel, size),
        out_shape=(
            jax.ShapeDtypeStruct((rows, width), BF16),
            jax.ShapeDtypeStruct((rows, width), F32),
            jax.ShapeDtypeStruct((shards, rows, width), BF16),
            jax.ShapeDtypeStruct((8, width), F32),
            jax.ShapeDtypeStruct((2, chain // 2, width), F32),
        ),
        in_specs=[vmem] * 6 + [hbm] * 4,
        out_specs=[vmem] * 4 + [hbm],
        scratch_shapes=[
            pltpu.VMEM((2, width, 2 * hidden), BF16),
            pltpu.VMEM((2 * hidden, width), BF16),
            pltpu.VMEM((2, rows, cols), BF16),
            pltpu.VMEM((rows, width), BF16),
            pltpu.VMEM((rows, width), BF16),
            pltpu.VMEM((2, rows, width), BF16),
            pltpu.VMEM((rows, width), F32),
            pltpu.VMEM((rows, width), F32),
            pltpu.VMEM((rows, width), F32),
            pltpu.VMEM((rows, LANES), F32),
            pltpu.VMEM((2, 2, rows, 2 * hidden), BF16),
            pltpu.VMEM((2, rows, 2 * hidden), BF16),
            pltpu.VMEM((2, rows, width), BF16),
            pltpu.VMEM((2, chain, width), F32),
            pltpu.VMEM((2, chain, width), BF16),
            pltpu.VMEM((2, chain, width), BF16),
            pltpu.VMEM((2, chain // 2, width), BF16),
            pltpu.VMEM((4, 8, width), F32),
            dma((2, 11, 2)),
            dma((4,)),
            dma((2,)),
        ],
        compiler_params=pltpu.CompilerParams(
            collective_id=0, has_side_effects=True, vmem_limit_bytes=WIDE_LIMIT
        ),
        cost_estimate=pl.CostEstimate(
            flops=36 * rows * width * hidden, bytes_accessed=40 * rows * width, transcendentals=0
        ),
        name="middle",
    )(att, w_out, w_out_near, tokens, cotangent, norms, w_in, w_in_near, w_down, w_down_near)


class Sum:
    def __init__(self, size, me, first, total, give, take, result, sems):
        self.orders, self.me = dp_orders(size), me
        self.halving, self.stages = halvings(size), size.bit_length() - 1
        self.total, self.give, self.take, self.result, self.sems = total, give, take, result, sems
        self.count = 1 << (self.halving - first)
        self.rows = total.shape[1] // self.count
        self.stage = first
        self.lows, self.bases = [0, 0], [0, 0]
        for chain in range(2):
            for done in range(first):
                mine = peer_of(me, self.orders[chain][done])[1]
                self.bases[chain] = self.bases[chain] + mine * (1 << (self.halving - 1 - done))
        self.copies = None
        self.spot = 0
        self.down = self.stages - 1

    def block(self, low, count):
        return pl.ds(pl.multiple_of(low * self.rows, 16), count * self.rows)

    def sem(self, chain, step, partner, source, target):
        return send(source, target, self.sems.at[0, chain, step], self.sems.at[1, chain, step], partner)

    def start(self):
        halve = self.stage < self.halving
        part = self.count // 2 if halve else self.count
        self.copies, self.keeps = [], []
        spot = pl.ds(self.spot, part * self.rows)
        for chain in range(2):
            peer, mine = peer_of(self.me, self.orders[chain][self.stage])
            away = self.lows[chain] + (1 - mine) * part if halve else self.lows[chain]
            self.keeps.append(self.lows[chain] + mine * part if halve else self.lows[chain])
            self.give[chain, spot, :] = self.total[chain, self.block(away, part), :].astype(BF16)
            self.copies.append(
                self.sem(chain, self.stage, {"dp": peer}, self.give.at[chain, spot], self.take.at[chain, spot])
            )

    def finish(self):
        halve = self.stage < self.halving
        part = self.count // 2 if halve else self.count
        spot = pl.ds(self.spot, part * self.rows)
        for chain in range(2):
            self.copies[chain].wait()
            keep = self.block(self.keeps[chain], part)
            mine = self.total[chain, keep, :] if halve else self.give[chain, spot, :].astype(F32)
            self.total[chain, keep, :] = mine + self.take[chain, spot, :].astype(F32)
        self.lows, self.count = self.keeps, part
        self.spot += part * self.rows
        self.stage += 1
        if self.stage == self.stages:
            for chain in range(2):
                low = self.lows[chain]
                self.lows[chain] = self.bases[chain] + low
                self.result[chain, self.block(self.lows[chain], 1), :] = self.total[
                    chain, self.block(low, 1), :
                ].astype(BF16)
            self.stage = self.halving - 1

    def start_gather(self):
        self.copies = []
        for chain in range(2):
            peer, mine = peer_of(self.me, self.orders[chain][self.stage])
            spot = self.result.at[chain, self.block(self.lows[chain], self.count)]
            self.copies.append(self.sem(chain, self.stages + self.stage, {"dp": peer}, spot, spot))
            self.lows[chain] = self.lows[chain] - mine * self.count

    def finish_gather(self):
        for copy in self.copies:
            copy.wait()
        self.count *= 2
        self.stage -= 1


def finish_kernel(
    size, x_ref, dq_ref, w_ref, w_near_ref, dh_ref, norms_ref, att_ref, slots_ref, kept_ref,
    dx_ref, grad_ref, big_ref, sums_ref,
    total, give, take, big, big_give, big_take, near, far_out, far_in, own, norm_in,
    near_sem, far_sem, sum_sems, big_sems, norm_sem, load,
):
    half = x_ref.shape[2] // 2
    cols = dq_ref.shape[2]
    m, me = lax.axis_index("mp"), lax.axis_index("dp")
    stages = size.bit_length() - 1
    core, far = {"mp": peer_of(m, 0)[0]}, {"mp": peer_of(m, 1)[0]}
    partners = [core, far] + [{"dp": peer_of(me, bit)[0]} for bit in range(stages)]
    fetch = pltpu.make_async_copy(kept_ref, big, load)
    fetch.start()
    greet(partners)
    near_copy = send(dq_ref.at[pl.ds(2, 2)], near, near_sem.at[0], near_sem.at[1], core)
    sums_ref[...] = norms_ref[...]
    large = Sum(size, me, 1, big, big_give, big_take, big_ref, big_sems)
    small = Sum(size, me, 0, total, give, take, grad_ref, sum_sems)
    fetch.wait()
    large.start()

    for chain in range(2):
        for part in range(0, half, LANES):
            at = chain * half + part
            piece = mm(x_ref[0, :, at : at + LANES], dq_ref[0], TN)
            for slot in range(1, x_ref.shape[0]):
                piece += mm(x_ref[slot, :, at : at + LANES], dq_ref[slot], TN)
            total[chain, part : part + LANES, :cols] = piece
            piece = mm(slots_ref[0, :, at : at + LANES], att_ref[0], TN)
            for slot in range(1, x_ref.shape[0]):
                piece += mm(slots_ref[slot, :, at : at + LANES], att_ref[slot], TN)
            total[chain, part : part + LANES, cols:] = piece
    small.start()

    def norm_exchange(stage):
        return send(sums_ref, norm_in.at[stage], norm_sem.at[0, stage], norm_sem.at[1, stage], partners[stage])

    def norm_add(stage, copy):
        copy.wait()
        sums_ref[...] += norm_in[stage]

    norm_copy, norm_done = norm_exchange(0), 0
    near_copy.wait()
    d_far = mm(dq_ref[1], w_ref[...], NT) + mm(near[1], w_near_ref[...], NT)
    far_out[...] = d_far.astype(BF16)
    far_copy = send(far_out, far_in, far_sem.at[0], far_sem.at[1], far)
    own[...] = dh_ref[...] + mm(dq_ref[0], w_ref[...], NT) + mm(near[0], w_near_ref[...], NT)

    plans = [[], []]
    for plan, one, first in ((plans[0], large, 1), (plans[1], small, 0)):
        for _ in range(stages - first):
            plan.append((one.start, one.finish))
        for _ in range(halvings(size)):
            plan.append((one.start_gather, one.finish_gather))
    steps = max(len(plan) for plan in plans)
    for step in range(steps):
        for plan in plans:
            if step > 0 and step < len(plan):
                plan[step][0]()
        for plan in plans:
            if step < len(plan):
                plan[step][1]()
        if norm_done < len(partners):
            norm_add(norm_done, norm_copy)
            norm_done += 1
            if norm_done < len(partners):
                norm_copy = norm_exchange(norm_done)
    while norm_done < len(partners):
        norm_add(norm_done, norm_copy)
        norm_done += 1
        if norm_done < len(partners):
            norm_copy = norm_exchange(norm_done)
    far_copy.wait()
    dx_ref[...] = (own[...] + far_in[...].astype(F32)).astype(BF16)


def finish(x_slots, d_qkv, w_qkv, w_near, dh, norms, att, dh_slots, kept):
    size = lax.axis_size("dp")
    stages = size.bit_length() - 1
    slots, rows, width = x_slots.shape
    cols = d_qkv.shape[2]
    all_cols = cols + att.shape[2]
    chain = kept.shape[1] * 2
    vmem = pl.BlockSpec(memory_space=pltpu.VMEM)
    dma = pltpu.SemaphoreType.DMA
    return pl.pallas_call(
        functools.partial(finish_kernel, size),
        out_shape=(
            jax.ShapeDtypeStruct((rows, width), BF16),
            jax.ShapeDtypeStruct((2, width // 2, all_cols), BF16),
            jax.ShapeDtypeStruct((2, chain, width), BF16),
            jax.ShapeDtypeStruct(norms.shape, F32),
        ),
        in_specs=[vmem] * 8 + [pl.BlockSpec(memory_space=pl.ANY)],
        out_specs=[vmem] * 4,
        scratch_shapes=[
            pltpu.VMEM((2, width // 2, all_cols), F32),
            pltpu.VMEM((2, width, all_cols), BF16),
            pltpu.VMEM((2, width, all_cols), BF16),
            pltpu.VMEM(kept.shape, F32),
            pltpu.VMEM((2, chain, width), BF16),
            pltpu.VMEM((2, chain, width), BF16),
            pltpu.VMEM((2, rows, cols), BF16),
            pltpu.VMEM((rows, width), BF16),
            pltpu.VMEM((rows, width), BF16),
            pltpu.VMEM((rows, width), F32),
            pltpu.VMEM((2 + stages,) + norms.shape, F32),
            dma((2,)),
            dma((2,)),
            dma((2, 2, 2 * stages)),
            dma((2, 2, 2 * stages)),
            dma((2, 2 + stages)),
            dma,
        ],
        compiler_params=pltpu.CompilerParams(
            collective_id=1, has_side_effects=True, vmem_limit_bytes=WIDE_LIMIT
        ),
        cost_estimate=pl.CostEstimate(
            flops=6 * slots * rows * width * cols, bytes_accessed=12 * rows * width, transcendentals=0
        ),
        name="finish",
    )(x_slots, d_qkv, w_qkv, w_near, dh, norms, att, dh_slots, kept)


def body(
    tokens, lengths, w_qkv, w_out, w_gate_up, w_down, ln1_scale, ln1_shift, ln2_scale, ln2_shift, cotangent
):
    rows, width = tokens.shape
    shards = lax.axis_size("mp")
    length = rows * shards
    local_cols = w_out.shape[0]
    heads = local_cols // HEAD_DIM
    hidden_cols = w_down.shape[0]
    m = lax.axis_index("mp")

    def swap(values, distance):
        return lax.ppermute(values, "mp", [(i, i ^ distance) for i in range(shards)])

    across = lambda values: swap(values, 2)
    beside = lambda values: swap(values, 1)

    x_far = across(tokens)
    x_near = beside(tokens)
    x_last = beside(x_far)
    positions, key_tiles, query_tiles, bounds = doc_tables(lengths[0], length, rows)
    cosine, sine = rotary(positions)
    place = jnp.stack([m.astype(jnp.int32)] + [jnp.int32(r) for r in (0, 2, 1, 3)])
    flat_qkv = w_qkv.reshape(width, 3 * local_cols)
    w_qkv_near = beside(flat_qkv)
    w_out_near = beside(w_out)
    flat_gate_up = w_gate_up.reshape(width, 2 * hidden_cols)
    w_gate_up_near = beside(flat_gate_up)
    w_down_near = beside(w_down)
    x_slots = jnp.stack([tokens, x_far, x_near, x_last])
    q, k, v, k_rows = project(x_slots, flat_qkv.T, cosine, sine, bounds, place, heads)
    att, att_along, q_rows = attend(q, k_rows, v, place, key_tiles, shards)
    norms = jnp.concatenate([jnp.stack([ln1_scale, ln1_shift, ln2_scale, ln2_shift]), jnp.zeros((4, width), F32)])
    output, dh, dh_slots, norms, kept = middle(
        att, w_out, w_out_near, tokens, cotangent, norms, flat_gate_up, w_gate_up_near, w_down, w_down_near
    )
    d_qkv = attend_back(
        q_rows, q, k_rows, k, v, att_along, dh_slots, w_out, cosine, sine, place, query_tiles
    )
    d_tokens, grads, grads_in, norms = finish(
        x_slots, d_qkv, flat_qkv, w_qkv_near, dh, norms, att, dh_slots, kept
    )
    grads = grads.reshape(width, 4 * local_cols).astype(F32)
    grad_qkv, grad_out = grads[:, : 3 * local_cols], grads[:, 3 * local_cols :].T
    half = width // 2
    parts = [grads_in[:, i * half : (i + 1) * half].reshape(width, width).astype(F32) for i in range(3)]
    grad_gate_up, grad_down = jnp.stack(parts[:2], axis=1), parts[2]
    norms = lax.dynamic_slice_in_dim(norms, m * local_cols, local_cols, 1)
    return (
        output,
        d_tokens,
        grad_qkv.reshape(width, 3, local_cols),
        grad_out,
        grad_gate_up.reshape(width, 2, hidden_cols),
        grad_down,
        norms[0],
        norms[1],
        norms[2],
        norms[3],
    )


def solution(mesh):
    return jax.shard_map(
        body,
        mesh=mesh,
        in_specs=(
            P(("dp", "mp"), None),
            P("dp", None),
            P(None, None, "mp"),
            P("mp", None),
            P(None, None, "mp"),
            P("mp", None),
            P(),
            P(),
            P(),
            P(),
            P(("dp", "mp"), None),
        ),
        out_specs=(
            P(("dp", "mp"), None),
            P(("dp", "mp"), None),
            P(None, None, "mp"),
            P("mp", None),
            P(None, None, "mp"),
            P("mp", None),
            P("mp"),
            P("mp"),
            P("mp"),
            P("mp"),
        ),
        check_vma=False,
    )
```

```python
import functools
import math

import jax
import jax.numpy as jnp
from jax import lax
from jax.experimental import pallas as pl
from jax.experimental.pallas import tpu as pltpu
from jax.sharding import PartitionSpec as P

F32 = jnp.float32
BF16 = jnp.bfloat16
HEAD_DIM = 64
LANES = 128
EPSILON = 1e-05
KEYS = 512
FAR = -(2.0**100)
LOG2E = math.log2(math.e)
NT = (((1,), (1,)), ((), ()))
TN = (((0,), (0,)), ((), ()))
NN = (((1,), (0,)), ((), ()))
VMEM_LIMIT = 58 << 20
WIDE_LIMIT = 62 << 20
MESH = pl.DeviceIdType.MESH


def mm(a, b, dims=NN):
    return lax.dot_general(a, b, dims, preferred_element_type=F32)


def thirds(row):
    high = row.astype(BF16).astype(F32)
    mid = (row - high).astype(BF16).astype(F32)
    low = row - high - mid
    return jnp.concatenate([high, mid, low, jnp.zeros((13, row.shape[1]), F32)], axis=0)


def slot_of(relative):
    return relative // 2 + 2 * (relative % 2)


def span(index, size):
    return pl.ds(pl.multiple_of(index * size, size), size)


def project_kernel(place, x_ref, w_ref, cos_ref, sin_ref, bounds_ref, q_ref, k_ref, v_ref, k_rows_ref):
    rows = x_ref.shape[1]
    heads = q_ref.shape[0]
    width = heads * HEAD_DIM
    shard = place[0] ^ place[1 + pl.program_id(0)]
    projected = mm(w_ref[...], x_ref[0], NT)
    cosine, sine = cos_ref[...], sin_ref[...]
    token = lax.broadcasted_iota(jnp.int32, (16, rows), 1) + shard * rows
    inside = (token >= bounds_ref[:, 0:1]) & (token < bounds_ref[:, 1:2])
    row = lax.broadcasted_iota(jnp.int32, (48, rows), 0)
    q_tail = jnp.concatenate([jnp.where(inside, 0.0, FAR), jnp.zeros((48 - 16 + 16, rows), F32)], axis=0)
    ones = jnp.where(row < 3, 1.0, 0.0)
    k_tail = jnp.concatenate([jnp.where(inside, 1.0, 0.0), ones], axis=0)
    v_tail = jnp.concatenate([ones, jnp.zeros((16, rows), F32)], axis=0)
    half = HEAD_DIM // 2

    def rotated(start):
        first, second = projected[start : start + half], projected[start + half : start + HEAD_DIM]
        return first * cosine - second * sine, second * cosine + first * sine

    scale = LOG2E / math.sqrt(HEAD_DIM)
    for h in range(heads):
        first, second = rotated(h * HEAD_DIM)
        q_ref[h] = jnp.concatenate([first * scale, second * scale, q_tail], axis=0).astype(BF16)
        first, second = rotated(width + h * HEAD_DIM)
        k = jnp.concatenate([first, second, k_tail], axis=0)
        k_ref[h] = k.astype(BF16)
        k_rows_ref[h] = k.T.astype(BF16)
        start = 2 * width + h * HEAD_DIM
        v_ref[h] = jnp.concatenate([projected[start : start + HEAD_DIM], v_tail], axis=0).astype(BF16)


def project(x_slots, w_turned, cosine, sine, bounds, place, heads):
    count, rows, width = x_slots.shape
    tokens = count * rows
    along = jax.ShapeDtypeStruct((heads, LANES, tokens), BF16)
    down = jax.ShapeDtypeStruct((heads, tokens, LANES), BF16)
    whole = lambda *shape: pl.BlockSpec(shape, lambda s, place: (0,) * len(shape))
    table = pl.BlockSpec((HEAD_DIM // 2, rows), lambda s, place: (0, place[0] ^ place[1 + s]))
    along_spec = pl.BlockSpec((heads, LANES, rows), lambda s, place: (0, 0, place[0] ^ place[1 + s]))
    down_spec = pl.BlockSpec((heads, rows, LANES), lambda s, place: (0, place[0] ^ place[1 + s], 0))
    return pl.pallas_call(
        project_kernel,
        out_shape=(along, along, along, down),
        grid_spec=pltpu.PrefetchScalarGridSpec(
            num_scalar_prefetch=1,
            grid=(count,),
            in_specs=[
                pl.BlockSpec((1, rows, width), lambda s, place: (s, 0, 0)),
                whole(*w_turned.shape),
                table,
                table,
                whole(*bounds.shape),
            ],
            out_specs=[along_spec] * 3 + [down_spec],
        ),
        compiler_params=pltpu.CompilerParams(vmem_limit_bytes=VMEM_LIMIT),
        cost_estimate=pl.CostEstimate(
            flops=2 * tokens * width * w_turned.shape[0],
            bytes_accessed=tokens * width * 2 + 4 * heads * tokens * LANES * 2,
            transcendentals=0,
        ),
        name="project",
    )(place, x_slots, w_turned, cosine, sine, bounds)


def attend_kernel(place, ranges, q_ref, k_ref, v_ref, o_ref, o_along_ref, q_rows_ref, top_ref, acc_ref):
    heads = q_ref.shape[0]
    i = pl.program_id(0)
    tiles = pl.num_programs(0)
    top_ref[...] = jnp.full_like(top_ref, FAR)
    acc_ref[...] = jnp.zeros_like(acc_ref)

    def over_keys(j, carry):
        for h in range(heads):
            s = mm(k_ref[h, span(j, KEYS), :], q_ref[h])
            old = top_ref[h, 0:1, :]
            top = jnp.maximum(old, jnp.max(s, axis=0, keepdims=True))
            probs = jnp.exp2(s - top).astype(BF16)
            top_ref[h, 0:1, :] = top
            acc_ref[h] = acc_ref[h] * jnp.exp2(old - top) + mm(v_ref[h, :80, span(j, KEYS)], probs)
        return carry

    lax.fori_loop(ranges[i], ranges[tiles + i] + 1, over_keys, 0)
    outs = []
    for h in range(heads):
        total = acc_ref[h, HEAD_DIM : HEAD_DIM + 1, :]
        outs.append(acc_ref[h, :HEAD_DIM, :] / total)
        level = top_ref[h, 0:1, :] + jnp.log2(total)
        query = q_ref[h].astype(F32)
        q_rows_ref[h] = jnp.concatenate([query[:80], thirds(-level), query[96:]], axis=0).T.astype(BF16)
    out = jnp.concatenate(outs, axis=0)
    o_along_ref[...] = out.astype(BF16)
    o_ref[0] = out.T.astype(BF16)


def attend(q, k_rows, v, place, ranges, shards):
    heads, _, tokens = q.shape
    rows = tokens // shards
    whole = lambda *shape: pl.BlockSpec(shape, lambda i, place, ranges: (0, 0, 0))
    return pl.pallas_call(
        attend_kernel,
        out_shape=(
            jax.ShapeDtypeStruct((shards, rows, heads * HEAD_DIM), BF16),
            jax.ShapeDtypeStruct((heads * HEAD_DIM, tokens), BF16),
            jax.ShapeDtypeStruct((heads, tokens, LANES), BF16),
        ),
        grid_spec=pltpu.PrefetchScalarGridSpec(
            num_scalar_prefetch=2,
            grid=(shards,),
            in_specs=[
                pl.BlockSpec((heads, LANES, rows), lambda i, place, ranges: (0, 0, i)),
                whole(heads, tokens, LANES),
                whole(heads, LANES, tokens),
            ],
            out_specs=[
                pl.BlockSpec(
                    (1, rows, heads * HEAD_DIM), lambda i, place, ranges: (slot_of(i ^ place[0]), 0, 0)
                ),
                pl.BlockSpec((heads * HEAD_DIM, rows), lambda i, place, ranges: (0, i)),
                pl.BlockSpec((heads, rows, LANES), lambda i, place, ranges: (0, i, 0)),
            ],
            scratch_shapes=[pltpu.VMEM((heads, 8, rows), F32), pltpu.VMEM((heads, 80, rows), F32)],
        ),
        compiler_params=pltpu.CompilerParams(vmem_limit_bytes=VMEM_LIMIT),
        cost_estimate=pl.CostEstimate(
            flops=2 * heads * tokens * tokens * LANES,
            bytes_accessed=5 * heads * tokens * LANES * 2,
            transcendentals=heads * tokens * tokens // 2,
        ),
        name="attend",
    )(place, ranges, q, k_rows, v)


def doc_tables(lengths, tokens, rows):
    ends = jnp.cumsum(lengths)
    starts = ends - lengths
    places = jnp.arange(tokens, dtype=jnp.int32)
    inside = (places[:, None] >= starts[None, :]) & (places[:, None] < ends[None, :])
    positions = places - jnp.sum(jnp.where(inside, starts[None, :], 0), axis=1)

    def shared(size, other):
        edge = jnp.arange(tokens // size, dtype=jnp.int32) * size
        touches = (starts[None, :] < edge[:, None] + size) & (ends[None, :] > edge[:, None])
        first = jnp.min(jnp.where(touches, starts[None, :], tokens), axis=1) // other
        last = (jnp.max(jnp.where(touches, ends[None, :], 0), axis=1) - 1) // other
        return jnp.concatenate([first, last]).astype(jnp.int32)

    bounds = jnp.stack([starts, ends], axis=1).astype(jnp.int32)
    return positions, shared(rows, KEYS), bounds


def rotary(positions):
    rate = jnp.exp(jnp.arange(HEAD_DIM // 2, dtype=F32) * (-2.0 * math.log(1000.0) / HEAD_DIM))
    angles = rate[:, None] * positions.astype(F32)[None, :]
    return jnp.cos(angles), jnp.sin(angles)


def dp_orders(size):
    bits = list(range(size.bit_length() - 1))
    return [bits, bits[1::-1] + bits[2:]]


def halvings(size):
    return min(3, size.bit_length() - 1)


def peer_of(index, bit):
    mine = (index // (1 << bit)) % 2
    return index + (1 - 2 * mine) * (1 << bit), mine


def send(source, target, send_sem, recv_sem, partner):
    copy = pltpu.make_async_remote_copy(
        source, target, send_sem, recv_sem, device_id=partner, device_id_type=MESH
    )
    copy.start()
    return copy


def greet(partners):
    barrier = pltpu.get_barrier_semaphore()
    for partner in partners:
        pl.semaphore_signal(barrier, inc=1, device_id=partner, device_id_type=MESH)
    pl.semaphore_wait(barrier, len(partners))


ATT, BRANCH, NORMED, OUT, DOUT, DNORMED, DH, DH_NEAR, DH_LAST, GRAD_NEAR, GRAD_DP = range(11)


def middle_kernel(
    size, att_ref, wo_ref, wo_near_ref, tok_ref, cot_ref, ln_ref, win_hbm, win_near_hbm, wdn_hbm, wdn_near_hbm,
    out_ref, dh_ref, slots_ref, norms_ref, kept_hbm,
    win, wdn, near, outbox, inbox, low, hat, res, own, r1, gu, hid, dlow, total, give, take, take_dp, sums,
    sems, loads, stores,
):
    rows, width = tok_ref.shape
    hidden = wdn.shape[0] // 2
    half = width // 2
    chunk = rows // 2
    chunks = [slice(c * chunk, (c + 1) * chunk) for c in range(2)]
    m, me = lax.axis_index("mp"), lax.axis_index("dp")
    core, far = {"mp": peer_of(m, 0)[0]}, {"mp": peer_of(m, 1)[0]}
    firsts = [order[0] for order in dp_orders(size)]
    greet([core, far] + [{"dp": peer_of(me, bit)[0]} for bit in sorted(set(firsts))])

    def post(kind, c, source, target, partner):
        return send(source, target, sems.at[0, kind, c], sems.at[1, kind, c], partner)

    att_copy = post(ATT, 0, att_ref.at[pl.ds(2, 2)], near, core)
    fetches = []
    for n, (source, target) in enumerate(
        [
            (win_hbm, win.at[0]),
            (win_near_hbm, win.at[1]),
            (wdn_hbm, wdn.at[pl.ds(0, hidden)]),
            (wdn_near_hbm, wdn.at[pl.ds(hidden, hidden)]),
        ]
    ):
        fetches.append(pltpu.make_async_copy(source, target, loads.at[n]))
        fetches[-1].start()
    sums[...] = jnp.zeros_like(sums)
    scale_one, shift_one, scale_two, shift_two = (ln_ref[i : i + 1, :] for i in range(4))
    att_copy.wait()

    def branch(index, where):
        return mm(att_ref[index, where, :], wo_ref[...]) + mm(near[index, where, :], wo_near_ref[...])

    def exchange(kind, value_of):
        copies = []
        for c, where in enumerate(chunks):
            outbox[where, :] = value_of(where).astype(BF16)
            copies.append(post(kind, c, outbox.at[where], inbox.at[where], far))
        return copies

    branch_copies = exchange(BRANCH, lambda where: branch(1, where))
    for where in chunks:
        hat[where, :] = tok_ref[where, :].astype(F32) + branch(0, where)

    def by_parts(c, part):
        step = 64

        def run(i, carry):
            part(pl.ds(pl.multiple_of(c * chunk + i * step, step), step))
            return carry

        lax.fori_loop(0, chunk // step, run, 0)

    def mean(values):
        return jnp.sum(values, axis=-1, keepdims=True) * (1.0 / width)

    def add_up(index, values):
        sums[index] += jnp.sum(values.reshape(values.shape[0] // 8, 8, width), axis=0)

    def norm_one(where):
        h = hat[where, :] + inbox[where, :].astype(F32)
        h = h - mean(h)
        r = lax.rsqrt(mean(h * h) + EPSILON)
        h = h * r
        hat[where, :] = h
        r1[where, :] = jnp.broadcast_to(r, (r.shape[0], LANES))
        h = h * scale_one + shift_one
        res[where, :] = h
        low[0, where, :] = h.astype(BF16)

    normed_copies = []
    for c, where in enumerate(chunks):
        branch_copies[c].wait()
        by_parts(c, norm_one)
        normed_copies.append(post(NORMED, c, low.at[0, where], low.at[1, where], far))
    for fetch in fetches:
        fetch.wait()

    tile = hidden // 2

    def mlp(side, where):
        def columns(t, carry):
            k, at = t // 2, (t % 2) * tile
            x = low[side, where, :]
            gate_at = pl.ds(pl.multiple_of(at, LANES), tile)
            up_at = pl.ds(pl.multiple_of(hidden + at, LANES), tile)
            gate, up = mm(x, win[k, :, gate_at]), mm(x, win[k, :, up_at])
            gu[side, k, where, gate_at] = gate.astype(BF16)
            gu[side, k, where, up_at] = up.astype(BF16)
            value = gate * jax.nn.sigmoid(gate) * up
            hid[side, where, pl.ds(pl.multiple_of(k * hidden + at, LANES), tile)] = value.astype(BF16)
            return carry

        lax.fori_loop(0, 4, columns, 0)
        return mm(hid[side, where, :], wdn[...])

    def both_sides(copies_in, kind, compute):
        copies = []
        for c, where in enumerate(chunks):
            own[where, :] = compute(0, where)
            copies_in[c].wait()
            outbox[where, :] = compute(1, where).astype(BF16)
            copies.append(post(kind, c, outbox.at[where], inbox.at[where], far))
        return copies

    out_copies = both_sides(normed_copies, OUT, mlp)

    def norm_two(where):
        z = res[where, :] + own[where, :] + inbox[where, :].astype(F32)
        z = z - mean(z)
        r = lax.rsqrt(mean(z * z) + EPSILON)
        z = z * r
        out_ref[where, :] = (z * scale_two + shift_two).astype(BF16)
        g = cot_ref[where, :].astype(F32)
        add_up(2, g * z)
        add_up(3, g)
        e = g * scale_two
        dz = r * (e - mean(e) - z * mean(e * z))
        res[where, :] = dz
        dlow[0, where, :] = dz.astype(BF16)

    dout_copies = []
    for c, where in enumerate(chunks):
        out_copies[c].wait()
        by_parts(c, norm_two)
        dout_copies.append(post(DOUT, c, dlow.at[0, where], dlow.at[1, where], far))

    def mlp_back(side, where):
        def columns(t, carry):
            k, at = t // 2, (t % 2) * tile
            d_hidden = mm(
                dlow[side, where, :], wdn[pl.ds(pl.multiple_of(k * hidden + at, LANES), tile), :], NT
            )
            gate_at = pl.ds(pl.multiple_of(at, LANES), tile)
            up_at = pl.ds(pl.multiple_of(hidden + at, LANES), tile)
            gate, up = gu[side, k, where, gate_at].astype(F32), gu[side, k, where, up_at].astype(F32)
            s = jax.nn.sigmoid(gate)
            gu[side, k, where, gate_at] = (d_hidden * up * s * (1.0 + gate * (1.0 - s))).astype(BF16)
            gu[side, k, where, up_at] = (d_hidden * gate * s).astype(BF16)
            return carry

        lax.fori_loop(0, 4, columns, 0)
        return mm(gu[side, 0, where, :], win[0], NT) + mm(gu[side, 1, where, :], win[1], NT)

    dnormed_copies = both_sides(dout_copies, DNORMED, mlp_back)

    def weight_grads(k, target):
        def chain(r, carry):
            at = pl.ds(pl.multiple_of(r * half, LANES), half)
            for n, place in enumerate((slice(0, hidden), slice(hidden, 2 * hidden))):
                piece = mm(low[0, :, at], gu[0, k, :, place], TN) + mm(low[1, :, at], gu[1, k, :, place], TN)
                target[r, n * half : (n + 1) * half, :] = piece.astype(target.dtype)
            at = pl.ds(pl.multiple_of(k * hidden + r * half, LANES), half)
            piece = mm(hid[0, :, at], dlow[0], TN) + mm(hid[1, :, at], dlow[1], TN)
            target[r, 2 * half : 3 * half, :] = piece.astype(target.dtype)
            return carry

        lax.fori_loop(0, 2, chain, 0)

    weight_grads(1, give)
    grad_copies = [post(GRAD_NEAR, r, give.at[r], take.at[r], core) for r in range(2)]

    def norm_one_back(where):
        d = res[where, :] + own[where, :] + inbox[where, :].astype(F32)
        h = hat[where, :]
        add_up(0, d * h)
        add_up(1, d)
        e = d * scale_one
        dh = r1[where, 0:1] * (e - mean(e) - h * mean(e * h))
        dh_ref[where, :] = dh
        slots_ref[0, where, :] = dh.astype(BF16)

    dh_copies, last_copies = [], []

    def dh_chunk(c):
        where = chunks[c]
        dnormed_copies[c].wait()
        by_parts(c, norm_one_back)
        mine = slots_ref.at[0, where]
        dh_copies.append(post(DH, c, mine, slots_ref.at[1, where], far))
        last_copies.append(post(DH_NEAR, c, mine, slots_ref.at[2, where], core))

    dh_chunk(0)
    weight_grads(0, total)
    dh_chunk(1)
    size_rows = total.shape[1] // 2
    dp_copies, keeps = [], []
    for r in range(2):
        grad_copies[r].wait()
        total[r] += take[r].astype(F32)
        partner, mine = peer_of(me, firsts[r])
        away = pl.ds(pl.multiple_of((1 - mine) * size_rows, 16), size_rows)
        keeps.append(pl.ds(pl.multiple_of(mine * size_rows, 16), size_rows))
        give[r, :size_rows, :] = total[r, away, :].astype(BF16)
        dp_copies.append(post(GRAD_DP, r, give.at[r, pl.ds(0, size_rows)], take_dp.at[r], {"dp": partner}))
    for c, where in enumerate(chunks):
        dh_copies[c].wait()
        last_copies.append(post(DH_LAST, c, slots_ref.at[1, where], slots_ref.at[3, where], core))
    for i in range(4):
        norms_ref[i : i + 1, :] = jnp.sum(sums[i], axis=0, keepdims=True)
    norms_ref[4:8, :] = jnp.zeros((4, width), F32)
    writes = []
    for r in range(2):
        dp_copies[r].wait()
        total[r, keeps[r], :] += take_dp[r].astype(F32)
        writes.append(pltpu.make_async_copy(total.at[r, keeps[r]], kept_hbm.at[r], stores.at[r]))
        writes[-1].start()
    for copy in last_copies + writes:
        copy.wait()


def middle(att, w_out, w_out_near, tokens, cotangent, norms, w_in, w_in_near, w_down, w_down_near):
    size = lax.axis_size("dp")
    shards, rows, cols = att.shape
    width = tokens.shape[1]
    hidden = w_down.shape[0]
    chain = 3 * width // 2
    vmem = pl.BlockSpec(memory_space=pltpu.VMEM)
    hbm = pl.BlockSpec(memory_space=pl.ANY)
    dma = pltpu.SemaphoreType.DMA
    return pl.pallas_call(
        functools.partial(middle_kernel, size),
        out_shape=(
            jax.ShapeDtypeStruct((rows, width), BF16),
            jax.ShapeDtypeStruct((rows, width), F32),
            jax.ShapeDtypeStruct((shards, rows, width), BF16),
            jax.ShapeDtypeStruct((8, width), F32),
            jax.ShapeDtypeStruct((2, chain // 2, width), F32),
        ),
        in_specs=[vmem] * 6 + [hbm] * 4,
        out_specs=[vmem] * 4 + [hbm],
        scratch_shapes=[
            pltpu.VMEM((2, width, 2 * hidden), BF16),
            pltpu.VMEM((2 * hidden, width), BF16),
            pltpu.VMEM((2, rows, cols), BF16),
            pltpu.VMEM((rows, width), BF16),
            pltpu.VMEM((rows, width), BF16),
            pltpu.VMEM((2, rows, width), BF16),
            pltpu.VMEM((rows, width), F32),
            pltpu.VMEM((rows, width), F32),
            pltpu.VMEM((rows, width), F32),
            pltpu.VMEM((rows, LANES), F32),
            pltpu.VMEM((2, 2, rows, 2 * hidden), BF16),
            pltpu.VMEM((2, rows, 2 * hidden), BF16),
            pltpu.VMEM((2, rows, width), BF16),
            pltpu.VMEM((2, chain, width), F32),
            pltpu.VMEM((2, chain, width), BF16),
            pltpu.VMEM((2, chain, width), BF16),
            pltpu.VMEM((2, chain // 2, width), BF16),
            pltpu.VMEM((4, 8, width), F32),
            dma((2, 11, 2)),
            dma((4,)),
            dma((2,)),
        ],
        compiler_params=pltpu.CompilerParams(
            collective_id=0, has_side_effects=True, vmem_limit_bytes=WIDE_LIMIT
        ),
        cost_estimate=pl.CostEstimate(
            flops=36 * rows * width * hidden, bytes_accessed=40 * rows * width, transcendentals=0
        ),
        name="middle",
    )(att, w_out, w_out_near, tokens, cotangent, norms, w_in, w_in_near, w_down, w_down_near)


class Sum:
    def __init__(self, size, me, first, total, give, take, result, sems):
        orders = dp_orders(size)
        self.total, self.give, self.take, self.result, self.sems = total, give, take, result, sems
        halving, stages = halvings(size), size.bit_length() - 1
        count = 1 << (halving - first)
        self.rows = total.shape[1] // count
        base, low, peers = [], [0, 0], []
        for chain in range(2):
            peers.append([peer_of(me, bit) for bit in orders[chain]])
            base.append(sum(peers[chain][done][1] * (1 << (halving - 1 - done)) for done in range(first)))
        self.steps, spot = [], 0
        for stage in range(first, stages):
            halve = stage < halving
            part = count // 2 if halve else count
            step = dict(kind="halve" if halve else "swap", part=part, spot=spot, chains=[], last=stage + 1 == stages)
            for chain in range(2):
                peer, mine = peers[chain][stage]
                away = low[chain] + (1 - mine) * part if halve else low[chain]
                low[chain] = low[chain] + mine * part if halve else low[chain]
                step["chains"].append(dict(peer=peer, away=away, keep=low[chain], final=base[chain] + low[chain]))
            self.steps.append(step)
            spot, count = spot + part, part
        low = [base[chain] + low[chain] for chain in range(2)]
        for stage in reversed(range(halving)):
            step = dict(kind="gather", part=count, chains=[])
            for chain in range(2):
                peer, mine = peers[chain][stage]
                step["chains"].append(dict(peer=peer, away=low[chain]))
                low[chain] = low[chain] - mine * count
            self.steps.append(step)
            count *= 2

    def block(self, low, count):
        return pl.ds(pl.multiple_of(low * self.rows, 16), count * self.rows)

    def copy(self, index, chain):
        step = self.steps[index]
        one = step["chains"][chain]
        if step["kind"] == "gather":
            source = target = self.result.at[chain, self.block(one["away"], step["part"])]
        else:
            spot = pl.ds(step["spot"] * self.rows, step["part"] * self.rows)
            source, target = self.give.at[chain, spot], self.take.at[chain, spot]
        return pltpu.make_async_remote_copy(
            source,
            target,
            self.sems.at[0, chain, index],
            self.sems.at[1, chain, index],
            device_id={"dp": one["peer"]},
            device_id_type=MESH,
        )

    def start(self, index):
        step = self.steps[index]
        for chain in range(2):
            if step["kind"] != "gather":
                spot = pl.ds(step["spot"] * self.rows, step["part"] * self.rows)
                away = self.block(step["chains"][chain]["away"], step["part"])
                self.give[chain, spot, :] = self.total[chain, away, :].astype(BF16)
            self.copy(index, chain).start()

    def finish(self, index):
        step = self.steps[index]
        for chain in range(2):
            self.copy(index, chain).wait()
            if step["kind"] == "gather":
                continue
            one = step["chains"][chain]
            spot = pl.ds(step["spot"] * self.rows, step["part"] * self.rows)
            keep = self.block(one["keep"], step["part"])
            mine = self.total[chain, keep, :] if step["kind"] == "halve" else self.give[chain, spot, :].astype(F32)
            value = mine + self.take[chain, spot, :].astype(F32)
            if step["last"]:
                self.result[chain, self.block(one["final"], 1), :] = value.astype(BF16)
            else:
                self.total[chain, keep, :] = value

    def advance(self, index):
        self.finish(index)
        if index + 1 < len(self.steps):
            self.start(index + 1)


def pieces_sent(size, first):
    halving = halvings(size)
    return (1 << (halving - first)) - 1 + size.bit_length() - 1 - halving


def back_kernel(
    size, att_ref, w_out_ref, cos_ref, sin_ref, norms_ref, w_ref, w_near_ref, dh_ref,
    kept_hbm, slots_hbm, q_rows_hbm, q_hbm, k_hbm, v_hbm, x_hbm,
    dx_ref, grad_ref, big_ref, sums_ref,
    big, slots, q_rows_ref, q_ref, k_ref, v_ref, x_ref,
    do_ref, do_rows_ref, dq_ref, dk_ref, dv_ref, d_qkv,
    total, give, take, big_give, big_take, near, far_out, far_in, own, norm_in,
    loads, near_sem, far_sem, sum_sems, big_sems, norm_sem,
):
    heads, _, tokens = k_ref.shape
    shards, rows, width = slots.shape
    cols = heads * HEAD_DIM
    half = HEAD_DIM // 2
    m, me = lax.axis_index("mp"), lax.axis_index("dp")
    stages = size.bit_length() - 1
    core, far = {"mp": peer_of(m, 0)[0]}, {"mp": peer_of(m, 1)[0]}
    partners = [core, far] + [{"dp": peer_of(me, bit)[0]} for bit in range(stages)]
    sources = [kept_hbm, slots_hbm, q_rows_hbm, q_hbm, k_hbm, v_hbm, x_hbm]
    targets = [big, slots, q_rows_ref, q_ref, k_ref, v_ref, x_ref]
    fetches = [
        pltpu.make_async_copy(source, target, loads.at[n])
        for n, (source, target) in enumerate(zip(sources, targets))
    ]
    for fetch in fetches:
        fetch.start()
    greet(partners)
    sums_ref[...] = norms_ref[...]
    large = Sum(size, me, 1, big, big_give, big_take, big_ref, big_sems)
    small = Sum(size, me, 0, total, give, take, grad_ref, sum_sems)
    fetches[0].wait()
    large.start(0)
    fetches[1].wait()

    def slot_at(shard):
        return (shard // 2 + m // 2) % 2 + 2 * ((shard + m) % 2)

    def shard_at(slot):
        return 2 * ((slot % 2 + m // 2) % 2) + (slot // 2 + m) % 2

    def prepare(i, carry):
        d_att = mm(w_out_ref[...], slots[slot_at(i)], NT).astype(BF16)
        do_ref[:, span(i, rows)] = d_att
        products = d_att.astype(F32) * att_ref[:, span(i, rows)].astype(F32)
        for h in range(heads):
            mine = slice(h * HEAD_DIM, (h + 1) * HEAD_DIM)
            dot = jnp.sum(products[mine], axis=0, keepdims=True)
            wide = [d_att[mine].astype(F32), thirds(-dot), jnp.zeros((LANES - HEAD_DIM - 16, rows), F32)]
            do_rows_ref[h, span(i, rows), :] = jnp.concatenate(wide, axis=0).T.astype(BF16)
        return carry

    lax.fori_loop(0, shards, prepare, 0)
    dq_ref[...] = jnp.zeros_like(dq_ref)
    for fetch in fetches[2:]:
        fetch.wait()

    def rotated_back(values, cosine, sine):
        first, second = values[:half], values[half:]
        return [first * cosine + second * sine, second * cosine - first * sine]

    def over_keys(j, carry):
        keys = span(j, rows)
        dk_ref[...] = jnp.zeros_like(dk_ref)
        dv_ref[...] = jnp.zeros_like(dv_ref)

        def over_queries(i, carry):
            queries = span(i, rows)
            for h in range(heads):
                k = k_ref[h, :, keys]
                probs = jnp.exp2(mm(q_rows_ref[h, queries, :], k))
                d_scores = (probs * mm(do_rows_ref[h, queries, :], v_ref[h, :, keys])).astype(BF16)
                dv_ref[h] += mm(do_ref[h * HEAD_DIM : (h + 1) * HEAD_DIM, queries], probs.astype(BF16))
                dk_ref[h] += mm(q_ref[h, :HEAD_DIM, queries], d_scores)
                dq_ref[h, :, queries] += mm(k[:HEAD_DIM], d_scores, NT)
            return carry

        lax.fori_loop(0, shards, over_queries, 0)
        cosine, sine = cos_ref[:, keys] * (1.0 / LOG2E), sin_ref[:, keys] * (1.0 / LOG2E)
        pieces = []
        for h in range(heads):
            pieces += rotated_back(dk_ref[h], cosine, sine)
        pieces += [dv_ref[h] for h in range(heads)]
        d_qkv[slot_at(j), cols:, :] = jnp.concatenate(pieces, axis=0).astype(BF16)
        for index, when in enumerate((0, 2)):
            pl.when(j == when)(lambda index=index: large.advance(index))
        return carry

    lax.fori_loop(0, shards, over_keys, 0)
    done = 2
    for i in range(shards):
        scale = 1.0 / math.sqrt(HEAD_DIM)
        cosine, sine = cos_ref[:, span(i, rows)] * scale, sin_ref[:, span(i, rows)] * scale
        pieces = []
        for h in range(heads):
            pieces += rotated_back(dq_ref[h, :, span(i, rows)], cosine, sine)
        d_qkv[slot_at(i), :cols, :] = jnp.concatenate(pieces, axis=0).astype(BF16)
    near_copy = send(d_qkv.at[pl.ds(2, 2)], near, near_sem.at[0], near_sem.at[1], core)

    def product(first, count):
        piece = mm(d_qkv[0, first : first + count, :], x_ref[0])
        for slot in range(1, shards):
            piece += mm(d_qkv[slot, first : first + count, :], x_ref[slot])
        return piece

    chain_rows = total.shape[1]
    total[0] = product(0, chain_rows)
    total[1, :cols, :] = product(chain_rows, cols)
    piece = mm(att_ref[:, span(shard_at(0), rows)], slots[0])
    for slot in range(1, shards):
        piece += mm(att_ref[:, span(shard_at(slot), rows)], slots[slot])
    total[1, cols:, :] = piece
    small.start(0)

    def norm_exchange(stage):
        return send(sums_ref, norm_in.at[stage], norm_sem.at[0, stage], norm_sem.at[1, stage], partners[stage])

    norm_copy, norm_done = norm_exchange(0), 0
    near_copy.wait()

    def d_tokens(index):
        return mm(d_qkv[index], w_ref[...], TN) + mm(near[index], w_near_ref[...], TN)

    far_out[...] = d_tokens(1).astype(BF16)
    far_copy = send(far_out, far_in, far_sem.at[0], far_sem.at[1], far)
    own[...] = dh_ref[...] + d_tokens(0)

    small_done = 0
    while done < len(large.steps) or small_done < len(small.steps) or norm_done < len(partners):
        if small_done < len(small.steps):
            small.advance(small_done)
            small_done += 1
        if done < len(large.steps):
            large.advance(done)
            done += 1
        if norm_done < len(partners):
            norm_copy.wait()
            sums_ref[...] += norm_in[norm_done]
            norm_done += 1
            if norm_done < len(partners):
                norm_copy = norm_exchange(norm_done)
    far_copy.wait()
    dx_ref[...] = (own[...] + far_in[...].astype(F32)).astype(BF16)


def back(att_along, w_out, cosine, sine, norms, w_turned, w_near, dh, kept, dh_slots, q_rows, q, k, v, x_slots):
    size = lax.axis_size("dp")
    stages = size.bit_length() - 1
    heads, _, tokens = q.shape
    shards, rows, width = x_slots.shape
    cols = w_turned.shape[0]
    chain, big_chain = width // 2, kept.shape[1] * 2
    sent = pieces_sent(size, 0) * (chain >> halvings(size))
    big_sent = pieces_sent(size, 1) * (big_chain >> halvings(size))
    steps = stages + halvings(size)
    vmem = pl.BlockSpec(memory_space=pltpu.VMEM)
    hbm = pl.BlockSpec(memory_space=pl.ANY)
    dma = pltpu.SemaphoreType.DMA
    along = pltpu.VMEM((heads, LANES, tokens), BF16)
    return pl.pallas_call(
        functools.partial(back_kernel, size),
        out_shape=(
            jax.ShapeDtypeStruct((rows, width), BF16),
            jax.ShapeDtypeStruct((2, chain, width), BF16),
            jax.ShapeDtypeStruct((2, big_chain, width), BF16),
            jax.ShapeDtypeStruct(norms.shape, F32),
        ),
        in_specs=[vmem] * 8 + [hbm] * 7,
        out_specs=[vmem] * 4,
        scratch_shapes=[
            pltpu.VMEM(kept.shape, F32),
            pltpu.VMEM(dh_slots.shape, BF16),
            pltpu.VMEM((heads, tokens, LANES), BF16),
            along,
            along,
            along,
            pltpu.VMEM(x_slots.shape, BF16),
            pltpu.VMEM((heads * HEAD_DIM, tokens), BF16),
            pltpu.VMEM((heads, tokens, LANES), BF16),
            pltpu.VMEM((heads, HEAD_DIM, tokens), F32),
            pltpu.VMEM((heads, HEAD_DIM, rows), F32),
            pltpu.VMEM((heads, HEAD_DIM, rows), F32),
            pltpu.VMEM((shards, cols, rows), BF16),
            pltpu.VMEM((2, chain, width), F32),
            pltpu.VMEM((2, sent, width), BF16),
            pltpu.VMEM((2, sent, width), BF16),
            pltpu.VMEM((2, big_sent, width), BF16),
            pltpu.VMEM((2, big_sent, width), BF16),
            pltpu.VMEM((2, cols, rows), BF16),
            pltpu.VMEM((rows, width), BF16),
            pltpu.VMEM((rows, width), BF16),
            pltpu.VMEM((rows, width), F32),
            pltpu.VMEM((2 + stages,) + norms.shape, F32),
            dma((7,)),
            dma((2,)),
            dma((2,)),
            dma((2, 2, steps)),
            dma((2, 2, steps)),
            dma((2, 2 + stages)),
        ],
        compiler_params=pltpu.CompilerParams(
            collective_id=1, has_side_effects=True, vmem_limit_bytes=WIDE_LIMIT
        ),
        cost_estimate=pl.CostEstimate(
            flops=5 * heads * tokens * tokens * LANES, bytes_accessed=60 * rows * width, transcendentals=0
        ),
        name="back",
    )(att_along, w_out, cosine, sine, norms, w_turned, w_near, dh, kept, dh_slots, q_rows, q, k, v, x_slots)


def emit_kernel(big_ref, small_ref, gate_up_ref, down_ref, qkv_ref, out_ref):
    for n in range(2):
        gate_up_ref[:, n, :] = big_ref[0, n].astype(F32)
    down_ref[...] = big_ref[0, 2].astype(F32)
    qkv_steps = pl.num_programs(0) * 3 // 4

    @pl.when(pl.program_id(0) < qkv_steps)
    def _():
        qkv_ref[...] = small_ref[0].astype(F32)

    @pl.when(pl.program_id(0) >= qkv_steps)
    def _():
        out_ref[...] = small_ref[0].astype(F32)


def emit(big, small):
    _, chain, width = small.shape
    steps = 8
    per, rows = steps // 2, width // steps
    qkv_steps = steps * 3 // 4
    shape = lambda *dims: jax.ShapeDtypeStruct(dims, F32)
    return pl.pallas_call(
        emit_kernel,
        out_shape=(
            shape(width, 2, width),
            shape(width, width),
            shape(qkv_steps * rows, width),
            shape((steps - qkv_steps) * rows, width),
        ),
        grid=(steps,),
        in_specs=[
            pl.BlockSpec((1, 3, rows, width), lambda i: (i // per, 0, i % per, 0)),
            pl.BlockSpec((1, rows, width), lambda i: (i // per, i % per, 0)),
        ],
        out_specs=[
            pl.BlockSpec((rows, 2, width), lambda i: (i, 0, 0)),
            pl.BlockSpec((rows, width), lambda i: (i, 0)),
            pl.BlockSpec((rows, width), lambda i: (jnp.minimum(i, qkv_steps - 1), 0)),
            pl.BlockSpec((rows, width), lambda i: (jnp.maximum(i - qkv_steps, 0), 0)),
        ],
        compiler_params=pltpu.CompilerParams(vmem_limit_bytes=VMEM_LIMIT),
        cost_estimate=pl.CostEstimate(flops=0, bytes_accessed=24 * width * width, transcendentals=0),
        name="emit",
    )(big.reshape(2, 3, chain, width), small)


def body(
    tokens, lengths, w_qkv, w_out, w_gate_up, w_down, ln1_scale, ln1_shift, ln2_scale, ln2_shift, cotangent
):
    rows, width = tokens.shape
    shards = lax.axis_size("mp")
    length = rows * shards
    local_cols = w_out.shape[0]
    heads = local_cols // HEAD_DIM
    hidden_cols = w_down.shape[0]
    m = lax.axis_index("mp")

    def swap(values, distance):
        return lax.ppermute(values, "mp", [(i, i ^ distance) for i in range(shards)])

    across = lambda values: swap(values, 2)
    beside = lambda values: swap(values, 1)

    x_far = across(tokens)
    x_near = beside(tokens)
    x_last = beside(x_far)
    positions, key_tiles, bounds = doc_tables(lengths[0], length, rows)
    cosine, sine = rotary(positions)
    place = jnp.stack([m.astype(jnp.int32)] + [jnp.int32(r) for r in (0, 2, 1, 3)])
    qkv_turned = w_qkv.transpose(1, 2, 0).reshape(3 * local_cols, width)
    qkv_near = beside(qkv_turned)
    w_out_near = beside(w_out)
    flat_gate_up = w_gate_up.reshape(width, 2 * hidden_cols)
    w_gate_up_near = beside(flat_gate_up)
    w_down_near = beside(w_down)
    x_slots = jnp.stack([tokens, x_far, x_near, x_last])
    q, k, v, k_rows = project(x_slots, qkv_turned, cosine, sine, bounds, place, heads)
    att, att_along, q_rows = attend(q, k_rows, v, place, key_tiles, shards)
    norms = jnp.concatenate([jnp.stack([ln1_scale, ln1_shift, ln2_scale, ln2_shift]), jnp.zeros((4, width), F32)])
    output, dh, dh_slots, norms, kept = middle(
        att, w_out, w_out_near, tokens, cotangent, norms, flat_gate_up, w_gate_up_near, w_down, w_down_near
    )
    d_tokens, small, big, norms = back(
        att_along, w_out, cosine, sine, norms, qkv_turned, qkv_near, dh, kept, dh_slots, q_rows, q, k, v, x_slots
    )
    grad_gate_up, grad_down, grad_qkv, grad_out = emit(big, small)
    grad_qkv = grad_qkv.reshape(3, local_cols, width).transpose(2, 0, 1)
    norms = lax.dynamic_slice_in_dim(norms, m * local_cols, local_cols, 1)
    return (
        output,
        d_tokens,
        grad_qkv,
        grad_out,
        grad_gate_up,
        grad_down,
        norms[0],
        norms[1],
        norms[2],
        norms[3],
    )


def solution(mesh):
    return jax.shard_map(
        body,
        mesh=mesh,
        in_specs=(
            P(("dp", "mp"), None),
            P("dp", None),
            P(None, None, "mp"),
            P("mp", None),
            P(None, None, "mp"),
            P("mp", None),
            P(),
            P(),
            P(),
            P(),
            P(("dp", "mp"), None),
        ),
        out_specs=(
            P(("dp", "mp"), None),
            P(("dp", "mp"), None),
            P(None, None, "mp"),
            P("mp", None),
            P(None, None, "mp"),
            P("mp", None),
            P("mp"),
            P("mp"),
            P("mp"),
            P("mp"),
        ),
        check_vma=False,
    )
```

```python
import functools
import math

import jax
import jax.numpy as jnp
from jax import lax
from jax.experimental import pallas as pl
from jax.experimental.pallas import tpu as pltpu
from jax.sharding import PartitionSpec as P

F32 = jnp.float32
BF16 = jnp.bfloat16
HEAD_DIM = 64
LANES = 128
EPSILON = 1e-05
FAR = -(2.0**100)
LOG2E = math.log2(math.e)
NT = (((1,), (1,)), ((), ()))
TN = (((0,), (0,)), ((), ()))
NN = (((1,), (0,)), ((), ()))
VMEM_LIMIT = 58 << 20
WIDE_LIMIT = 62 << 20
MESH = pl.DeviceIdType.MESH


def mm(a, b, dims=NN):
    return lax.dot_general(a, b, dims, preferred_element_type=F32)


def thirds(row):
    high = row.astype(BF16).astype(F32)
    mid = (row - high).astype(BF16).astype(F32)
    low = row - high - mid
    return jnp.concatenate([high, mid, low, jnp.zeros((13, row.shape[1]), F32)], axis=0)


def span(index, size):
    if isinstance(index, int):
        return pl.ds(index * size, size)
    return pl.ds(pl.multiple_of(index * size, size), size)


def dp_orders(size):
    bits = list(range(size.bit_length() - 1))
    return [bits, bits[1::-1] + bits[2:]]


def halvings(size):
    return min(3, size.bit_length() - 1)


def peer_of(index, bit):
    mine = (index // (1 << bit)) % 2
    return index + (1 - 2 * mine) * (1 << bit), mine


def send(source, target, send_sem, recv_sem, partner):
    copy = pltpu.make_async_remote_copy(
        source, target, send_sem, recv_sem, device_id=partner, device_id_type=MESH
    )
    copy.start()
    return copy


def greet(partners):
    barrier = pltpu.get_barrier_semaphore()
    for partner in partners:
        pl.semaphore_signal(barrier, inc=1, device_id=partner, device_id_type=MESH)
    pl.semaphore_wait(barrier, len(partners))


RING_PIECES = 8
RING_EARLY = 2


class Ring:
    def __init__(self, size, me, total, give, take, result, scatter_sems, gather_sems):
        self.n = n = min(RING_PIECES, size)
        self.me, self.size = me, size
        self.total, self.give, self.take, self.result = total, give, take, result
        self.scatter_sems, self.gather_sems = scatter_sems, gather_sems
        self.rows, self.cols = total.shape[1] // n, total.shape[2] // 2
        low = me % n
        across, along = low % 2, low // 2
        self.spot = (1 - across) * along + across * (n - 1 - along)
        self.peers = [self.index_at((self.spot + step) % n) for step in (1, n - 1)]

    def index_at(self, spot):
        across = spot // (self.n // 2)
        along = (1 - across) * spot + across * (self.n - 1 - spot)
        return self.me - self.me % self.n + 2 * along + across

    def piece(self, chain, step):
        shift = self.n * 4 - step if chain == 0 else step
        return pl.ds(pl.multiple_of((self.spot + shift) % self.n * self.rows, 16), self.rows)

    def half(self, sub):
        return span(sub, self.cols)

    def scatter(self, chain, sub, step):
        return pltpu.make_async_remote_copy(
            self.give.at[chain, sub],
            self.take.at[chain, sub, step],
            self.scatter_sems.at[0, chain, sub, step],
            self.scatter_sems.at[1, chain, sub, step],
            device_id={"dp": self.peers[chain]},
            device_id_type=MESH,
        )

    def gather(self, chain, sub, step):
        part = self.result.at[chain, self.piece(chain, step + self.n - 1), self.half(sub)]
        return pltpu.make_async_remote_copy(
            part,
            part,
            self.gather_sems.at[0, chain, sub, step],
            self.gather_sems.at[1, chain, sub, step],
            device_id={"dp": self.peers[chain]},
            device_id_type=MESH,
        )

    def begin(self, step, chain):
        for sub in range(2):
            self.give[chain, sub] = self.total[chain, self.piece(chain, step), self.half(sub)].astype(BF16)
            self.scatter(chain, sub, step).start()

    def arrived(self, step, chain, sub):
        self.scatter(chain, sub, step).wait()
        mine = self.total[chain, self.piece(chain, step + 1), self.half(sub)]
        return mine + self.take[chain, sub, step].astype(F32)

    def keep(self, step):
        for chain in range(2):
            for sub in range(2):
                value = self.arrived(step, chain, sub)
                self.total[chain, self.piece(chain, step + 1), self.half(sub)] = value

    def pass_on(self, step, sub):
        for chain in range(2):
            self.give[chain, sub] = self.arrived(step, chain, sub).astype(BF16)
            self.scatter(chain, sub, step + 1).start()

    def turn(self, step, sub):
        for chain in range(2):
            value = self.arrived(step, chain, sub).astype(BF16)
            self.give[chain, sub] = value
        for stage in range((self.size // self.n).bit_length() - 1):
            copies = []
            for chain in range(2):
                peer = self.me // self.n
                mine = (peer // (1 << stage)) % 2
                copies.append(
                    pltpu.make_async_remote_copy(
                        self.give.at[chain, sub],
                        self.take.at[chain, sub, self.n - 1 + stage],
                        self.scatter_sems.at[0, chain, sub, self.n - 1 + stage],
                        self.scatter_sems.at[1, chain, sub, self.n - 1 + stage],
                        device_id={"dp": self.me + (1 - 2 * mine) * (self.n << stage)},
                        device_id_type=MESH,
                    )
                )
                copies[-1].start()
            for chain in range(2):
                copies[chain].wait()
                value = self.give[chain, sub].astype(F32) + self.take[chain, sub, self.n - 1 + stage].astype(F32)
                self.give[chain, sub] = value.astype(BF16)
        for chain in range(2):
            self.result[chain, self.piece(chain, self.n - 1), self.half(sub)] = self.give[chain, sub]
            self.gather(chain, sub, 0).start()

    def event(self, number):
        step, sub, n = number // 2, number % 2, self.n

        @pl.when(step < n - 2)
        def _():
            self.pass_on(step, sub)

        @pl.when(step == n - 2)
        def _():
            self.turn(n - 2, sub)

        @pl.when(step >= n - 1)
        def _():
            for chain in range(2):
                self.gather(chain, sub, step - (n - 1)).wait()

            @pl.when(step < 2 * n - 3)
            def _():
                for chain in range(2):
                    self.gather(chain, sub, step - (n - 2)).start()


def ring_scratch(size, rows, cols, steps):
    piece = (rows // min(RING_PIECES, size), cols // 2)
    return [
        pltpu.VMEM((2, 2) + piece, BF16),
        pltpu.VMEM((2, 2, steps) + piece, BF16),
        pltpu.SemaphoreType.DMA((2, 2, 2, steps)),
    ]


X_FAR, X_NEAR, X_LAST, W_IN, W_DOWN, W_OUT, ATT = range(7)
BRANCH, NORMED, OUT, DOUT, DNORMED, DH, DH_NEAR, DH_LAST, GRAD_NEAR = range(7, 16)
KINDS = 16


def first_kernel(
    size, lengths, tok_ref, cot_ref, ln_ref, w_ref, wo_ref, win_hbm, wdn_hbm,
    out_ref, dh_ref, slots_ref, norms_ref, total_hbm, x_hbm, q_hbm, k_hbm, v_hbm, q_rows_hbm, att_hbm, cos_hbm, sin_hbm,
    x_ref, win, wdn, wo_near_ref, att, near, outbox, inbox, low, hat, res, own, r1, dlow, give, take, sums,
    ring_give, ring_take, ring_sems, sems, loads, stores,
):
    rows, width = tok_ref.shape
    hidden = wdn.shape[0] // 2
    cols = wo_ref.shape[0]
    heads = cols // HEAD_DIM
    shards = x_ref.shape[0]
    tokens = shards * rows
    half = width // 2
    chunk = rows // 2
    chunks = [slice(c * chunk, (c + 1) * chunk) for c in range(2)]
    m, me = lax.axis_index("mp"), lax.axis_index("dp")
    core, far = {"mp": peer_of(m, 0)[0]}, {"mp": peer_of(m, 1)[0]}
    ring_peers = Ring(size, me, give, None, None, None, None, None).peers
    greet([core, far] + [{"dp": peer} for peer in ring_peers])

    def post(kind, c, source, target, partner):
        return send(source, target, sems.at[0, kind, c], sems.at[1, kind, c], partner)

    far_copies = [post(X_FAR, c, tok_ref.at[where], x_ref.at[1, where], far) for c, where in enumerate(chunks)]
    near_copy = post(X_NEAR, 0, tok_ref, x_ref.at[2], core)
    weight_copies = [
        post(W_OUT, 0, wo_ref, wo_near_ref, core),
        post(W_IN, 0, win_hbm, win.at[1], core),
        post(W_DOWN, 0, wdn_hbm, wdn.at[pl.ds(hidden, hidden)], core),
    ]
    fetches = []
    for n, (source, target) in enumerate([(win_hbm, win.at[0]), (wdn_hbm, wdn.at[pl.ds(0, hidden)])]):
        fetches.append(pltpu.make_async_copy(source, target, loads.at[n]))
        fetches[-1].start()
    x_ref[0] = tok_ref[...]
    sums[...] = jnp.zeros_like(sums)
    scale_one, shift_one, scale_two, shift_two = (ln_ref[i : i + 1, :] for i in range(4))

    def exchange(kind, value_of):
        copies = []
        for c, where in enumerate(chunks):
            outbox[where, :] = value_of(where).astype(BF16)
            copies.append(post(kind, c, outbox.at[where], inbox.at[where], far))
        return copies

    def branch(index, where):
        return mm(att[index, :, where], wo_ref[...], TN) + mm(near[index, :, where], wo_near_ref[...], TN)

    def attention(q_ref, k_ref, v_ref, k_rows_ref, q_rows_ref, cos_ref, sin_ref, top_ref, acc_ref):
        half_head = HEAD_DIM // 2
        starts, ends, end = [], [], 0
        for d in range(lengths.shape[1]):
            starts.append(end)
            end = end + lengths[0, d]
            ends.append(end)
        doc = lax.broadcasted_iota(jnp.int32, (16, rows), 0)
        first, last = jnp.zeros((16, rows), jnp.int32), jnp.zeros((16, rows), jnp.int32)
        for d in range(lengths.shape[1]):
            first, last = jnp.where(doc == d, starts[d], first), jnp.where(doc == d, ends[d], last)
        exponent = lax.broadcasted_iota(jnp.int32, (half_head, rows), 0).astype(F32)
        rate = jnp.exp(exponent * (-2.0 * math.log(1000.0) / HEAD_DIM))
        row = lax.broadcasted_iota(jnp.int32, (48, rows), 0)
        ones = jnp.where(row < 3, 1.0, 0.0)
        v_tail = jnp.concatenate([ones, jnp.zeros((16, rows), F32)], axis=0)
        top_ref[...] = jnp.full_like(top_ref, FAR)
        acc_ref[...] = jnp.zeros_like(acc_ref)

        def tables(slot):
            where = slice(slot * rows, (slot + 1) * rows)
            shard = 2 * ((slot % 2 + m // 2) % 2) + (slot // 2 + m) % 2
            token = lax.broadcasted_iota(jnp.int32, (16, rows), 1) + shard * rows
            inside = (token >= first) & (token < last)
            begin = jnp.max(jnp.where(inside, first, 0), axis=0, keepdims=True)
            angles = rate * (token[0:1] - begin).astype(F32)
            cos_ref[:, where], sin_ref[:, where] = jnp.cos(angles), jnp.sin(angles)
            for h in range(heads):
                q_ref[h, HEAD_DIM:, where] = jnp.concatenate(
                    [jnp.where(inside, 0.0, FAR), jnp.zeros((48, rows), F32)], axis=0
                ).astype(BF16)
                k_ref[h, HEAD_DIM:, where] = jnp.concatenate([jnp.where(inside, 1.0, 0.0), ones], axis=0).astype(BF16)
                v_ref[h, HEAD_DIM:, where] = v_tail.astype(BF16)

        def project(slot):
            where = slice(slot * rows, (slot + 1) * rows)
            projected = mm(w_ref[...], x_ref[slot], NT)
            cosine, sine = cos_ref[:, where], sin_ref[:, where]

            def rotated(start, scale):
                one, two = projected[start : start + half_head], projected[start + half_head : start + HEAD_DIM]
                turned = jnp.concatenate([one * cosine - two * sine, two * cosine + one * sine], axis=0)
                return turned * scale

            for h in range(heads):
                q_ref[h, :HEAD_DIM, where] = rotated(h * HEAD_DIM, LOG2E / math.sqrt(HEAD_DIM)).astype(BF16)
                k = rotated(cols + h * HEAD_DIM, 1.0)
                k_ref[h, :HEAD_DIM, where] = k.astype(BF16)
                tail = k_ref[h, HEAD_DIM:, where].astype(F32)
                k_rows_ref[h, where, :] = jnp.concatenate([k, tail], axis=0).T.astype(BF16)
                start = 2 * cols + h * HEAD_DIM
                v_ref[h, :HEAD_DIM, where] = projected[start : start + HEAD_DIM].astype(BF16)

        def pairs(count, pair):
            def run(n, carry):
                qs, ks = pair(n)
                queries, keys = span(qs, rows), span(ks, rows)
                for h in range(heads):
                    s = mm(k_rows_ref[h, keys, :], q_ref[h, :, queries])
                    old = top_ref[qs, h, 0:1, :]
                    top = jnp.maximum(old, jnp.max(s, axis=0, keepdims=True))
                    probs = jnp.exp2(s - top).astype(BF16)
                    top_ref[qs, h, 0:1, :] = top
                    acc_ref[qs, h] = acc_ref[qs, h] * jnp.exp2(old - top) + mm(v_ref[h, :80, keys], probs)
                return carry

            lax.fori_loop(0, count, run, 0)

        writes = []

        def write(source, target):
            writes.append(pltpu.make_async_copy(source, target, stores.at[len(writes)]))
            writes[-1].start()

        def settle(slot):
            where = slice(slot * rows, (slot + 1) * rows)
            for h in range(heads):
                total = acc_ref[slot, h, HEAD_DIM : HEAD_DIM + 1, :]
                out = acc_ref[slot, h, :HEAD_DIM, :] / total
                att[slot, h * HEAD_DIM : (h + 1) * HEAD_DIM, :] = out.astype(BF16)
                level = top_ref[slot, h, 0:1, :] + jnp.log2(total)
                query = q_ref[h, :, where].astype(F32)
                wide = jnp.concatenate([query[:80], thirds(-level), query[96:]], axis=0)
                q_rows_ref[h, where, :] = wide.T.astype(BF16)

        for slot in range(4):
            tables(slot)
        project(0)
        near_copy.wait()
        project(2)
        pairs(4, lambda n: (2 * (n // 2), 2 * (n % 2)))
        last_copies = []
        for c, where in enumerate(chunks):
            far_copies[c].wait()
            last_copies.append(post(X_LAST, c, x_ref.at[1, where], x_ref.at[3, where], core))
        project(1)
        for copy in last_copies:
            copy.wait()
        project(3)
        for source, target in [
            (x_ref, x_hbm), (q_ref, q_hbm), (k_ref, k_hbm), (v_ref, v_hbm), (cos_ref, cos_hbm), (sin_ref, sin_hbm)
        ]:
            write(source, target)
        pairs(4, lambda n: (3, n))
        settle(3)
        copies = [post(ATT, 1, att.at[3], near.at[1], core)]
        pairs(4, lambda n: (1, n))
        settle(1)
        weight_copies[0].wait()
        copies[0].wait()
        exchange(BRANCH, lambda where: branch(1, where))
        pairs(4, lambda n: (2 * (1 - n // 2), 2 * (n % 2) + 1))
        settle(2)
        copies.append(post(ATT, 0, att.at[2], near.at[0], core))
        settle(0)
        write(q_rows_ref, q_rows_hbm)
        write(att, att_hbm)
        copies[1].wait()
        for where in chunks:
            hat[where, :] = tok_ref[where, :].astype(F32) + branch(0, where)
        for copy in writes:
            copy.wait()

    along = pltpu.VMEM((heads, LANES, tokens), BF16)
    down = pltpu.VMEM((heads, tokens, LANES), BF16)
    table = pltpu.VMEM((HEAD_DIM // 2, tokens), F32)
    pl.run_scoped(
        attention, along, along, along, down, down, table, table,
        pltpu.VMEM((shards, heads, 8, rows), F32), pltpu.VMEM((shards, heads, 80, rows), F32),
    )
    branch_copies = [
        pltpu.make_async_remote_copy(
            outbox.at[where],
            inbox.at[where],
            sems.at[0, BRANCH, c],
            sems.at[1, BRANCH, c],
            device_id=far,
            device_id_type=MESH,
        )
        for c, where in enumerate(chunks)
    ]

    def by_parts(c, part):
        step = 64

        def run(i, carry):
            part(pl.ds(pl.multiple_of(c * chunk + i * step, step), step))
            return carry

        lax.fori_loop(0, chunk // step, run, 0)

    def mean(values):
        return jnp.sum(values, axis=-1, keepdims=True) * (1.0 / width)

    def add_up(index, values):
        sums[index] += jnp.sum(values.reshape(values.shape[0] // 8, 8, width), axis=0)

    def norm_one(where):
        h = hat[where, :] + inbox[where, :].astype(F32)
        h = h - mean(h)
        r = lax.rsqrt(mean(h * h) + EPSILON)
        h = h * r
        hat[where, :] = h
        r1[where, :] = jnp.broadcast_to(r, (r.shape[0], LANES))
        h = h * scale_one + shift_one
        res[where, :] = h
        low[0, where, :] = h.astype(BF16)

    normed_copies = []
    for c, where in enumerate(chunks):
        branch_copies[c].wait()
        by_parts(c, norm_one)
        normed_copies.append(post(NORMED, c, low.at[0, where], low.at[1, where], far))
    for copy in fetches + weight_copies[1:]:
        copy.wait()

    def feed_forward(gu, hid, total):
        ring = Ring(size, me, total, ring_give, ring_take, None, ring_sems, None)
        tile = hidden // 2

        def mlp(side, where):
            def columns(t, carry):
                k, at = t // 2, (t % 2) * tile
                x = low[side, where, :]
                gate_at = pl.ds(pl.multiple_of(at, LANES), tile)
                up_at = pl.ds(pl.multiple_of(hidden + at, LANES), tile)
                gate, up = mm(x, win[k, :, gate_at]), mm(x, win[k, :, up_at])
                gu[side, k, where, gate_at] = gate.astype(BF16)
                gu[side, k, where, up_at] = up.astype(BF16)
                value = gate * jax.nn.sigmoid(gate) * up
                hid[side, where, pl.ds(pl.multiple_of(k * hidden + at, LANES), tile)] = value.astype(BF16)
                return carry

            lax.fori_loop(0, 4, columns, 0)
            return mm(hid[side, where, :], wdn[...])

        def both_sides(copies_in, kind, compute):
            copies = []
            for c, where in enumerate(chunks):
                own[where, :] = compute(0, where)
                copies_in[c].wait()
                outbox[where, :] = compute(1, where).astype(BF16)
                copies.append(post(kind, c, outbox.at[where], inbox.at[where], far))
            return copies

        out_copies = both_sides(normed_copies, OUT, mlp)

        def norm_two(where):
            z = res[where, :] + own[where, :] + inbox[where, :].astype(F32)
            z = z - mean(z)
            r = lax.rsqrt(mean(z * z) + EPSILON)
            z = z * r
            out_ref[where, :] = (z * scale_two + shift_two).astype(BF16)
            g = cot_ref[where, :].astype(F32)
            add_up(2, g * z)
            add_up(3, g)
            e = g * scale_two
            dz = r * (e - mean(e) - z * mean(e * z))
            res[where, :] = dz
            dlow[0, where, :] = dz.astype(BF16)

        dout_copies = []
        for c, where in enumerate(chunks):
            out_copies[c].wait()
            by_parts(c, norm_two)
            dout_copies.append(post(DOUT, c, dlow.at[0, where], dlow.at[1, where], far))

        def mlp_back(side, where):
            def columns(t, carry):
                k, at = t // 2, (t % 2) * tile
                d_hidden = mm(
                    dlow[side, where, :], wdn[pl.ds(pl.multiple_of(k * hidden + at, LANES), tile), :], NT
                )
                gate_at = pl.ds(pl.multiple_of(at, LANES), tile)
                up_at = pl.ds(pl.multiple_of(hidden + at, LANES), tile)
                gate, up = gu[side, k, where, gate_at].astype(F32), gu[side, k, where, up_at].astype(F32)
                s = jax.nn.sigmoid(gate)
                gu[side, k, where, gate_at] = (d_hidden * up * s * (1.0 + gate * (1.0 - s))).astype(BF16)
                gu[side, k, where, up_at] = (d_hidden * gate * s).astype(BF16)
                return carry

            lax.fori_loop(0, 4, columns, 0)
            return mm(gu[side, 0, where, :], win[0], NT) + mm(gu[side, 1, where, :], win[1], NT)

        dnormed_copies = both_sides(dout_copies, DNORMED, mlp_back)

        def weight_grads(k, target, then=lambda r: None):
            def chain(r, carry):
                at = pl.ds(pl.multiple_of(r * half, LANES), half)
                for n, place in enumerate((slice(0, hidden), slice(hidden, 2 * hidden))):
                    piece = mm(low[0, :, at], gu[0, k, :, place], TN) + mm(low[1, :, at], gu[1, k, :, place], TN)
                    target[r, n * half : (n + 1) * half, :] = piece.astype(target.dtype)
                at = pl.ds(pl.multiple_of(k * hidden + r * half, LANES), half)
                piece = mm(hid[0, :, at], dlow[0], TN) + mm(hid[1, :, at], dlow[1], TN)
                target[r, 2 * half : 3 * half, :] = piece.astype(target.dtype)
                then(r)
                return carry

            lax.fori_loop(0, 2, chain, 0)

        def grad_copy(r):
            return pltpu.make_async_remote_copy(
                give.at[r],
                take.at[r],
                sems.at[0, GRAD_NEAR, r],
                sems.at[1, GRAD_NEAR, r],
                device_id=core,
                device_id_type=MESH,
            )

        weight_grads(1, give, lambda r: grad_copy(r).start())

        def norm_one_back(where):
            d = res[where, :] + own[where, :] + inbox[where, :].astype(F32)
            h = hat[where, :]
            add_up(0, d * h)
            add_up(1, d)
            e = d * scale_one
            dh = r1[where, 0:1] * (e - mean(e) - h * mean(e * h))
            dh_ref[where, :] = dh
            slots_ref[0, where, :] = dh.astype(BF16)

        dh_copies, last_copies = [], []

        def dh_chunk(c):
            where = chunks[c]
            dnormed_copies[c].wait()
            by_parts(c, norm_one_back)
            mine = slots_ref.at[0, where]
            dh_copies.append(post(DH, c, mine, slots_ref.at[1, where], far))
            last_copies.append(post(DH_NEAR, c, mine, slots_ref.at[2, where], core))

        dh_chunk(0)
        weight_grads(0, total)
        dh_chunk(1)
        for r in range(2):
            grad_copy(r).wait()
            total[r] += take[r].astype(F32)
            ring.begin(0, r)

        def hand_on(c):
            dh_copies[c].wait()
            where = chunks[c]
            last_copies.append(post(DH_LAST, c, slots_ref.at[1, where], slots_ref.at[3, where], core))

        for i in range(4):
            norms_ref[i : i + 1, :] = jnp.sum(sums[i], axis=0, keepdims=True)
        norms_ref[4:8, :] = jnp.zeros((4, width), F32)
        hand_on(0)
        for step in range(RING_EARLY - 1):
            for sub in range(2):
                ring.pass_on(step, sub)
        hand_on(1)
        ring.keep(RING_EARLY - 1)
        write = pltpu.make_async_copy(total, total_hbm, loads.at[0])
        write.start()
        for copy in last_copies:
            copy.wait()
        write.wait()

    pl.run_scoped(
        feed_forward,
        pltpu.VMEM((2, 2, rows, 2 * hidden), BF16),
        pltpu.VMEM((2, rows, 2 * hidden), BF16),
        pltpu.VMEM((2, 3 * half, width), F32),
    )


def first(lengths, tokens, cotangent, norms, w_turned, w_out, w_in, w_down):
    size, shards = lax.axis_size("dp"), lax.axis_size("mp")
    rows, width = tokens.shape
    cols, hidden = w_out.shape[0], w_down.shape[0]
    heads, length = cols // HEAD_DIM, rows * shards
    chain = 3 * width // 2
    vmem = pl.BlockSpec(memory_space=pltpu.VMEM)
    hbm = pl.BlockSpec(memory_space=pl.ANY)
    dma = pltpu.SemaphoreType.DMA
    shape = jax.ShapeDtypeStruct
    along, table = shape((heads, LANES, length), BF16), shape((HEAD_DIM // 2, length), F32)
    wide = lambda dtype, *lead: pltpu.VMEM(lead + (rows, width), dtype)
    return pl.pallas_call(
        functools.partial(first_kernel, size),
        out_shape=(
            shape((rows, width), BF16),
            shape((rows, width), F32),
            shape((shards, rows, width), BF16),
            shape((8, width), F32),
            shape((2, chain, width), F32),
            shape((shards, rows, width), BF16),
            along,
            along,
            along,
            shape((heads, length, LANES), BF16),
            shape((shards, cols, rows), BF16),
            table,
            table,
        ),
        in_specs=[pl.BlockSpec(memory_space=pltpu.SMEM)] + [vmem] * 5 + [hbm] * 2,
        out_specs=[vmem] * 4 + [hbm] * 9,
        scratch_shapes=[
            wide(BF16, shards),
            pltpu.VMEM((2, width, 2 * hidden), BF16),
            pltpu.VMEM((2 * hidden, width), BF16),
            pltpu.VMEM((cols, width), BF16),
            pltpu.VMEM((shards, cols, rows), BF16),
            pltpu.VMEM((2, cols, rows), BF16),
            wide(BF16),
            wide(BF16),
            wide(BF16, 2),
            wide(F32),
            wide(F32),
            wide(F32),
            pltpu.VMEM((rows, LANES), F32),
            wide(BF16, 2),
            pltpu.VMEM((2, chain, width), BF16),
            pltpu.VMEM((2, chain, width), BF16),
            pltpu.VMEM((4, 8, width), F32),
            *ring_scratch(size, chain, width, RING_EARLY),
            dma((2, KINDS, 2)),
            dma((2,)),
            dma((8,)),
        ],
        compiler_params=pltpu.CompilerParams(
            collective_id=0, has_side_effects=True, vmem_limit_bytes=WIDE_LIMIT
        ),
        cost_estimate=pl.CostEstimate(
            flops=36 * rows * width * hidden, bytes_accessed=40 * rows * width, transcendentals=0
        ),
        name="first",
    )(lengths, tokens, cotangent, norms, w_turned, w_out, w_in, w_down)


class Sum:
    def __init__(self, size, me, first, total, give, take, result, sems):
        orders = dp_orders(size)
        self.total, self.give, self.take, self.result, self.sems = total, give, take, result, sems
        halving, stages = halvings(size), size.bit_length() - 1
        count = 1 << (halving - first)
        self.rows = total.shape[1] // count
        base, low, peers = [], [0, 0], []
        for chain in range(2):
            peers.append([peer_of(me, bit) for bit in orders[chain]])
            base.append(sum(peers[chain][done][1] * (1 << (halving - 1 - done)) for done in range(first)))
        self.steps, spot = [], 0
        for stage in range(first, stages):
            halve = stage < halving
            part = count // 2 if halve else count
            step = dict(kind="halve" if halve else "swap", part=part, spot=spot, chains=[], last=stage + 1 == stages)
            for chain in range(2):
                peer, mine = peers[chain][stage]
                away = low[chain] + (1 - mine) * part if halve else low[chain]
                low[chain] = low[chain] + mine * part if halve else low[chain]
                step["chains"].append(dict(peer=peer, away=away, keep=low[chain], final=base[chain] + low[chain]))
            self.steps.append(step)
            spot, count = spot + part, part
        low = [base[chain] + low[chain] for chain in range(2)]
        for stage in reversed(range(halving)):
            step = dict(kind="gather", part=count, chains=[])
            for chain in range(2):
                peer, mine = peers[chain][stage]
                step["chains"].append(dict(peer=peer, away=low[chain]))
                low[chain] = low[chain] - mine * count
            self.steps.append(step)
            count *= 2

    def block(self, low, count):
        return pl.ds(pl.multiple_of(low * self.rows, 16), count * self.rows)

    def copy(self, index, chain):
        step = self.steps[index]
        one = step["chains"][chain]
        if step["kind"] == "gather":
            source = target = self.result.at[chain, self.block(one["away"], step["part"])]
        else:
            spot = pl.ds(step["spot"] * self.rows, step["part"] * self.rows)
            source, target = self.give.at[chain, spot], self.take.at[chain, spot]
        return pltpu.make_async_remote_copy(
            source,
            target,
            self.sems.at[0, chain, index],
            self.sems.at[1, chain, index],
            device_id={"dp": one["peer"]},
            device_id_type=MESH,
        )

    def start(self, index):
        step = self.steps[index]
        for chain in range(2):
            if step["kind"] != "gather":
                spot = pl.ds(step["spot"] * self.rows, step["part"] * self.rows)
                away = self.block(step["chains"][chain]["away"], step["part"])
                self.give[chain, spot, :] = self.total[chain, away, :].astype(BF16)
            self.copy(index, chain).start()

    def finish(self, index):
        step = self.steps[index]
        for chain in range(2):
            self.copy(index, chain).wait()
            if step["kind"] == "gather":
                continue
            one = step["chains"][chain]
            spot = pl.ds(step["spot"] * self.rows, step["part"] * self.rows)
            keep = self.block(one["keep"], step["part"])
            mine = self.total[chain, keep, :] if step["kind"] == "halve" else self.give[chain, spot, :].astype(F32)
            value = mine + self.take[chain, spot, :].astype(F32)
            if step["last"]:
                self.result[chain, self.block(one["final"], 1), :] = value.astype(BF16)
            else:
                self.total[chain, keep, :] = value

    def advance(self, index):
        self.finish(index)
        if index + 1 < len(self.steps):
            self.start(index + 1)


def pieces_sent(size, first):
    halving = halvings(size)
    return (1 << (halving - first)) - 1 + size.bit_length() - 1 - halving


def back_kernel(
    size, att_ref, w_out_ref, cos_ref, sin_ref, norms_ref, w_ref, w_near_ref, dh_ref,
    total_hbm, slots_hbm, q_rows_hbm, q_hbm, k_hbm, v_hbm, x_hbm,
    dx_ref, grad_ref, big_ref, sums_ref,
    big, slots, q_rows_ref, q_ref, k_ref, v_ref, x_ref,
    do_ref, do_rows_ref, dq_ref, dk_ref, dv_ref, d_qkv,
    total, give, take, near, far_out, far_in, own, norm_in,
    ring_give, ring_take, ring_sems, gather_sems, loads, near_sem, far_sem, sum_sems, norm_sem,
):
    heads, _, tokens = k_ref.shape
    shards, rows, width = slots.shape
    cols = heads * HEAD_DIM
    half = HEAD_DIM // 2
    m, me = lax.axis_index("mp"), lax.axis_index("dp")
    stages = size.bit_length() - 1
    core, far = {"mp": peer_of(m, 0)[0]}, {"mp": peer_of(m, 1)[0]}
    partners = [core, far] + [{"dp": peer_of(me, bit)[0]} for bit in range(stages)]
    sources = [total_hbm, slots_hbm, q_rows_hbm, q_hbm, k_hbm, v_hbm, x_hbm]
    targets = [big, slots, q_rows_ref, q_ref, k_ref, v_ref, x_ref]
    fetches = [
        pltpu.make_async_copy(source, target, loads.at[n])
        for n, (source, target) in enumerate(zip(sources, targets))
    ]
    for fetch in fetches:
        fetch.start()
    ring = Ring(size, me, big, ring_give, ring_take, big_ref, ring_sems, gather_sems)
    greet(partners + [{"dp": peer} for peer in ring.peers])
    sums_ref[...] = norms_ref[...]
    small = Sum(size, me, 0, total, give, take, grad_ref, sum_sems)
    fetches[0].wait()
    for chain in range(2):
        ring.begin(RING_EARLY, chain)
    fetches[1].wait()
    events = 2 * (2 * ring.n - 2)
    first_event = 2 * RING_EARLY

    def prepare(i, carry):
        d_att = mm(w_out_ref[...], slots[i], NT).astype(BF16)
        do_ref[:, span(i, rows)] = d_att
        products = d_att.astype(F32) * att_ref[i].astype(F32)
        for h in range(heads):
            mine = slice(h * HEAD_DIM, (h + 1) * HEAD_DIM)
            dot = jnp.sum(products[mine], axis=0, keepdims=True)
            wide = [d_att[mine].astype(F32), thirds(-dot), jnp.zeros((LANES - HEAD_DIM - 16, rows), F32)]
            do_rows_ref[h, span(i, rows), :] = jnp.concatenate(wide, axis=0).T.astype(BF16)
        return carry

    lax.fori_loop(0, shards, prepare, 0)
    dq_ref[...] = jnp.zeros_like(dq_ref)
    for fetch in fetches[2:]:
        fetch.wait()

    def rotated_back(values, cosine, sine):
        first, second = values[:half], values[half:]
        return [first * cosine + second * sine, second * cosine - first * sine]

    def over_keys(j, carry):
        keys = span(j, rows)
        dk_ref[...] = jnp.zeros_like(dk_ref)
        dv_ref[...] = jnp.zeros_like(dv_ref)

        def over_queries(i, carry):
            queries = span(i, rows)
            for h in range(heads):
                k = k_ref[h, :, keys]
                probs = jnp.exp2(mm(q_rows_ref[h, queries, :], k))
                d_scores = (probs * mm(do_rows_ref[h, queries, :], v_ref[h, :, keys])).astype(BF16)
                dv_ref[h] += mm(do_ref[h * HEAD_DIM : (h + 1) * HEAD_DIM, queries], probs.astype(BF16))
                dk_ref[h] += mm(q_ref[h, :HEAD_DIM, queries], d_scores)
                dq_ref[h, :, queries] += mm(k[:HEAD_DIM], d_scores, NT)
            number = first_event + j * shards + i
            pl.when(number < events)(lambda: ring.event(number))
            return carry

        lax.fori_loop(0, shards, over_queries, 0)
        cosine, sine = cos_ref[:, keys] * (1.0 / LOG2E), sin_ref[:, keys] * (1.0 / LOG2E)
        pieces = []
        for h in range(heads):
            pieces += rotated_back(dk_ref[h], cosine, sine)
        pieces += [dv_ref[h] for h in range(heads)]
        d_qkv[j, cols:, :] = jnp.concatenate(pieces, axis=0).astype(BF16)
        return carry

    lax.fori_loop(0, shards, over_keys, 0)
    first_event = min(first_event + shards * shards, events)
    for i in range(shards):
        scale = 1.0 / math.sqrt(HEAD_DIM)
        cosine, sine = cos_ref[:, span(i, rows)] * scale, sin_ref[:, span(i, rows)] * scale
        pieces = []
        for h in range(heads):
            pieces += rotated_back(dq_ref[h, :, span(i, rows)], cosine, sine)
        d_qkv[i, :cols, :] = jnp.concatenate(pieces, axis=0).astype(BF16)
    near_copy = send(d_qkv.at[pl.ds(2, 2)], near, near_sem.at[0], near_sem.at[1], core)

    def product(first, count):
        piece = mm(d_qkv[0, first : first + count, :], x_ref[0])
        for slot in range(1, shards):
            piece += mm(d_qkv[slot, first : first + count, :], x_ref[slot])
        return piece

    chain_rows = total.shape[1]
    total[0] = product(0, chain_rows)
    total[1, :cols, :] = product(chain_rows, cols)
    piece = mm(att_ref[0], slots[0])
    for slot in range(1, shards):
        piece += mm(att_ref[slot], slots[slot])
    total[1, cols:, :] = piece
    small.start(0)

    def norm_exchange(stage):
        return send(sums_ref, norm_in.at[stage], norm_sem.at[0, stage], norm_sem.at[1, stage], partners[stage])

    norm_copy, norm_done = norm_exchange(0), 0
    near_copy.wait()

    def d_tokens(index):
        return mm(d_qkv[index], w_ref[...], TN) + mm(near[index], w_near_ref[...], TN)

    far_out[...] = d_tokens(1).astype(BF16)
    far_copy = send(far_out, far_in, far_sem.at[0], far_sem.at[1], far)
    own[...] = dh_ref[...] + d_tokens(0)

    left, share = first_event, -(-(events - first_event) // len(small.steps))
    small_done = 0
    while small_done < len(small.steps) or norm_done < len(partners):
        if small_done < len(small.steps):
            small.advance(small_done)
            small_done += 1
            for number in range(left, min(left + share, events)):
                ring.event(number)
            left = min(left + share, events)
        if norm_done < len(partners):
            norm_copy.wait()
            sums_ref[...] += norm_in[norm_done]
            norm_done += 1
            if norm_done < len(partners):
                norm_copy = norm_exchange(norm_done)
    far_copy.wait()
    dx_ref[...] = (own[...] + far_in[...].astype(F32)).astype(BF16)


def back(att, w_out, cosine, sine, norms, w_turned, w_near, dh, totals, dh_slots, q_rows, q, k, v, x_slots):
    size = lax.axis_size("dp")
    stages = size.bit_length() - 1
    heads, _, tokens = q.shape
    shards, rows, width = x_slots.shape
    cols = w_turned.shape[0]
    chain, big_chain = width // 2, totals.shape[1]
    sent = pieces_sent(size, 0) * (chain >> halvings(size))
    spots = min(RING_PIECES, size)
    ring_steps = spots - 1 + (size // spots).bit_length() - 1
    steps = stages + halvings(size)
    vmem = pl.BlockSpec(memory_space=pltpu.VMEM)
    hbm = pl.BlockSpec(memory_space=pl.ANY)
    dma = pltpu.SemaphoreType.DMA
    along = pltpu.VMEM((heads, LANES, tokens), BF16)
    return pl.pallas_call(
        functools.partial(back_kernel, size),
        out_shape=(
            jax.ShapeDtypeStruct((rows, width), BF16),
            jax.ShapeDtypeStruct((2, chain, width), BF16),
            jax.ShapeDtypeStruct((2, big_chain, width), BF16),
            jax.ShapeDtypeStruct(norms.shape, F32),
        ),
        in_specs=[vmem] * 8 + [hbm] * 7,
        out_specs=[vmem] * 4,
        scratch_shapes=[
            pltpu.VMEM(totals.shape, F32),
            pltpu.VMEM(dh_slots.shape, BF16),
            pltpu.VMEM((heads, tokens, LANES), BF16),
            along,
            along,
            along,
            pltpu.VMEM(x_slots.shape, BF16),
            pltpu.VMEM((heads * HEAD_DIM, tokens), BF16),
            pltpu.VMEM((heads, tokens, LANES), BF16),
            pltpu.VMEM((heads, HEAD_DIM, tokens), F32),
            pltpu.VMEM((heads, HEAD_DIM, rows), F32),
            pltpu.VMEM((heads, HEAD_DIM, rows), F32),
            pltpu.VMEM((shards, cols, rows), BF16),
            pltpu.VMEM((2, chain, width), F32),
            pltpu.VMEM((2, sent, width), BF16),
            pltpu.VMEM((2, sent, width), BF16),
            pltpu.VMEM((2, cols, rows), BF16),
            pltpu.VMEM((rows, width), BF16),
            pltpu.VMEM((rows, width), BF16),
            pltpu.VMEM((rows, width), F32),
            pltpu.VMEM((2 + stages,) + norms.shape, F32),
            *ring_scratch(size, big_chain, width, ring_steps),
            dma((2, 2, 2, spots - 1)),
            dma((7,)),
            dma((2,)),
            dma((2,)),
            dma((2, 2, steps)),
            dma((2, 2 + stages)),
        ],
        compiler_params=pltpu.CompilerParams(
            collective_id=1, has_side_effects=True, vmem_limit_bytes=WIDE_LIMIT
        ),
        cost_estimate=pl.CostEstimate(
            flops=5 * heads * tokens * tokens * LANES, bytes_accessed=60 * rows * width, transcendentals=0
        ),
        name="back",
    )(att, w_out, cosine, sine, norms, w_turned, w_near, dh, totals, dh_slots, q_rows, q, k, v, x_slots)


def emit_kernel(big_ref, small_ref, gate_up_ref, down_ref, qkv_ref, out_ref):
    for n in range(2):
        gate_up_ref[:, n, :] = big_ref[0, n].astype(F32)
    down_ref[...] = big_ref[0, 2].astype(F32)
    qkv_steps = pl.num_programs(0) * 3 // 4

    @pl.when(pl.program_id(0) < qkv_steps)
    def _():
        qkv_ref[...] = small_ref[0].astype(F32)

    @pl.when(pl.program_id(0) >= qkv_steps)
    def _():
        out_ref[...] = small_ref[0].astype(F32)


def emit(big, small):
    _, chain, width = small.shape
    steps = 8
    per, rows = steps // 2, width // steps
    qkv_steps = steps * 3 // 4
    shape = lambda *dims: jax.ShapeDtypeStruct(dims, F32)
    return pl.pallas_call(
        emit_kernel,
        out_shape=(
            shape(width, 2, width),
            shape(width, width),
            shape(qkv_steps * rows, width),
            shape((steps - qkv_steps) * rows, width),
        ),
        grid=(steps,),
        in_specs=[
            pl.BlockSpec((1, 3, rows, width), lambda i: (i // per, 0, i % per, 0)),
            pl.BlockSpec((1, rows, width), lambda i: (i // per, i % per, 0)),
        ],
        out_specs=[
            pl.BlockSpec((rows, 2, width), lambda i: (i, 0, 0)),
            pl.BlockSpec((rows, width), lambda i: (i, 0)),
            pl.BlockSpec((rows, width), lambda i: (jnp.minimum(i, qkv_steps - 1), 0)),
            pl.BlockSpec((rows, width), lambda i: (jnp.maximum(i - qkv_steps, 0), 0)),
        ],
        compiler_params=pltpu.CompilerParams(vmem_limit_bytes=VMEM_LIMIT),
        cost_estimate=pl.CostEstimate(flops=0, bytes_accessed=24 * width * width, transcendentals=0),
        name="emit",
    )(big.reshape(2, 3, chain, width), small)


def body(
    tokens, lengths, w_qkv, w_out, w_gate_up, w_down, ln1_scale, ln1_shift, ln2_scale, ln2_shift, cotangent
):
    rows, width = tokens.shape
    shards = lax.axis_size("mp")
    local_cols = w_out.shape[0]
    hidden_cols = w_down.shape[0]
    m = lax.axis_index("mp")
    qkv_turned = w_qkv.transpose(1, 2, 0).reshape(3 * local_cols, width)
    qkv_near = lax.ppermute(qkv_turned, "mp", [(i, i ^ 1) for i in range(shards)])
    norms = jnp.concatenate([jnp.stack([ln1_scale, ln1_shift, ln2_scale, ln2_shift]), jnp.zeros((4, width), F32)])
    output, dh, dh_slots, norms, totals, x_slots, q, k, v, q_rows, att, cosine, sine = first(
        lengths, tokens, cotangent, norms, qkv_turned, w_out, w_gate_up.reshape(width, 2 * hidden_cols), w_down
    )
    d_tokens, small, big, norms = back(
        att, w_out, cosine, sine, norms, qkv_turned, qkv_near, dh, totals, dh_slots, q_rows, q, k, v, x_slots
    )
    grad_gate_up, grad_down, grad_qkv, grad_out = emit(big, small)
    grad_qkv = grad_qkv.reshape(3, local_cols, width).transpose(2, 0, 1)
    norms = lax.dynamic_slice_in_dim(norms, m * local_cols, local_cols, 1)
    return (
        output,
        d_tokens,
        grad_qkv,
        grad_out,
        grad_gate_up,
        grad_down,
        norms[0],
        norms[1],
        norms[2],
        norms[3],
    )


def solution(mesh):
    return jax.shard_map(
        body,
        mesh=mesh,
        in_specs=(
            P(("dp", "mp"), None),
            P("dp", None),
            P(None, None, "mp"),
            P("mp", None),
            P(None, None, "mp"),
            P("mp", None),
            P(),
            P(),
            P(),
            P(),
            P(("dp", "mp"), None),
        ),
        out_specs=(
            P(("dp", "mp"), None),
            P(("dp", "mp"), None),
            P(None, None, "mp"),
            P("mp", None),
            P(None, None, "mp"),
            P("mp", None),
            P("mp"),
            P("mp"),
            P("mp"),
            P("mp"),
        ),
        check_vma=False,
    )
```

```python
import functools
import math

import jax
import jax.numpy as jnp
from jax import lax
from jax.experimental import pallas as pl
from jax.experimental.pallas import tpu as pltpu
from jax.sharding import PartitionSpec as P

F32 = jnp.float32
BF16 = jnp.bfloat16
HEAD_DIM = 64
LANES = 128
EPSILON = 1e-05
FAR = -(2.0**100)
LOG2E = math.log2(math.e)
NT = (((1,), (1,)), ((), ()))
TN = (((0,), (0,)), ((), ()))
NN = (((1,), (0,)), ((), ()))
VMEM_LIMIT = 58 << 20
WIDE_LIMIT = 62 << 20
MESH = pl.DeviceIdType.MESH


def mm(a, b, dims=NN):
    return lax.dot_general(a, b, dims, preferred_element_type=F32)


def thirds(row):
    high = row.astype(BF16).astype(F32)
    mid = (row - high).astype(BF16).astype(F32)
    low = row - high - mid
    return jnp.concatenate([high, mid, low, jnp.zeros((13, row.shape[1]), F32)], axis=0)


def span(index, size):
    if isinstance(index, int):
        return pl.ds(index * size, size)
    return pl.ds(pl.multiple_of(index * size, size), size)


def dp_orders(size):
    bits = list(range(size.bit_length() - 1))
    return [bits, bits[1::-1] + bits[2:]]


def halvings(size):
    return min(3, size.bit_length() - 1)


def peer_of(index, bit):
    mine = (index // (1 << bit)) % 2
    return index + (1 - 2 * mine) * (1 << bit), mine


def send(source, target, send_sem, recv_sem, partner):
    copy = pltpu.make_async_remote_copy(
        source, target, send_sem, recv_sem, device_id=partner, device_id_type=MESH
    )
    copy.start()
    return copy


def greet(partners):
    barrier = pltpu.get_barrier_semaphore()
    for partner in partners:
        pl.semaphore_signal(barrier, inc=1, device_id=partner, device_id_type=MESH)
    pl.semaphore_wait(barrier, len(partners))


RING_PIECES = 8
RING_EARLY = 2


class Ring:
    def __init__(self, size, me, total, give, take, result, scatter_sems, gather_sems):
        self.n = n = min(RING_PIECES, size)
        self.me, self.size = me, size
        self.total, self.give, self.take, self.result = total, give, take, result
        self.scatter_sems, self.gather_sems = scatter_sems, gather_sems
        self.rows, self.cols = total.shape[1] // n, total.shape[2] // 2
        low = me % n
        across, along = low % 2, low // 2
        self.spot = (1 - across) * along + across * (n - 1 - along)
        self.peers = [self.index_at((self.spot + step) % n) for step in (1, n - 1)]

    def index_at(self, spot):
        across = spot // (self.n // 2)
        along = (1 - across) * spot + across * (self.n - 1 - spot)
        return self.me - self.me % self.n + 2 * along + across

    def piece(self, chain, step):
        shift = self.n * 4 - step if chain == 0 else step
        return pl.ds(pl.multiple_of((self.spot + shift) % self.n * self.rows, 16), self.rows)

    def half(self, sub):
        return span(sub, self.cols)

    def scatter(self, chain, sub, step):
        return pltpu.make_async_remote_copy(
            self.give.at[chain, sub],
            self.take.at[chain, sub, step],
            self.scatter_sems.at[0, chain, sub, step],
            self.scatter_sems.at[1, chain, sub, step],
            device_id={"dp": self.peers[chain]},
            device_id_type=MESH,
        )

    def gather(self, chain, sub, step):
        part = self.result.at[chain, self.piece(chain, step + self.n - 1), self.half(sub)]
        return pltpu.make_async_remote_copy(
            part,
            part,
            self.gather_sems.at[0, chain, sub, step],
            self.gather_sems.at[1, chain, sub, step],
            device_id={"dp": self.peers[chain]},
            device_id_type=MESH,
        )

    def begin(self, step, chain):
        for sub in range(2):
            self.give[chain, sub] = self.total[chain, self.piece(chain, step), self.half(sub)].astype(BF16)
            self.scatter(chain, sub, step).start()

    def arrived(self, step, chain, sub):
        self.scatter(chain, sub, step).wait()
        mine = self.total[chain, self.piece(chain, step + 1), self.half(sub)]
        return mine + self.take[chain, sub, step].astype(F32)

    def keep(self, step):
        for chain in range(2):
            for sub in range(2):
                value = self.arrived(step, chain, sub)
                self.total[chain, self.piece(chain, step + 1), self.half(sub)] = value

    def pass_on(self, step, sub):
        for chain in range(2):
            self.give[chain, sub] = self.arrived(step, chain, sub).astype(BF16)
            self.scatter(chain, sub, step + 1).start()

    def turn(self, step, sub):
        for chain in range(2):
            value = self.arrived(step, chain, sub).astype(BF16)
            self.give[chain, sub] = value
        for stage in range((self.size // self.n).bit_length() - 1):
            copies = []
            for chain in range(2):
                peer = self.me // self.n
                mine = (peer // (1 << stage)) % 2
                copies.append(
                    pltpu.make_async_remote_copy(
                        self.give.at[chain, sub],
                        self.take.at[chain, sub, self.n - 1 + stage],
                        self.scatter_sems.at[0, chain, sub, self.n - 1 + stage],
                        self.scatter_sems.at[1, chain, sub, self.n - 1 + stage],
                        device_id={"dp": self.me + (1 - 2 * mine) * (self.n << stage)},
                        device_id_type=MESH,
                    )
                )
                copies[-1].start()
            for chain in range(2):
                copies[chain].wait()
                value = self.give[chain, sub].astype(F32) + self.take[chain, sub, self.n - 1 + stage].astype(F32)
                self.give[chain, sub] = value.astype(BF16)
        for chain in range(2):
            self.result[chain, self.piece(chain, self.n - 1), self.half(sub)] = self.give[chain, sub]
            self.gather(chain, sub, 0).start()

    def event(self, number):
        step, sub, n = number // 2, number % 2, self.n

        @pl.when(step < n - 2)
        def _():
            self.pass_on(step, sub)

        @pl.when(step == n - 2)
        def _():
            self.turn(n - 2, sub)

        @pl.when(step >= n - 1)
        def _():
            for chain in range(2):
                self.gather(chain, sub, step - (n - 1)).wait()

            @pl.when(step < 2 * n - 3)
            def _():
                for chain in range(2):
                    self.gather(chain, sub, step - (n - 2)).start()


def ring_scratch(size, rows, cols, steps):
    piece = (rows // min(RING_PIECES, size), cols // 2)
    return [
        pltpu.VMEM((2, 2) + piece, BF16),
        pltpu.VMEM((2, 2, steps) + piece, BF16),
        pltpu.SemaphoreType.DMA((2, 2, 2, steps)),
    ]


X_FAR, X_NEAR, X_LAST, W_IN, W_DOWN, W_OUT, ATT_NEAR, ATT_LAST = range(8)
BRANCH, NORMED, OUT, DOUT, DNORMED, DH, DH_NEAR, DH_LAST, GRAD_NEAR = range(8, 17)
KINDS = 17


def first_kernel(
    size, lengths, tok_ref, cot_ref, ln_ref, w_ref, wo_ref, win_hbm, wdn_hbm,
    out_ref, dh_ref, slots_ref, norms_ref, total_hbm, x_hbm, q_hbm, k_hbm, v_hbm, q_rows_hbm, att_hbm, cos_hbm, sin_hbm,
    x_ref, win, wdn, wo_near_ref, att, near, outbox, inbox, low, hat, res, own, r1, dlow, give, take, sums,
    ring_give, ring_take, ring_sems, sems, loads, stores,
):
    rows, width = tok_ref.shape
    hidden = wdn.shape[0] // 2
    cols = wo_ref.shape[0]
    heads = cols // HEAD_DIM
    shards = x_ref.shape[0]
    tokens = shards * rows
    half = width // 2
    chunk = rows // 2
    chunks = [slice(c * chunk, (c + 1) * chunk) for c in range(2)]
    m, me = lax.axis_index("mp"), lax.axis_index("dp")
    core, far = {"mp": peer_of(m, 0)[0]}, {"mp": peer_of(m, 1)[0]}
    ring_peers = Ring(size, me, give, None, None, None, None, None).peers
    greet([core, far] + [{"dp": peer} for peer in ring_peers])

    def link(kind, c, source, target, partner):
        return pltpu.make_async_remote_copy(
            source, target, sems.at[0, kind, c], sems.at[1, kind, c], device_id=partner, device_id_type=MESH
        )

    def post(kind, c, source, target, partner):
        copy = link(kind, c, source, target, partner)
        copy.start()
        return copy

    far_copies = [post(X_FAR, c, tok_ref.at[where], x_ref.at[2, where], far) for c, where in enumerate(chunks)]
    near_copy = post(X_NEAR, 0, tok_ref, x_ref.at[1], core)
    weight_copies = [
        post(W_OUT, 0, wo_ref, wo_near_ref, core),
        post(W_IN, 0, win_hbm, win.at[1], core),
        post(W_DOWN, 0, wdn_hbm, wdn.at[pl.ds(hidden, hidden)], core),
    ]
    fetches = []
    for n, (source, target) in enumerate([(win_hbm, win.at[0]), (wdn_hbm, wdn.at[pl.ds(0, hidden)])]):
        fetches.append(pltpu.make_async_copy(source, target, loads.at[n]))
        fetches[-1].start()
    x_ref[0] = tok_ref[...]
    sums[...] = jnp.zeros_like(sums)
    scale_one, shift_one, scale_two, shift_two = (ln_ref[i : i + 1, :] for i in range(4))

    def branch(slot, other, where):
        return mm(att[slot, :, where], wo_ref[...], TN) + mm(near[other, :, where], wo_near_ref[...], TN)

    def by_parts(c, part):
        step = 64

        def run(i, carry):
            part(pl.ds(pl.multiple_of(c * chunk + i * step, step), step))
            return carry

        lax.fori_loop(0, chunk // step, run, 0)

    def mean(values):
        return jnp.sum(values, axis=-1, keepdims=True) * (1.0 / width)

    def add_up(index, values):
        sums[index] += jnp.sum(values.reshape(values.shape[0] // 8, 8, width), axis=0)

    def norm_one(where):
        h = hat[where, :] + inbox[where, :].astype(F32)
        h = h - mean(h)
        r = lax.rsqrt(mean(h * h) + EPSILON)
        h = h * r
        hat[where, :] = h
        r1[where, :] = jnp.broadcast_to(r, (r.shape[0], LANES))
        h = h * scale_one + shift_one
        res[where, :] = h
        low[0, where, :] = h.astype(BF16)

    def attention(q_ref, k_ref, v_ref, k_rows_ref, q_rows_ref, cos_ref, sin_ref, top_ref, acc_ref):
        half_head = HEAD_DIM // 2
        starts, ends, end = [], [], 0
        for d in range(lengths.shape[1]):
            starts.append(end)
            end = end + lengths[0, d]
            ends.append(end)
        doc = lax.broadcasted_iota(jnp.int32, (16, rows), 0)
        first, last = jnp.zeros((16, rows), jnp.int32), jnp.zeros((16, rows), jnp.int32)
        for d in range(lengths.shape[1]):
            first, last = jnp.where(doc == d, starts[d], first), jnp.where(doc == d, ends[d], last)
        exponent = lax.broadcasted_iota(jnp.int32, (half_head, rows), 0).astype(F32)
        rate = jnp.exp(exponent * (-2.0 * math.log(1000.0) / HEAD_DIM))
        row = lax.broadcasted_iota(jnp.int32, (48, rows), 0)
        ones = jnp.where(row < 3, 1.0, 0.0)
        v_tail = jnp.concatenate([ones, jnp.zeros((16, rows), F32)], axis=0)
        top_ref[...] = jnp.full_like(top_ref, FAR)
        acc_ref[...] = jnp.zeros_like(acc_ref)

        def tables(slot):
            where = slice(slot * rows, (slot + 1) * rows)
            shard = 2 * ((slot // 2 + m // 2) % 2) + (slot + m) % 2
            token = lax.broadcasted_iota(jnp.int32, (16, rows), 1) + shard * rows
            inside = (token >= first) & (token < last)
            begin = jnp.max(jnp.where(inside, first, 0), axis=0, keepdims=True)
            angles = rate * (token[0:1] - begin).astype(F32)
            cos_ref[:, where], sin_ref[:, where] = jnp.cos(angles), jnp.sin(angles)
            for h in range(heads):
                q_ref[h, HEAD_DIM:, where] = jnp.concatenate(
                    [jnp.where(inside, 0.0, FAR), jnp.zeros((48, rows), F32)], axis=0
                ).astype(BF16)
                k_ref[h, HEAD_DIM:, where] = jnp.concatenate([jnp.where(inside, 1.0, 0.0), ones], axis=0).astype(BF16)
                v_ref[h, HEAD_DIM:, where] = v_tail.astype(BF16)

        def project(slot, c):
            where = slice(slot * rows + c * chunk, slot * rows + (c + 1) * chunk)
            projected = mm(w_ref[...], x_ref[slot, chunks[c], :], NT)
            cosine, sine = cos_ref[:, where], sin_ref[:, where]

            def rotated(start, scale):
                one, two = projected[start : start + half_head], projected[start + half_head : start + HEAD_DIM]
                turned = jnp.concatenate([one * cosine - two * sine, two * cosine + one * sine], axis=0)
                return turned * scale

            for h in range(heads):
                q_ref[h, :HEAD_DIM, where] = rotated(h * HEAD_DIM, LOG2E / math.sqrt(HEAD_DIM)).astype(BF16)
                k = rotated(cols + h * HEAD_DIM, 1.0)
                k_ref[h, :HEAD_DIM, where] = k.astype(BF16)
                tail = k_ref[h, HEAD_DIM:, where].astype(F32)
                k_rows_ref[h, where, :] = jnp.concatenate([k, tail], axis=0).T.astype(BF16)
                start = 2 * cols + h * HEAD_DIM
                v_ref[h, :HEAD_DIM, where] = projected[start : start + HEAD_DIM].astype(BF16)

        def pairs(count, pair):
            def run(n, carry):
                qs, group = pair(n)
                queries, keys = span(qs, chunk), span(group, 2 * rows)
                scores, olds, tops = [], [], []
                for h in range(heads):
                    s = mm(k_rows_ref[h, keys, :], q_ref[h, :, queries])
                    olds.append(top_ref[qs, h, 0:1, :])
                    tops.append(jnp.maximum(olds[h], jnp.max(s, axis=0, keepdims=True)))
                    scores.append(s)
                for h in range(heads):
                    probs = jnp.exp2(scores[h] - tops[h]).astype(BF16)
                    top_ref[qs, h, 0:1, :] = tops[h]
                    acc_ref[qs, h] = acc_ref[qs, h] * jnp.exp2(olds[h] - tops[h]) + mm(v_ref[h, :80, keys], probs)
                return carry

            lax.fori_loop(0, count, run, 0)

        writes = []

        def write(source, target):
            writes.append(pltpu.make_async_copy(source, target, stores.at[len(writes)]))
            writes[-1].start()

        def settle(slot, c):
            part = 2 * slot + c
            for h in range(heads):
                total = acc_ref[part, h, HEAD_DIM : HEAD_DIM + 1, :]
                out = acc_ref[part, h, :HEAD_DIM, :] / total
                att[slot, h * HEAD_DIM : (h + 1) * HEAD_DIM, chunks[c]] = out.astype(BF16)
                top_ref[part, h, 1:2, :] = top_ref[part, h, 0:1, :] + jnp.log2(total)

        def turn(part, carry):
            where = span(part, chunk)
            for h in range(heads):
                query = q_ref[h, :, where].astype(F32)
                wide = jnp.concatenate([query[:80], thirds(-top_ref[part, h, 1:2, :]), query[96:]], axis=0)
                q_rows_ref[h, where, :] = wide.T.astype(BF16)
            return carry

        for slot in range(4):
            tables(slot)
        last_copies = []

        def hand_on(c):
            far_copies[c].wait()
            last_copies.append(post(X_LAST, c, x_ref.at[2, chunks[c]], x_ref.at[3, chunks[c]], core))

        for c in range(2):
            project(0, c)
        near_copy.wait()
        for c in range(2):
            project(1, c)
        hand_on(0)
        pairs(4, lambda n: (n, 0))
        project(2, 0)
        last_copies[0].wait()
        project(3, 0)
        hand_on(1)
        project(2, 1)
        last_copies[1].wait()
        project(3, 1)
        for source, target in [
            (x_ref, x_hbm), (q_ref, q_hbm), (k_ref, k_hbm), (v_ref, v_hbm), (cos_ref, cos_hbm), (sin_ref, sin_hbm)
        ]:
            write(source, target)
        weight_copies[0].wait()
        branch_copies = []
        for c, where in enumerate(chunks):
            pairs(2, lambda n: (6 + c, n))
            settle(3, c)
            last_att = post(ATT_LAST, c, att.at[3, :, where], near.at[1, :, where], core)
            pairs(2, lambda n: (4 + c, n))
            settle(2, c)
            last_att.wait()
            outbox[where, :] = branch(2, 1, where).astype(BF16)
            branch_copies.append(post(BRANCH, c, outbox.at[where], inbox.at[where], far))
        pairs(4, lambda n: (3 - n, 1))
        for c in range(2):
            settle(1, c)
        near_att = post(ATT_NEAR, 0, att.at[1], near.at[0], core)
        for c in range(2):
            settle(0, c)
        write(att, att_hbm)
        near_att.wait()
        for where in chunks:
            hat[where, :] = tok_ref[where, :].astype(F32) + branch(0, 0, where)
        for c, where in enumerate(chunks):
            branch_copies[c].wait()
            by_parts(c, norm_one)
            post(NORMED, c, low.at[0, where], low.at[1, where], far)
        lax.fori_loop(0, 2 * shards, turn, 0)
        write(q_rows_ref, q_rows_hbm)
        for copy in writes:
            copy.wait()

    along = pltpu.VMEM((heads, LANES, tokens), BF16)
    down = pltpu.VMEM((heads, tokens, LANES), BF16)
    table = pltpu.VMEM((HEAD_DIM // 2, tokens), F32)
    pl.run_scoped(
        attention, along, along, along, down, down, table, table,
        pltpu.VMEM((2 * shards, heads, 8, chunk), F32), pltpu.VMEM((2 * shards, heads, 80, chunk), F32),
    )
    normed_copies = [link(NORMED, c, low.at[0, where], low.at[1, where], far) for c, where in enumerate(chunks)]
    for copy in fetches + weight_copies[1:]:
        copy.wait()

    def feed_forward(gu, hid, total):
        ring = Ring(size, me, total, ring_give, ring_take, None, ring_sems, None)
        tile = hidden // 2

        def mlp(side, where):
            def columns(t, carry):
                k, at = t // 2, (t % 2) * tile
                x = low[side, where, :]
                gate_at = pl.ds(pl.multiple_of(at, LANES), tile)
                up_at = pl.ds(pl.multiple_of(hidden + at, LANES), tile)
                gate, up = mm(x, win[k, :, gate_at]), mm(x, win[k, :, up_at])
                gu[side, k, where, gate_at] = gate.astype(BF16)
                gu[side, k, where, up_at] = up.astype(BF16)
                value = gate * jax.nn.sigmoid(gate) * up
                hid[side, where, pl.ds(pl.multiple_of(k * hidden + at, LANES), tile)] = value.astype(BF16)
                return carry

            lax.fori_loop(0, 4, columns, 0)
            return mm(hid[side, where, :], wdn[...])

        def both_sides(copies_in, kind, compute):
            copies = []
            for c, where in enumerate(chunks):
                own[where, :] = compute(0, where)
                copies_in[c].wait()
                outbox[where, :] = compute(1, where).astype(BF16)
                copies.append(post(kind, c, outbox.at[where], inbox.at[where], far))
            return copies

        out_copies = both_sides(normed_copies, OUT, mlp)

        def norm_two(where):
            z = res[where, :] + own[where, :] + inbox[where, :].astype(F32)
            z = z - mean(z)
            r = lax.rsqrt(mean(z * z) + EPSILON)
            z = z * r
            out_ref[where, :] = (z * scale_two + shift_two).astype(BF16)
            g = cot_ref[where, :].astype(F32)
            add_up(2, g * z)
            add_up(3, g)
            e = g * scale_two
            dz = r * (e - mean(e) - z * mean(e * z))
            res[where, :] = dz
            dlow[0, where, :] = dz.astype(BF16)

        dout_copies = []
        for c, where in enumerate(chunks):
            out_copies[c].wait()
            by_parts(c, norm_two)
            dout_copies.append(post(DOUT, c, dlow.at[0, where], dlow.at[1, where], far))

        def mlp_back(side, where):
            def columns(t, carry):
                k, at = t // 2, (t % 2) * tile
                d_hidden = mm(
                    dlow[side, where, :], wdn[pl.ds(pl.multiple_of(k * hidden + at, LANES), tile), :], NT
                )
                gate_at = pl.ds(pl.multiple_of(at, LANES), tile)
                up_at = pl.ds(pl.multiple_of(hidden + at, LANES), tile)
                gate, up = gu[side, k, where, gate_at].astype(F32), gu[side, k, where, up_at].astype(F32)
                s = jax.nn.sigmoid(gate)
                gu[side, k, where, gate_at] = (d_hidden * up * s * (1.0 + gate * (1.0 - s))).astype(BF16)
                gu[side, k, where, up_at] = (d_hidden * gate * s).astype(BF16)
                return carry

            lax.fori_loop(0, 4, columns, 0)
            return mm(gu[side, 0, where, :], win[0], NT) + mm(gu[side, 1, where, :], win[1], NT)

        dnormed_copies = both_sides(dout_copies, DNORMED, mlp_back)

        def weight_grads(k, target, then=lambda r: None):
            def chain(r, carry):
                at = pl.ds(pl.multiple_of(r * half, LANES), half)
                for n, place in enumerate((slice(0, hidden), slice(hidden, 2 * hidden))):
                    piece = mm(low[0, :, at], gu[0, k, :, place], TN) + mm(low[1, :, at], gu[1, k, :, place], TN)
                    target[r, n * half : (n + 1) * half, :] = piece.astype(target.dtype)
                at = pl.ds(pl.multiple_of(k * hidden + r * half, LANES), half)
                piece = mm(hid[0, :, at], dlow[0], TN) + mm(hid[1, :, at], dlow[1], TN)
                target[r, 2 * half : 3 * half, :] = piece.astype(target.dtype)
                then(r)
                return carry

            lax.fori_loop(0, 2, chain, 0)

        def grad_copy(r):
            return link(GRAD_NEAR, r, give.at[r], take.at[r], core)

        weight_grads(1, give, lambda r: grad_copy(r).start())

        def norm_one_back(where):
            d = res[where, :] + own[where, :] + inbox[where, :].astype(F32)
            h = hat[where, :]
            add_up(0, d * h)
            add_up(1, d)
            e = d * scale_one
            dh = r1[where, 0:1] * (e - mean(e) - h * mean(e * h))
            dh_ref[where, :] = dh
            slots_ref[0, where, :] = dh.astype(BF16)

        dh_copies, last_copies = [], []

        def dh_chunk(c):
            where = chunks[c]
            dnormed_copies[c].wait()
            by_parts(c, norm_one_back)
            mine = slots_ref.at[0, where]
            dh_copies.append(post(DH, c, mine, slots_ref.at[2, where], far))
            last_copies.append(post(DH_NEAR, c, mine, slots_ref.at[1, where], core))

        dh_chunk(0)
        weight_grads(0, total)
        dh_chunk(1)
        for r in range(2):
            grad_copy(r).wait()
            total[r] += take[r].astype(F32)
            ring.begin(0, r)

        def hand_on(c):
            dh_copies[c].wait()
            where = chunks[c]
            last_copies.append(post(DH_LAST, c, slots_ref.at[2, where], slots_ref.at[3, where], core))

        for i in range(4):
            norms_ref[i : i + 1, :] = jnp.sum(sums[i], axis=0, keepdims=True)
        norms_ref[4:8, :] = jnp.zeros((4, width), F32)
        for step in range(RING_EARLY - 1):
            for sub in range(2):
                ring.pass_on(step, sub)
            if step < 2:
                hand_on(step)
        for step in range(RING_EARLY - 1, 2):
            hand_on(step)
        ring.keep(RING_EARLY - 1)
        write = pltpu.make_async_copy(total, total_hbm, loads.at[0])
        write.start()
        for copy in last_copies:
            copy.wait()
        write.wait()

    pl.run_scoped(
        feed_forward,
        pltpu.VMEM((2, 2, rows, 2 * hidden), BF16),
        pltpu.VMEM((2, rows, 2 * hidden), BF16),
        pltpu.VMEM((2, 3 * half, width), F32),
    )


def first(lengths, tokens, cotangent, norms, w_turned, w_out, w_in, w_down):
    size, shards = lax.axis_size("dp"), lax.axis_size("mp")
    rows, width = tokens.shape
    cols, hidden = w_out.shape[0], w_down.shape[0]
    heads, length = cols // HEAD_DIM, rows * shards
    chain = 3 * width // 2
    vmem = pl.BlockSpec(memory_space=pltpu.VMEM)
    hbm = pl.BlockSpec(memory_space=pl.ANY)
    dma = pltpu.SemaphoreType.DMA
    shape = jax.ShapeDtypeStruct
    along, table = shape((heads, LANES, length), BF16), shape((HEAD_DIM // 2, length), F32)
    wide = lambda dtype, *lead: pltpu.VMEM(lead + (rows, width), dtype)
    return pl.pallas_call(
        functools.partial(first_kernel, size),
        out_shape=(
            shape((rows, width), BF16),
            shape((rows, width), F32),
            shape((shards, rows, width), BF16),
            shape((8, width), F32),
            shape((2, chain, width), F32),
            shape((shards, rows, width), BF16),
            along,
            along,
            along,
            shape((heads, length, LANES), BF16),
            shape((shards, cols, rows), BF16),
            table,
            table,
        ),
        in_specs=[pl.BlockSpec(memory_space=pltpu.SMEM)] + [vmem] * 5 + [hbm] * 2,
        out_specs=[vmem] * 4 + [hbm] * 9,
        scratch_shapes=[
            wide(BF16, shards),
            pltpu.VMEM((2, width, 2 * hidden), BF16),
            pltpu.VMEM((2 * hidden, width), BF16),
            pltpu.VMEM((cols, width), BF16),
            pltpu.VMEM((shards, cols, rows), BF16),
            pltpu.VMEM((2, cols, rows), BF16),
            wide(BF16),
            wide(BF16),
            wide(BF16, 2),
            wide(F32),
            wide(F32),
            wide(F32),
            pltpu.VMEM((rows, LANES), F32),
            wide(BF16, 2),
            pltpu.VMEM((2, chain, width), BF16),
            pltpu.VMEM((2, chain, width), BF16),
            pltpu.VMEM((4, 8, width), F32),
            *ring_scratch(size, chain, width, RING_EARLY),
            dma((2, KINDS, 2)),
            dma((2,)),
            dma((8,)),
        ],
        compiler_params=pltpu.CompilerParams(
            collective_id=0, has_side_effects=True, vmem_limit_bytes=WIDE_LIMIT
        ),
        cost_estimate=pl.CostEstimate(
            flops=36 * rows * width * hidden, bytes_accessed=40 * rows * width, transcendentals=0
        ),
        name="first",
    )(lengths, tokens, cotangent, norms, w_turned, w_out, w_in, w_down)


class Sum:
    def __init__(self, size, me, first, total, give, take, result, sems):
        orders = dp_orders(size)
        self.total, self.give, self.take, self.result, self.sems = total, give, take, result, sems
        halving, stages = halvings(size), size.bit_length() - 1
        count = 1 << (halving - first)
        self.rows = total.shape[1] // count
        base, low, peers = [], [0, 0], []
        for chain in range(2):
            peers.append([peer_of(me, bit) for bit in orders[chain]])
            base.append(sum(peers[chain][done][1] * (1 << (halving - 1 - done)) for done in range(first)))
        self.steps, spot = [], 0
        for stage in range(first, stages):
            halve = stage < halving
            part = count // 2 if halve else count
            step = dict(kind="halve" if halve else "swap", part=part, spot=spot, chains=[], last=stage + 1 == stages)
            for chain in range(2):
                peer, mine = peers[chain][stage]
                away = low[chain] + (1 - mine) * part if halve else low[chain]
                low[chain] = low[chain] + mine * part if halve else low[chain]
                step["chains"].append(dict(peer=peer, away=away, keep=low[chain], final=base[chain] + low[chain]))
            self.steps.append(step)
            spot, count = spot + part, part
        low = [base[chain] + low[chain] for chain in range(2)]
        for stage in reversed(range(halving)):
            step = dict(kind="gather", part=count, chains=[])
            for chain in range(2):
                peer, mine = peers[chain][stage]
                step["chains"].append(dict(peer=peer, away=low[chain]))
                low[chain] = low[chain] - mine * count
            self.steps.append(step)
            count *= 2

    def block(self, low, count):
        return pl.ds(pl.multiple_of(low * self.rows, 16), count * self.rows)

    def copy(self, index, chain):
        step = self.steps[index]
        one = step["chains"][chain]
        if step["kind"] == "gather":
            source = target = self.result.at[chain, self.block(one["away"], step["part"])]
        else:
            spot = pl.ds(step["spot"] * self.rows, step["part"] * self.rows)
            source, target = self.give.at[chain, spot], self.take.at[chain, spot]
        return pltpu.make_async_remote_copy(
            source,
            target,
            self.sems.at[0, chain, index],
            self.sems.at[1, chain, index],
            device_id={"dp": one["peer"]},
            device_id_type=MESH,
        )

    def start(self, index):
        step = self.steps[index]
        for chain in range(2):
            if step["kind"] != "gather":
                spot = pl.ds(step["spot"] * self.rows, step["part"] * self.rows)
                away = self.block(step["chains"][chain]["away"], step["part"])
                self.give[chain, spot, :] = self.total[chain, away, :].astype(BF16)
            self.copy(index, chain).start()

    def finish(self, index):
        step = self.steps[index]
        for chain in range(2):
            self.copy(index, chain).wait()
            if step["kind"] == "gather":
                continue
            one = step["chains"][chain]
            spot = pl.ds(step["spot"] * self.rows, step["part"] * self.rows)
            keep = self.block(one["keep"], step["part"])
            mine = self.total[chain, keep, :] if step["kind"] == "halve" else self.give[chain, spot, :].astype(F32)
            value = mine + self.take[chain, spot, :].astype(F32)
            if step["last"]:
                self.result[chain, self.block(one["final"], 1), :] = value.astype(BF16)
            else:
                self.total[chain, keep, :] = value

    def advance(self, index):
        self.finish(index)
        if index + 1 < len(self.steps):
            self.start(index + 1)


def pieces_sent(size, first):
    halving = halvings(size)
    return (1 << (halving - first)) - 1 + size.bit_length() - 1 - halving


def back_kernel(
    size, att_ref, w_out_ref, cos_ref, sin_ref, norms_ref, w_ref, w_near_ref, dh_ref,
    total_hbm, slots_hbm, q_rows_hbm, q_hbm, k_hbm, v_hbm, x_hbm,
    dx_ref, grad_ref, big_ref, sums_ref,
    big, slots, q_rows_ref, q_ref, k_ref, v_ref, x_ref,
    do_ref, do_rows_ref, dq_ref, dk_ref, dv_ref, d_qkv,
    total, give, take, near, far_out, far_in, own, norm_in,
    ring_give, ring_take, ring_sems, gather_sems, loads, near_sem, far_sem, sum_sems, norm_sem,
):
    heads, _, tokens = k_ref.shape
    shards, rows, width = slots.shape
    cols = heads * HEAD_DIM
    half = HEAD_DIM // 2
    m, me = lax.axis_index("mp"), lax.axis_index("dp")
    stages = size.bit_length() - 1
    core, far = {"mp": peer_of(m, 0)[0]}, {"mp": peer_of(m, 1)[0]}
    partners = [core, far] + [{"dp": peer_of(me, bit)[0]} for bit in range(stages)]
    sources = [total_hbm, slots_hbm, q_rows_hbm, q_hbm, k_hbm, v_hbm, x_hbm]
    targets = [big, slots, q_rows_ref, q_ref, k_ref, v_ref, x_ref]
    fetches = [
        pltpu.make_async_copy(source, target, loads.at[n])
        for n, (source, target) in enumerate(zip(sources, targets))
    ]
    for fetch in fetches:
        fetch.start()
    ring = Ring(size, me, big, ring_give, ring_take, big_ref, ring_sems, gather_sems)
    greet(partners + [{"dp": peer} for peer in ring.peers])
    sums_ref[...] = norms_ref[...]
    small = Sum(size, me, 0, total, give, take, grad_ref, sum_sems)
    fetches[0].wait()
    for chain in range(2):
        ring.begin(RING_EARLY, chain)
    fetches[1].wait()
    events = 2 * (2 * ring.n - 2)
    first_event = 2 * RING_EARLY

    def prepare(i, carry):
        d_att = mm(w_out_ref[...], slots[i], NT).astype(BF16)
        do_ref[:, span(i, rows)] = d_att
        products = d_att.astype(F32) * att_ref[i].astype(F32)
        for h in range(heads):
            mine = slice(h * HEAD_DIM, (h + 1) * HEAD_DIM)
            dot = jnp.sum(products[mine], axis=0, keepdims=True)
            wide = [d_att[mine].astype(F32), thirds(-dot), jnp.zeros((LANES - HEAD_DIM - 16, rows), F32)]
            do_rows_ref[h, span(i, rows), :] = jnp.concatenate(wide, axis=0).T.astype(BF16)
        return carry

    lax.fori_loop(0, shards, prepare, 0)
    dq_ref[...] = jnp.zeros_like(dq_ref)
    for fetch in fetches[2:]:
        fetch.wait()

    def rotated_back(values, cosine, sine):
        first, second = values[:half], values[half:]
        return [first * cosine + second * sine, second * cosine - first * sine]

    def over_keys(j, carry):
        keys = span(j, rows)
        dk_ref[...] = jnp.zeros_like(dk_ref)
        dv_ref[...] = jnp.zeros_like(dv_ref)

        def over_queries(i, carry):
            queries = span(i, rows)
            for h in range(heads):
                k = k_ref[h, :, keys]
                probs = jnp.exp2(mm(q_rows_ref[h, queries, :], k))
                d_scores = (probs * mm(do_rows_ref[h, queries, :], v_ref[h, :, keys])).astype(BF16)
                dv_ref[h] += mm(do_ref[h * HEAD_DIM : (h + 1) * HEAD_DIM, queries], probs.astype(BF16))
                dk_ref[h] += mm(q_ref[h, :HEAD_DIM, queries], d_scores)
                dq_ref[h, :, queries] += mm(k[:HEAD_DIM], d_scores, NT)
            number = first_event + j * shards + i
            pl.when(number < events)(lambda: ring.event(number))
            return carry

        lax.fori_loop(0, shards, over_queries, 0)
        cosine, sine = cos_ref[:, keys] * (1.0 / LOG2E), sin_ref[:, keys] * (1.0 / LOG2E)
        pieces = []
        for h in range(heads):
            pieces += rotated_back(dk_ref[h], cosine, sine)
        pieces += [dv_ref[h] for h in range(heads)]
        d_qkv[j, cols:, :] = jnp.concatenate(pieces, axis=0).astype(BF16)
        return carry

    lax.fori_loop(0, shards, over_keys, 0)
    first_event = min(first_event + shards * shards, events)
    for i in range(shards):
        scale = 1.0 / math.sqrt(HEAD_DIM)
        cosine, sine = cos_ref[:, span(i, rows)] * scale, sin_ref[:, span(i, rows)] * scale
        pieces = []
        for h in range(heads):
            pieces += rotated_back(dq_ref[h, :, span(i, rows)], cosine, sine)
        d_qkv[i, :cols, :] = jnp.concatenate(pieces, axis=0).astype(BF16)
    near_copies = [send(d_qkv.at[2 * i + 1], near.at[i], near_sem.at[0, i], near_sem.at[1, i], core) for i in range(2)]

    def product(first, count):
        piece = mm(d_qkv[0, first : first + count, :], x_ref[0])
        for slot in range(1, shards):
            piece += mm(d_qkv[slot, first : first + count, :], x_ref[slot])
        return piece

    chain_rows = total.shape[1]
    total[0] = product(0, chain_rows)
    total[1, :cols, :] = product(chain_rows, cols)
    piece = mm(att_ref[0], slots[0])
    for slot in range(1, shards):
        piece += mm(att_ref[slot], slots[slot])
    total[1, cols:, :] = piece
    small.start(0)

    def norm_exchange(stage):
        return send(sums_ref, norm_in.at[stage], norm_sem.at[0, stage], norm_sem.at[1, stage], partners[stage])

    norm_copy, norm_done = norm_exchange(0), 0
    for copy in near_copies:
        copy.wait()

    def d_tokens(index):
        return mm(d_qkv[2 * index], w_ref[...], TN) + mm(near[index], w_near_ref[...], TN)

    far_out[...] = d_tokens(1).astype(BF16)
    far_copy = send(far_out, far_in, far_sem.at[0], far_sem.at[1], far)
    own[...] = dh_ref[...] + d_tokens(0)

    left, share = first_event, -(-(events - first_event) // len(small.steps))
    small_done = 0
    while small_done < len(small.steps) or norm_done < len(partners):
        if small_done < len(small.steps):
            small.advance(small_done)
            small_done += 1
            for number in range(left, min(left + share, events)):
                ring.event(number)
            left = min(left + share, events)
        if norm_done < len(partners):
            norm_copy.wait()
            sums_ref[...] += norm_in[norm_done]
            norm_done += 1
            if norm_done < len(partners):
                norm_copy = norm_exchange(norm_done)
    far_copy.wait()
    dx_ref[...] = (own[...] + far_in[...].astype(F32)).astype(BF16)


def back(att, w_out, cosine, sine, norms, w_turned, w_near, dh, totals, dh_slots, q_rows, q, k, v, x_slots):
    size = lax.axis_size("dp")
    stages = size.bit_length() - 1
    heads, _, tokens = q.shape
    shards, rows, width = x_slots.shape
    cols = w_turned.shape[0]
    chain, big_chain = width // 2, totals.shape[1]
    sent = pieces_sent(size, 0) * (chain >> halvings(size))
    spots = min(RING_PIECES, size)
    ring_steps = spots - 1 + (size // spots).bit_length() - 1
    steps = stages + halvings(size)
    vmem = pl.BlockSpec(memory_space=pltpu.VMEM)
    hbm = pl.BlockSpec(memory_space=pl.ANY)
    dma = pltpu.SemaphoreType.DMA
    along = pltpu.VMEM((heads, LANES, tokens), BF16)
    return pl.pallas_call(
        functools.partial(back_kernel, size),
        out_shape=(
            jax.ShapeDtypeStruct((rows, width), BF16),
            jax.ShapeDtypeStruct((2, chain, width), BF16),
            jax.ShapeDtypeStruct((2, big_chain, width), BF16),
            jax.ShapeDtypeStruct(norms.shape, F32),
        ),
        in_specs=[vmem] * 8 + [hbm] * 7,
        out_specs=[vmem] * 4,
        scratch_shapes=[
            pltpu.VMEM(totals.shape, F32),
            pltpu.VMEM(dh_slots.shape, BF16),
            pltpu.VMEM((heads, tokens, LANES), BF16),
            along,
            along,
            along,
            pltpu.VMEM(x_slots.shape, BF16),
            pltpu.VMEM((heads * HEAD_DIM, tokens), BF16),
            pltpu.VMEM((heads, tokens, LANES), BF16),
            pltpu.VMEM((heads, HEAD_DIM, tokens), F32),
            pltpu.VMEM((heads, HEAD_DIM, rows), F32),
            pltpu.VMEM((heads, HEAD_DIM, rows), F32),
            pltpu.VMEM((shards, cols, rows), BF16),
            pltpu.VMEM((2, chain, width), F32),
            pltpu.VMEM((2, sent, width), BF16),
            pltpu.VMEM((2, sent, width), BF16),
            pltpu.VMEM((2, cols, rows), BF16),
            pltpu.VMEM((rows, width), BF16),
            pltpu.VMEM((rows, width), BF16),
            pltpu.VMEM((rows, width), F32),
            pltpu.VMEM((2 + stages,) + norms.shape, F32),
            *ring_scratch(size, big_chain, width, ring_steps),
            dma((2, 2, 2, spots - 1)),
            dma((7,)),
            dma((2, 2)),
            dma((2,)),
            dma((2, 2, steps)),
            dma((2, 2 + stages)),
        ],
        compiler_params=pltpu.CompilerParams(
            collective_id=1, has_side_effects=True, vmem_limit_bytes=WIDE_LIMIT
        ),
        cost_estimate=pl.CostEstimate(
            flops=5 * heads * tokens * tokens * LANES, bytes_accessed=60 * rows * width, transcendentals=0
        ),
        name="back",
    )(att, w_out, cosine, sine, norms, w_turned, w_near, dh, totals, dh_slots, q_rows, q, k, v, x_slots)


def emit_kernel(big_ref, small_ref, out_ref, dx_ref, gate_up_hbm, down_ref, qkv_ref, w_out_ref, out_copy_ref, dx_copy_ref, wide, sems):
    step, steps = pl.program_id(0), pl.num_programs(0)
    rows = down_ref.shape[0]

    def copies(which):
        return [
            pltpu.make_async_copy(
                wide.at[which % 2, n], gate_up_hbm.at[span(which, rows), n, :], sems.at[which % 2, n]
            )
            for n in range(2)
        ]

    @pl.when(step >= 2)
    def _():
        for copy in copies(step - 2):
            copy.wait()

    for n in range(2):
        wide[step % 2, n] = big_ref[0, n].astype(F32)
    for copy in copies(step):
        copy.start()
    down_ref[...] = big_ref[0, 2].astype(F32)
    out_copy_ref[...] = out_ref[...]
    dx_copy_ref[...] = dx_ref[...]
    qkv_steps = steps * 3 // 4

    @pl.when(step < qkv_steps)
    def _():
        qkv_ref[...] = small_ref[0].astype(F32)

    @pl.when(step >= qkv_steps)
    def _():
        w_out_ref[...] = small_ref[0].astype(F32)

    @pl.when(step == steps - 1)
    def _():
        for which in (steps - 2, steps - 1):
            for copy in copies(which):
                copy.wait()


def emit(big, small, output, d_tokens):
    _, chain, width = small.shape
    steps = 8
    per, rows = steps // 2, width // steps
    qkv_steps = steps * 3 // 4
    tokens = output.shape[0] // steps
    shape = lambda *dims: jax.ShapeDtypeStruct(dims, F32)
    low = jax.ShapeDtypeStruct(output.shape, BF16)
    few = pl.BlockSpec((tokens, width), lambda i: (i, 0))
    return pl.pallas_call(
        emit_kernel,
        out_shape=(
            shape(width, 2, width),
            shape(width, width),
            shape(qkv_steps * rows, width),
            shape((steps - qkv_steps) * rows, width),
            low,
            low,
        ),
        grid=(steps,),
        in_specs=[
            pl.BlockSpec((1, 3, rows, width), lambda i: (i // per, 0, i % per, 0)),
            pl.BlockSpec((1, rows, width), lambda i: (i // per, i % per, 0)),
            few,
            few,
        ],
        out_specs=[
            pl.BlockSpec(memory_space=pl.ANY),
            pl.BlockSpec((rows, width), lambda i: (i, 0)),
            pl.BlockSpec((rows, width), lambda i: (jnp.minimum(i, qkv_steps - 1), 0)),
            pl.BlockSpec((rows, width), lambda i: (jnp.maximum(i - qkv_steps, 0), 0)),
            few,
            few,
        ],
        scratch_shapes=[pltpu.VMEM((2, 2, rows, width), F32), pltpu.SemaphoreType.DMA((2, 2))],
        compiler_params=pltpu.CompilerParams(vmem_limit_bytes=VMEM_LIMIT),
        cost_estimate=pl.CostEstimate(flops=0, bytes_accessed=24 * width * width, transcendentals=0),
        name="emit",
    )(big.reshape(2, 3, chain, width), small, output, d_tokens)


def body(
    tokens, lengths, w_qkv, w_out, w_gate_up, w_down, ln1_scale, ln1_shift, ln2_scale, ln2_shift, cotangent
):
    rows, width = tokens.shape
    shards = lax.axis_size("mp")
    local_cols = w_out.shape[0]
    hidden_cols = w_down.shape[0]
    m = lax.axis_index("mp")
    qkv_turned = w_qkv.transpose(1, 2, 0).reshape(3 * local_cols, width)
    qkv_near = lax.ppermute(qkv_turned, "mp", [(i, i ^ 1) for i in range(shards)])
    norms = jnp.concatenate([jnp.stack([ln1_scale, ln1_shift, ln2_scale, ln2_shift]), jnp.zeros((4, width), F32)])
    output, dh, dh_slots, norms, totals, x_slots, q, k, v, q_rows, att, cosine, sine = first(
        lengths, tokens, cotangent, norms, qkv_turned, w_out, w_gate_up.reshape(width, 2 * hidden_cols), w_down
    )
    d_tokens, small, big, norms = back(
        att, w_out, cosine, sine, norms, qkv_turned, qkv_near, dh, totals, dh_slots, q_rows, q, k, v, x_slots
    )
    grad_gate_up, grad_down, grad_qkv, grad_out, output, d_tokens = emit(big, small, output, d_tokens)
    grad_qkv = grad_qkv.reshape(3, local_cols, width).transpose(2, 0, 1)
    norms = lax.dynamic_slice_in_dim(norms, m * local_cols, local_cols, 1)
    return (
        output,
        d_tokens,
        grad_qkv,
        grad_out,
        grad_gate_up,
        grad_down,
        norms[0],
        norms[1],
        norms[2],
        norms[3],
    )


def solution(mesh):
    return jax.shard_map(
        body,
        mesh=mesh,
        in_specs=(
            P(("dp", "mp"), None),
            P("dp", None),
            P(None, None, "mp"),
            P("mp", None),
            P(None, None, "mp"),
            P("mp", None),
            P(),
            P(),
            P(),
            P(),
            P(("dp", "mp"), None),
        ),
        out_specs=(
            P(("dp", "mp"), None),
            P(("dp", "mp"), None),
            P(None, None, "mp"),
            P("mp", None),
            P(None, None, "mp"),
            P("mp", None),
            P("mp"),
            P("mp"),
            P("mp"),
            P("mp"),
        ),
        check_vma=False,
    )
```

```python
import functools
import math

import jax
import jax.numpy as jnp
from jax import lax
from jax.experimental import pallas as pl
from jax.experimental.pallas import tpu as pltpu
from jax.sharding import PartitionSpec as P

F32 = jnp.float32
BF16 = jnp.bfloat16
HEAD_DIM = 64
LANES = 128
EPSILON = 1e-05
FAR = -(2.0**100)
LOG2E = math.log2(math.e)
NT = (((1,), (1,)), ((), ()))
TN = (((0,), (0,)), ((), ()))
NN = (((1,), (0,)), ((), ()))
VMEM_LIMIT = 58 << 20
WIDE_LIMIT = 62 << 20
MESH = pl.DeviceIdType.MESH


def mm(a, b, dims=NN):
    return lax.dot_general(a, b, dims, preferred_element_type=F32)


def thirds(row):
    high = row.astype(BF16).astype(F32)
    mid = (row - high).astype(BF16).astype(F32)
    low = row - high - mid
    return jnp.concatenate([high, mid, low, jnp.zeros((13, row.shape[1]), F32)], axis=0)


def span(index, size):
    if isinstance(index, int):
        return pl.ds(index * size, size)
    return pl.ds(pl.multiple_of(index * size, size), size)


def dp_orders(size):
    bits = list(range(size.bit_length() - 1))
    return [bits, bits[1::-1] + bits[2:]]


def halvings(size):
    return min(3, size.bit_length() - 1)


def peer_of(index, bit):
    mine = (index // (1 << bit)) % 2
    return index + (1 - 2 * mine) * (1 << bit), mine


def send(source, target, send_sem, recv_sem, partner):
    copy = pltpu.make_async_remote_copy(
        source, target, send_sem, recv_sem, device_id=partner, device_id_type=MESH
    )
    copy.start()
    return copy


def greet(partners):
    barrier = pltpu.get_barrier_semaphore()
    for partner in partners:
        pl.semaphore_signal(barrier, inc=1, device_id=partner, device_id_type=MESH)
    pl.semaphore_wait(barrier, len(partners))


RING_PIECES = 8
RING_EARLY = 2


class Ring:
    def __init__(self, size, me, total, give, take, result, scatter_sems, gather_sems):
        self.n = n = min(RING_PIECES, size)
        self.me, self.size = me, size
        self.total, self.give, self.take, self.result = total, give, take, result
        self.scatter_sems, self.gather_sems = scatter_sems, gather_sems
        self.rows, self.cols = total.shape[1] // n, total.shape[2] // 2
        low = me % n
        across, along = low % 2, low // 2
        self.spot = (1 - across) * along + across * (n - 1 - along)
        self.peers = [self.index_at((self.spot + step) % n) for step in (1, n - 1)]

    def index_at(self, spot):
        across = spot // (self.n // 2)
        along = (1 - across) * spot + across * (self.n - 1 - spot)
        return self.me - self.me % self.n + 2 * along + across

    def piece(self, chain, step):
        shift = self.n * 4 - step if chain == 0 else step
        return pl.ds(pl.multiple_of((self.spot + shift) % self.n * self.rows, 16), self.rows)

    def half(self, sub):
        return span(sub, self.cols)

    def scatter(self, chain, sub, step):
        return pltpu.make_async_remote_copy(
            self.give.at[chain, sub],
            self.take.at[chain, sub, step],
            self.scatter_sems.at[0, chain, sub, step],
            self.scatter_sems.at[1, chain, sub, step],
            device_id={"dp": self.peers[chain]},
            device_id_type=MESH,
        )

    def gather(self, chain, sub, step):
        part = self.result.at[chain, self.piece(chain, step + self.n - 1), self.half(sub)]
        return pltpu.make_async_remote_copy(
            part,
            part,
            self.gather_sems.at[0, chain, sub, step],
            self.gather_sems.at[1, chain, sub, step],
            device_id={"dp": self.peers[chain]},
            device_id_type=MESH,
        )

    def begin(self, step, chain):
        for sub in range(2):
            self.give[chain, sub] = self.total[chain, self.piece(chain, step), self.half(sub)].astype(BF16)
            self.scatter(chain, sub, step).start()

    def arrived(self, step, chain, sub):
        self.scatter(chain, sub, step).wait()
        mine = self.total[chain, self.piece(chain, step + 1), self.half(sub)]
        return mine + self.take[chain, sub, step].astype(F32)

    def keep(self, step):
        for chain in range(2):
            for sub in range(2):
                value = self.arrived(step, chain, sub)
                self.total[chain, self.piece(chain, step + 1), self.half(sub)] = value

    def pass_on(self, step, sub):
        for chain in range(2):
            self.give[chain, sub] = self.arrived(step, chain, sub).astype(BF16)
            self.scatter(chain, sub, step + 1).start()

    def turn(self, step, sub):
        for chain in range(2):
            value = self.arrived(step, chain, sub).astype(BF16)
            self.give[chain, sub] = value
        for stage in range((self.size // self.n).bit_length() - 1):
            copies = []
            for chain in range(2):
                peer = self.me // self.n
                mine = (peer // (1 << stage)) % 2
                copies.append(
                    pltpu.make_async_remote_copy(
                        self.give.at[chain, sub],
                        self.take.at[chain, sub, self.n - 1 + stage],
                        self.scatter_sems.at[0, chain, sub, self.n - 1 + stage],
                        self.scatter_sems.at[1, chain, sub, self.n - 1 + stage],
                        device_id={"dp": self.me + (1 - 2 * mine) * (self.n << stage)},
                        device_id_type=MESH,
                    )
                )
                copies[-1].start()
            for chain in range(2):
                copies[chain].wait()
                value = self.give[chain, sub].astype(F32) + self.take[chain, sub, self.n - 1 + stage].astype(F32)
                self.give[chain, sub] = value.astype(BF16)
        for chain in range(2):
            self.result[chain, self.piece(chain, self.n - 1), self.half(sub)] = self.give[chain, sub]
            self.gather(chain, sub, 0).start()

    def event(self, number):
        step, sub, n = number // 2, number % 2, self.n

        @pl.when(step < n - 2)
        def _():
            self.pass_on(step, sub)

        @pl.when(step == n - 2)
        def _():
            self.turn(n - 2, sub)

        @pl.when(step >= n - 1)
        def _():
            for chain in range(2):
                self.gather(chain, sub, step - (n - 1)).wait()

            @pl.when(step < 2 * n - 3)
            def _():
                for chain in range(2):
                    self.gather(chain, sub, step - (n - 2)).start()


def ring_scratch(size, rows, cols, steps):
    piece = (rows // min(RING_PIECES, size), cols // 2)
    return [
        pltpu.VMEM((2, 2) + piece, BF16),
        pltpu.VMEM((2, 2, steps) + piece, BF16),
        pltpu.SemaphoreType.DMA((2, 2, 2, steps)),
    ]


X_FAR, X_NEAR, X_LAST, W_IN, W_DOWN, W_OUT, ATT_NEAR, ATT_LAST = range(8)
BRANCH, NORMED, OUT, DOUT, DNORMED, DH, DH_NEAR, DH_LAST, GRAD_NEAR = range(8, 17)
KINDS = 17


def first_kernel(
    size, lengths, tok_ref, cot_ref, ln_ref, w_ref, wo_ref, win_hbm, wdn_hbm,
    out_ref, dh_ref, slots_ref, norms_ref, total_hbm, x_hbm, q_hbm, k_hbm, v_hbm, q_rows_hbm, att_hbm, cos_hbm, sin_hbm,
    x_ref, win, wdn, wo_near_ref, att, near, outbox, inbox, low, hat, res, own, r1, dlow, give, take, sums,
    ring_give, ring_take, ring_sems, sems, loads, stores,
):
    rows, width = tok_ref.shape
    hidden = wdn.shape[0] // 2
    cols = wo_ref.shape[0]
    heads = cols // HEAD_DIM
    shards = x_ref.shape[0]
    tokens = shards * rows
    half = width // 2
    chunk = rows // 2
    chunks = [slice(c * chunk, (c + 1) * chunk) for c in range(2)]
    m, me = lax.axis_index("mp"), lax.axis_index("dp")
    core, far = {"mp": peer_of(m, 0)[0]}, {"mp": peer_of(m, 1)[0]}
    ring_peers = Ring(size, me, give, None, None, None, None, None).peers
    greet([core, far] + [{"dp": peer} for peer in ring_peers])

    def link(kind, c, source, target, partner):
        return pltpu.make_async_remote_copy(
            source, target, sems.at[0, kind, c], sems.at[1, kind, c], device_id=partner, device_id_type=MESH
        )

    def post(kind, c, source, target, partner):
        copy = link(kind, c, source, target, partner)
        copy.start()
        return copy

    far_copies = [post(X_FAR, c, tok_ref.at[where], x_ref.at[2, where], far) for c, where in enumerate(chunks)]
    near_copy = post(X_NEAR, 0, tok_ref, x_ref.at[1], core)
    weight_copies = [
        post(W_OUT, 0, wo_ref, wo_near_ref, core),
        post(W_DOWN, 0, wdn_hbm, wdn.at[pl.ds(hidden, hidden)], core),
    ]
    fetches = []
    for n, (source, target) in enumerate([(wdn_hbm, wdn.at[pl.ds(0, hidden)])]):
        fetches.append(pltpu.make_async_copy(source, target, loads.at[n]))
        fetches[-1].start()
    x_ref[0] = tok_ref[...]
    sums[...] = jnp.zeros_like(sums)
    scale_one, shift_one, scale_two, shift_two = (ln_ref[i : i + 1, :] for i in range(4))

    def branch(slot, other, where):
        return mm(att[slot, :, where], wo_ref[...], TN) + mm(near[other, :, where], wo_near_ref[...], TN)

    def by_parts(c, part):
        step = 64

        def run(i, carry):
            part(pl.ds(pl.multiple_of(c * chunk + i * step, step), step))
            return carry

        lax.fori_loop(0, chunk // step, run, 0)

    def mean(values):
        return jnp.sum(values, axis=-1, keepdims=True) * (1.0 / width)

    def add_up(index, values):
        sums[index] += jnp.sum(values.reshape(values.shape[0] // 8, 8, width), axis=0)

    def norm_one(where):
        h = hat[where, :] + inbox[where, :].astype(F32)
        h = h - mean(h)
        r = lax.rsqrt(mean(h * h) + EPSILON)
        h = h * r
        hat[where, :] = h
        r1[where, :] = jnp.broadcast_to(r, (r.shape[0], LANES))
        h = h * scale_one + shift_one
        res[where, :] = h
        low[0, where, :] = h.astype(BF16)

    def attention(raw, q_ref, k_ref, v_ref, k_rows_ref, q_rows_ref, cos_ref, sin_ref, top_ref, acc_ref):
        fetch = pltpu.make_async_copy(win_hbm, raw, loads.at[1])
        fetch.start()
        half_head = HEAD_DIM // 2
        starts, ends, end = [], [], 0
        for d in range(lengths.shape[1]):
            starts.append(end)
            end = end + lengths[0, d]
            ends.append(end)
        doc = lax.broadcasted_iota(jnp.int32, (16, rows), 0)
        first, last = jnp.zeros((16, rows), jnp.int32), jnp.zeros((16, rows), jnp.int32)
        for d in range(lengths.shape[1]):
            first, last = jnp.where(doc == d, starts[d], first), jnp.where(doc == d, ends[d], last)
        exponent = lax.broadcasted_iota(jnp.int32, (half_head, rows), 0).astype(F32)
        rate = jnp.exp(exponent * (-2.0 * math.log(1000.0) / HEAD_DIM))
        row = lax.broadcasted_iota(jnp.int32, (48, rows), 0)
        ones = jnp.where(row < 3, 1.0, 0.0)
        v_tail = jnp.concatenate([ones, jnp.zeros((16, rows), F32)], axis=0)
        top_ref[...] = jnp.full_like(top_ref, FAR)
        acc_ref[...] = jnp.zeros_like(acc_ref)

        def tables(slot, carry):
            where = span(slot, rows)
            shard = 2 * ((slot // 2 + m // 2) % 2) + (slot + m) % 2
            token = lax.broadcasted_iota(jnp.int32, (16, rows), 1) + shard * rows
            inside = (token >= first) & (token < last)
            begin = jnp.max(jnp.where(inside, first, 0), axis=0, keepdims=True)
            angles = rate * (token[0:1] - begin).astype(F32)
            cos_ref[:, where], sin_ref[:, where] = jnp.cos(angles), jnp.sin(angles)
            for h in range(heads):
                q_ref[h, HEAD_DIM:, where] = jnp.concatenate(
                    [jnp.where(inside, 0.0, FAR), jnp.zeros((48, rows), F32)], axis=0
                ).astype(BF16)
                k_ref[h, HEAD_DIM:, where] = jnp.concatenate([jnp.where(inside, 1.0, 0.0), ones], axis=0).astype(BF16)
                v_ref[h, HEAD_DIM:, where] = v_tail.astype(BF16)
            return carry

        def project(part, carry):
            where = span(part, chunk)
            projected = mm(w_ref[...], x_ref[part // 2, span(part % 2, chunk), :], NT)
            cosine, sine = cos_ref[:, where], sin_ref[:, where]

            def rotated(start, scale):
                one, two = projected[start : start + half_head], projected[start + half_head : start + HEAD_DIM]
                turned = jnp.concatenate([one * cosine - two * sine, two * cosine + one * sine], axis=0)
                return turned * scale

            for h in range(heads):
                q_ref[h, :HEAD_DIM, where] = rotated(h * HEAD_DIM, LOG2E / math.sqrt(HEAD_DIM)).astype(BF16)
                k = rotated(cols + h * HEAD_DIM, 1.0)
                k_ref[h, :HEAD_DIM, where] = k.astype(BF16)
                tail = k_ref[h, HEAD_DIM:, where].astype(F32)
                k_rows_ref[h, where, :] = jnp.concatenate([k, tail], axis=0).T.astype(BF16)
                start = 2 * cols + h * HEAD_DIM
                v_ref[h, :HEAD_DIM, where] = projected[start : start + HEAD_DIM].astype(BF16)
            return carry

        def pairs(count, pair):
            def run(n, carry):
                qs, group = pair(n)
                queries, keys = span(qs, chunk), span(group, 2 * rows)
                scores, olds, tops = [], [], []
                for h in range(heads):
                    s = mm(k_rows_ref[h, keys, :], q_ref[h, :, queries])
                    olds.append(top_ref[qs, h, 0:1, :])
                    tops.append(jnp.maximum(olds[h], jnp.max(s, axis=0, keepdims=True)))
                    scores.append(s)
                for h in range(heads):
                    probs = jnp.exp2(scores[h] - tops[h]).astype(BF16)
                    top_ref[qs, h, 0:1, :] = tops[h]
                    acc_ref[qs, h] = acc_ref[qs, h] * jnp.exp2(olds[h] - tops[h]) + mm(v_ref[h, :80, keys], probs)
                return carry

            lax.fori_loop(0, count, run, 0)

        writes = []

        def write(source, target):
            writes.append(pltpu.make_async_copy(source, target, stores.at[len(writes)]))
            writes[-1].start()

        def settle(slot, c):
            part = 2 * slot + c
            for h in range(heads):
                total = acc_ref[part, h, HEAD_DIM : HEAD_DIM + 1, :]
                out = acc_ref[part, h, :HEAD_DIM, :] / total
                att[slot, h * HEAD_DIM : (h + 1) * HEAD_DIM, chunks[c]] = out.astype(BF16)
                top_ref[part, h, 1:2, :] = top_ref[part, h, 0:1, :] + jnp.log2(total)

        def turn(part, carry):
            where = span(part, chunk)
            for h in range(heads):
                query = q_ref[h, :, where].astype(F32)
                wide = jnp.concatenate([query[:80], thirds(-top_ref[part, h, 1:2, :]), query[96:]], axis=0)
                q_rows_ref[h, where, :] = wide.T.astype(BF16)
            return carry

        lax.fori_loop(0, shards, tables, 0)
        fetch.wait()

        def untangle(i, carry):
            where = span(i, 32)
            for n in range(2):
                win[0, where, n * hidden : (n + 1) * hidden] = raw[where, n, :]
            return carry

        lax.fori_loop(0, width // 32, untangle, 0)
        post(W_IN, 0, win.at[0], win.at[1], core)
        last_copies = []

        def hand_on(c):
            far_copies[c].wait()
            last_copies.append(post(X_LAST, c, x_ref.at[2, chunks[c]], x_ref.at[3, chunks[c]], core))

        near_copy.wait()
        lax.fori_loop(0, 4, project, 0)
        hand_on(0)
        pairs(4, lambda n: (n, 0))
        last_copies[0].wait()
        lax.fori_loop(0, 2, lambda n, carry: project(4 + 2 * n, carry), 0)
        hand_on(1)
        project(5, 0)
        last_copies[1].wait()
        project(7, 0)
        for source, target in [
            (x_ref, x_hbm), (q_ref, q_hbm), (k_ref, k_hbm), (v_ref, v_hbm), (cos_ref, cos_hbm), (sin_ref, sin_hbm)
        ]:
            write(source, target)
        weight_copies[0].wait()
        branch_copies = []
        for c, where in enumerate(chunks):
            pairs(2, lambda n: (6 + c, n))
            settle(3, c)
            last_att = post(ATT_LAST, c, att.at[3, :, where], near.at[1, :, where], core)
            pairs(2, lambda n: (4 + c, n))
            settle(2, c)
            last_att.wait()
            outbox[where, :] = branch(2, 1, where).astype(BF16)
            branch_copies.append(post(BRANCH, c, outbox.at[where], inbox.at[where], far))
        pairs(4, lambda n: (3 - n, 1))
        for c in range(2):
            settle(1, c)
        near_att = post(ATT_NEAR, 0, att.at[1], near.at[0], core)
        for c in range(2):
            settle(0, c)
        write(att, att_hbm)
        near_att.wait()
        for where in chunks:
            hat[where, :] = tok_ref[where, :].astype(F32) + branch(0, 0, where)
        for c, where in enumerate(chunks):
            branch_copies[c].wait()
            by_parts(c, norm_one)
            post(NORMED, c, low.at[0, where], low.at[1, where], far)
        lax.fori_loop(0, 2 * shards, turn, 0)
        write(q_rows_ref, q_rows_hbm)
        for copy in writes:
            copy.wait()

    along = pltpu.VMEM((heads, LANES, tokens), BF16)
    down = pltpu.VMEM((heads, tokens, LANES), BF16)
    table = pltpu.VMEM((HEAD_DIM // 2, tokens), F32)
    pl.run_scoped(
        attention, pltpu.VMEM((width, 2, hidden), BF16), along, along, along, down, down, table, table,
        pltpu.VMEM((2 * shards, heads, 8, chunk), F32), pltpu.VMEM((2 * shards, heads, 80, chunk), F32),
    )
    normed_copies = [link(NORMED, c, low.at[0, where], low.at[1, where], far) for c, where in enumerate(chunks)]
    for copy in fetches + weight_copies[1:] + [link(W_IN, 0, win.at[0], win.at[1], core)]:
        copy.wait()

    def feed_forward(gu, hid, total):
        ring = Ring(size, me, total, ring_give, ring_take, None, ring_sems, None)
        tile = hidden // 2

        def mlp(side, where):
            def columns(t, carry):
                k, at = t // 2, (t % 2) * tile
                x = low[side, where, :]
                gate_at = pl.ds(pl.multiple_of(at, LANES), tile)
                up_at = pl.ds(pl.multiple_of(hidden + at, LANES), tile)
                gate, up = mm(x, win[k, :, gate_at]), mm(x, win[k, :, up_at])
                gu[side, k, where, gate_at] = gate.astype(BF16)
                gu[side, k, where, up_at] = up.astype(BF16)
                value = gate * jax.nn.sigmoid(gate) * up
                hid[side, where, pl.ds(pl.multiple_of(k * hidden + at, LANES), tile)] = value.astype(BF16)
                return carry

            lax.fori_loop(0, 4, columns, 0)
            return mm(hid[side, where, :], wdn[...])

        def both_sides(copies_in, kind, compute):
            copies = []
            for c, where in enumerate(chunks):
                own[where, :] = compute(0, where)
                copies_in[c].wait()
                outbox[where, :] = compute(1, where).astype(BF16)
                copies.append(post(kind, c, outbox.at[where], inbox.at[where], far))
            return copies

        out_copies = both_sides(normed_copies, OUT, mlp)

        def norm_two(where):
            z = res[where, :] + own[where, :] + inbox[where, :].astype(F32)
            z = z - mean(z)
            r = lax.rsqrt(mean(z * z) + EPSILON)
            z = z * r
            out_ref[where, :] = (z * scale_two + shift_two).astype(BF16)
            g = cot_ref[where, :].astype(F32)
            add_up(2, g * z)
            add_up(3, g)
            e = g * scale_two
            dz = r * (e - mean(e) - z * mean(e * z))
            res[where, :] = dz
            dlow[0, where, :] = dz.astype(BF16)

        dout_copies = []
        for c, where in enumerate(chunks):
            out_copies[c].wait()
            by_parts(c, norm_two)
            dout_copies.append(post(DOUT, c, dlow.at[0, where], dlow.at[1, where], far))

        def mlp_back(side, where):
            def columns(t, carry):
                k, at = t // 2, (t % 2) * tile
                d_hidden = mm(
                    dlow[side, where, :], wdn[pl.ds(pl.multiple_of(k * hidden + at, LANES), tile), :], NT
                )
                gate_at = pl.ds(pl.multiple_of(at, LANES), tile)
                up_at = pl.ds(pl.multiple_of(hidden + at, LANES), tile)
                gate, up = gu[side, k, where, gate_at].astype(F32), gu[side, k, where, up_at].astype(F32)
                s = jax.nn.sigmoid(gate)
                gu[side, k, where, gate_at] = (d_hidden * up * s * (1.0 + gate * (1.0 - s))).astype(BF16)
                gu[side, k, where, up_at] = (d_hidden * gate * s).astype(BF16)
                return carry

            lax.fori_loop(0, 4, columns, 0)
            return mm(gu[side, 0, where, :], win[0], NT) + mm(gu[side, 1, where, :], win[1], NT)

        dnormed_copies = both_sides(dout_copies, DNORMED, mlp_back)

        def weight_grads(k, target, then=lambda r: None):
            def chain(r, carry):
                at = pl.ds(pl.multiple_of(r * half, LANES), half)
                for n, place in enumerate((slice(0, hidden), slice(hidden, 2 * hidden))):
                    piece = mm(low[0, :, at], gu[0, k, :, place], TN) + mm(low[1, :, at], gu[1, k, :, place], TN)
                    target[r, n * half : (n + 1) * half, :] = piece.astype(target.dtype)
                at = pl.ds(pl.multiple_of(k * hidden + r * half, LANES), half)
                piece = mm(hid[0, :, at], dlow[0], TN) + mm(hid[1, :, at], dlow[1], TN)
                target[r, 2 * half : 3 * half, :] = piece.astype(target.dtype)
                then(r)
                return carry

            lax.fori_loop(0, 2, chain, 0)

        def grad_copy(r):
            return link(GRAD_NEAR, r, give.at[r], take.at[r], core)

        weight_grads(1, give, lambda r: grad_copy(r).start())

        def norm_one_back(where):
            d = res[where, :] + own[where, :] + inbox[where, :].astype(F32)
            h = hat[where, :]
            add_up(0, d * h)
            add_up(1, d)
            e = d * scale_one
            dh = r1[where, 0:1] * (e - mean(e) - h * mean(e * h))
            dh_ref[where, :] = dh
            slots_ref[0, where, :] = dh.astype(BF16)

        dh_copies, last_copies = [], []

        def dh_chunk(c):
            where = chunks[c]
            dnormed_copies[c].wait()
            by_parts(c, norm_one_back)
            mine = slots_ref.at[0, where]
            dh_copies.append(post(DH, c, mine, slots_ref.at[2, where], far))
            last_copies.append(post(DH_NEAR, c, mine, slots_ref.at[1, where], core))

        dh_chunk(0)
        weight_grads(0, total)
        dh_chunk(1)
        for r in range(2):
            grad_copy(r).wait()
            total[r] += take[r].astype(F32)
            ring.begin(0, r)

        def hand_on(c):
            dh_copies[c].wait()
            where = chunks[c]
            last_copies.append(post(DH_LAST, c, slots_ref.at[2, where], slots_ref.at[3, where], core))

        for i in range(4):
            norms_ref[i : i + 1, :] = jnp.sum(sums[i], axis=0, keepdims=True)
        norms_ref[4:8, :] = jnp.zeros((4, width), F32)
        for step in range(RING_EARLY - 1):
            for sub in range(2):
                ring.pass_on(step, sub)
            if step < 2:
                hand_on(step)
        for step in range(RING_EARLY - 1, 2):
            hand_on(step)
        ring.keep(RING_EARLY - 1)
        write = pltpu.make_async_copy(total, total_hbm, loads.at[0])
        write.start()
        for copy in last_copies:
            copy.wait()
        write.wait()

    pl.run_scoped(
        feed_forward,
        pltpu.VMEM((2, 2, rows, 2 * hidden), BF16),
        pltpu.VMEM((2, rows, 2 * hidden), BF16),
        pltpu.VMEM((2, 3 * half, width), F32),
    )


def first(lengths, tokens, cotangent, norms, w_turned, w_out, w_in, w_down):
    size, shards = lax.axis_size("dp"), lax.axis_size("mp")
    rows, width = tokens.shape
    cols, hidden = w_out.shape[0], w_down.shape[0]
    heads, length = cols // HEAD_DIM, rows * shards
    chain = 3 * width // 2
    vmem = pl.BlockSpec(memory_space=pltpu.VMEM)
    hbm = pl.BlockSpec(memory_space=pl.ANY)
    dma = pltpu.SemaphoreType.DMA
    shape = jax.ShapeDtypeStruct
    along, table = shape((heads, LANES, length), BF16), shape((HEAD_DIM // 2, length), F32)
    wide = lambda dtype, *lead: pltpu.VMEM(lead + (rows, width), dtype)
    return pl.pallas_call(
        functools.partial(first_kernel, size),
        out_shape=(
            shape((rows, width), BF16),
            shape((rows, width), F32),
            shape((shards, rows, width), BF16),
            shape((8, width), F32),
            shape((2, chain, width), F32),
            shape((shards, rows, width), BF16),
            along,
            along,
            along,
            shape((heads, length, LANES), BF16),
            shape((shards, cols, rows), BF16),
            table,
            table,
        ),
        in_specs=[pl.BlockSpec(memory_space=pltpu.SMEM)] + [vmem] * 5 + [hbm] * 2,
        out_specs=[vmem] * 4 + [hbm] * 9,
        scratch_shapes=[
            wide(BF16, shards),
            pltpu.VMEM((2, width, 2 * hidden), BF16),
            pltpu.VMEM((2 * hidden, width), BF16),
            pltpu.VMEM((cols, width), BF16),
            pltpu.VMEM((shards, cols, rows), BF16),
            pltpu.VMEM((2, cols, rows), BF16),
            wide(BF16),
            wide(BF16),
            wide(BF16, 2),
            wide(F32),
            wide(F32),
            wide(F32),
            pltpu.VMEM((rows, LANES), F32),
            wide(BF16, 2),
            pltpu.VMEM((2, chain, width), BF16),
            pltpu.VMEM((2, chain, width), BF16),
            pltpu.VMEM((4, 8, width), F32),
            *ring_scratch(size, chain, width, RING_EARLY),
            dma((2, KINDS, 2)),
            dma((2,)),
            dma((8,)),
        ],
        compiler_params=pltpu.CompilerParams(
            collective_id=0, has_side_effects=True, vmem_limit_bytes=WIDE_LIMIT
        ),
        cost_estimate=pl.CostEstimate(
            flops=36 * rows * width * hidden, bytes_accessed=40 * rows * width, transcendentals=0
        ),
        name="first",
    )(lengths, tokens, cotangent, norms, w_turned, w_out, w_in, w_down)


class Sum:
    def __init__(self, size, me, first, total, give, take, result, sems):
        orders = dp_orders(size)
        self.total, self.give, self.take, self.result, self.sems = total, give, take, result, sems
        halving, stages = halvings(size), size.bit_length() - 1
        count = 1 << (halving - first)
        self.rows = total.shape[1] // count
        base, low, peers = [], [0, 0], []
        for chain in range(2):
            peers.append([peer_of(me, bit) for bit in orders[chain]])
            base.append(sum(peers[chain][done][1] * (1 << (halving - 1 - done)) for done in range(first)))
        self.steps, spot = [], 0
        for stage in range(first, stages):
            halve = stage < halving
            part = count // 2 if halve else count
            step = dict(kind="halve" if halve else "swap", part=part, spot=spot, chains=[], last=stage + 1 == stages)
            for chain in range(2):
                peer, mine = peers[chain][stage]
                away = low[chain] + (1 - mine) * part if halve else low[chain]
                low[chain] = low[chain] + mine * part if halve else low[chain]
                step["chains"].append(dict(peer=peer, away=away, keep=low[chain], final=base[chain] + low[chain]))
            self.steps.append(step)
            spot, count = spot + part, part
        low = [base[chain] + low[chain] for chain in range(2)]
        for stage in reversed(range(halving)):
            step = dict(kind="gather", part=count, chains=[])
            for chain in range(2):
                peer, mine = peers[chain][stage]
                step["chains"].append(dict(peer=peer, away=low[chain]))
                low[chain] = low[chain] - mine * count
            self.steps.append(step)
            count *= 2

    def block(self, low, count):
        return pl.ds(pl.multiple_of(low * self.rows, 16), count * self.rows)

    def copy(self, index, chain):
        step = self.steps[index]
        one = step["chains"][chain]
        if step["kind"] == "gather":
            source = target = self.result.at[chain, self.block(one["away"], step["part"])]
        else:
            spot = pl.ds(step["spot"] * self.rows, step["part"] * self.rows)
            source, target = self.give.at[chain, spot], self.take.at[chain, spot]
        return pltpu.make_async_remote_copy(
            source,
            target,
            self.sems.at[0, chain, index],
            self.sems.at[1, chain, index],
            device_id={"dp": one["peer"]},
            device_id_type=MESH,
        )

    def start(self, index, chains=(0, 1)):
        step = self.steps[index]
        for chain in chains:
            if step["kind"] != "gather":
                spot = pl.ds(step["spot"] * self.rows, step["part"] * self.rows)
                away = self.block(step["chains"][chain]["away"], step["part"])
                self.give[chain, spot, :] = self.total[chain, away, :].astype(BF16)
            self.copy(index, chain).start()

    def finish(self, index):
        step = self.steps[index]
        for chain in range(2):
            self.copy(index, chain).wait()
            if step["kind"] == "gather":
                continue
            one = step["chains"][chain]
            spot = pl.ds(step["spot"] * self.rows, step["part"] * self.rows)
            keep = self.block(one["keep"], step["part"])
            mine = self.total[chain, keep, :] if step["kind"] == "halve" else self.give[chain, spot, :].astype(F32)
            value = mine + self.take[chain, spot, :].astype(F32)
            if step["last"]:
                self.result[chain, self.block(one["final"], 1), :] = value.astype(BF16)
            else:
                self.total[chain, keep, :] = value

    def advance(self, index):
        self.finish(index)
        if index + 1 < len(self.steps):
            self.start(index + 1)


def pieces_sent(size, first):
    halving = halvings(size)
    return (1 << (halving - first)) - 1 + size.bit_length() - 1 - halving


def back_kernel(
    size, att_ref, w_out_ref, cos_ref, sin_ref, norms_ref, w_ref, w_near_ref, dh_ref,
    total_hbm, slots_hbm, q_rows_hbm, q_hbm, k_hbm, v_hbm, x_hbm,
    dx_ref, grad_ref, big_ref, sums_ref,
    big, slots, q_rows_ref, q_ref, k_ref, v_ref, x_ref,
    do_ref, do_rows_ref, dq_ref, dk_ref, dv_ref, d_qkv,
    total, give, take, near, far_out, far_in, own, norm_in,
    ring_give, ring_take, ring_sems, gather_sems, loads, near_sem, far_sem, sum_sems, norm_sem,
):
    heads, _, tokens = k_ref.shape
    shards, rows, width = slots.shape
    cols = heads * HEAD_DIM
    half = HEAD_DIM // 2
    m, me = lax.axis_index("mp"), lax.axis_index("dp")
    stages = size.bit_length() - 1
    core, far = {"mp": peer_of(m, 0)[0]}, {"mp": peer_of(m, 1)[0]}
    partners = [core, far] + [{"dp": peer_of(me, bit)[0]} for bit in range(stages)]
    sources = [total_hbm, slots_hbm, q_rows_hbm, q_hbm, k_hbm, v_hbm, x_hbm]
    targets = [big, slots, q_rows_ref, q_ref, k_ref, v_ref, x_ref]
    fetches = [
        pltpu.make_async_copy(source, target, loads.at[n])
        for n, (source, target) in enumerate(zip(sources, targets))
    ]
    for fetch in fetches:
        fetch.start()
    ring = Ring(size, me, big, ring_give, ring_take, big_ref, ring_sems, gather_sems)
    greet(partners + [{"dp": peer} for peer in ring.peers])
    sums_ref[...] = norms_ref[...]
    small = Sum(size, me, 0, total, give, take, grad_ref, sum_sems)
    fetches[0].wait()
    for chain in range(2):
        ring.begin(RING_EARLY, chain)
    fetches[1].wait()
    events = 2 * (2 * ring.n - 2)
    first_event = 2 * RING_EARLY

    def prepare(i, carry):
        d_att = mm(w_out_ref[...], slots[i], NT).astype(BF16)
        do_ref[:, span(i, rows)] = d_att
        products = d_att.astype(F32) * att_ref[i].astype(F32)
        for h in range(heads):
            mine = slice(h * HEAD_DIM, (h + 1) * HEAD_DIM)
            dot = jnp.sum(products[mine], axis=0, keepdims=True)
            wide = [d_att[mine].astype(F32), thirds(-dot), jnp.zeros((LANES - HEAD_DIM - 16, rows), F32)]
            do_rows_ref[h, span(i, rows), :] = jnp.concatenate(wide, axis=0).T.astype(BF16)
        return carry

    lax.fori_loop(0, shards, prepare, 0)
    dq_ref[...] = jnp.zeros_like(dq_ref)
    for fetch in fetches[2:]:
        fetch.wait()

    def rotated_back(values, cosine, sine):
        first, second = values[:half], values[half:]
        return [first * cosine + second * sine, second * cosine - first * sine]

    def over_keys(j, carry):
        keys = span(j, rows)
        dk_ref[...] = jnp.zeros_like(dk_ref)
        dv_ref[...] = jnp.zeros_like(dv_ref)

        def over_queries(i, carry):
            queries = span(i, rows)
            for h in range(heads):
                k = k_ref[h, :, keys]
                probs = jnp.exp2(mm(q_rows_ref[h, queries, :], k))
                d_scores = (probs * mm(do_rows_ref[h, queries, :], v_ref[h, :, keys])).astype(BF16)
                dv_ref[h] += mm(do_ref[h * HEAD_DIM : (h + 1) * HEAD_DIM, queries], probs.astype(BF16))
                dk_ref[h] += mm(q_ref[h, :HEAD_DIM, queries], d_scores)
                dq_ref[h, :, queries] += mm(k[:HEAD_DIM], d_scores, NT)
            number = first_event + j * shards + i
            pl.when(number < events)(lambda: ring.event(number))
            return carry

        lax.fori_loop(0, shards, over_queries, 0)
        cosine, sine = cos_ref[:, keys] * (1.0 / LOG2E), sin_ref[:, keys] * (1.0 / LOG2E)
        pieces = []
        for h in range(heads):
            pieces += rotated_back(dk_ref[h], cosine, sine)
        pieces += [dv_ref[h] for h in range(heads)]
        d_qkv[j, cols:, :] = jnp.concatenate(pieces, axis=0).astype(BF16)
        return carry

    lax.fori_loop(0, shards, over_keys, 0)
    first_event = min(first_event + shards * shards, events)
    for i in range(shards):
        scale = 1.0 / math.sqrt(HEAD_DIM)
        cosine, sine = cos_ref[:, span(i, rows)] * scale, sin_ref[:, span(i, rows)] * scale
        pieces = []
        for h in range(heads):
            pieces += rotated_back(dq_ref[h, :, span(i, rows)], cosine, sine)
        d_qkv[i, :cols, :] = jnp.concatenate(pieces, axis=0).astype(BF16)
    near_copies = [send(d_qkv.at[2 * i + 1], near.at[i], near_sem.at[0, i], near_sem.at[1, i], core) for i in range(2)]

    def product(first, count):
        piece = mm(d_qkv[0, first : first + count, :], x_ref[0])
        for slot in range(1, shards):
            piece += mm(d_qkv[slot, first : first + count, :], x_ref[slot])
        return piece

    chain_rows = total.shape[1]
    total[0] = product(0, chain_rows)
    total[1, :cols, :] = product(chain_rows, cols)
    piece = mm(att_ref[0], slots[0])
    for slot in range(1, shards):
        piece += mm(att_ref[slot], slots[slot])
    total[1, cols:, :] = piece
    small.start(0)

    def norm_exchange(stage):
        return send(sums_ref, norm_in.at[stage], norm_sem.at[0, stage], norm_sem.at[1, stage], partners[stage])

    norm_copy, norm_done = norm_exchange(0), 0
    for copy in near_copies:
        copy.wait()

    def d_tokens(index):
        return mm(d_qkv[2 * index], w_ref[...], TN) + mm(near[index], w_near_ref[...], TN)

    far_out[...] = d_tokens(1).astype(BF16)
    far_copy = send(far_out, far_in, far_sem.at[0], far_sem.at[1], far)
    own[...] = dh_ref[...] + d_tokens(0)

    left, share = first_event, -(-(events - first_event) // len(small.steps))
    small_done = 0
    while small_done < len(small.steps) or norm_done < len(partners):
        if small_done < len(small.steps):
            small.advance(small_done)
            small_done += 1
            for number in range(left, min(left + share, events)):
                ring.event(number)
            left = min(left + share, events)
        if norm_done < len(partners):
            norm_copy.wait()
            sums_ref[...] += norm_in[norm_done]
            norm_done += 1
            if norm_done < len(partners):
                norm_copy = norm_exchange(norm_done)
    far_copy.wait()
    dx_ref[...] = (own[...] + far_in[...].astype(F32)).astype(BF16)


def back(att, w_out, cosine, sine, norms, w_turned, w_near, dh, totals, dh_slots, q_rows, q, k, v, x_slots):
    size = lax.axis_size("dp")
    stages = size.bit_length() - 1
    heads, _, tokens = q.shape
    shards, rows, width = x_slots.shape
    cols = w_turned.shape[0]
    chain, big_chain = width // 2, totals.shape[1]
    sent = pieces_sent(size, 0) * (chain >> halvings(size))
    spots = min(RING_PIECES, size)
    ring_steps = spots - 1 + (size // spots).bit_length() - 1
    steps = stages + halvings(size)
    vmem = pl.BlockSpec(memory_space=pltpu.VMEM)
    hbm = pl.BlockSpec(memory_space=pl.ANY)
    dma = pltpu.SemaphoreType.DMA
    along = pltpu.VMEM((heads, LANES, tokens), BF16)
    return pl.pallas_call(
        functools.partial(back_kernel, size),
        out_shape=(
            jax.ShapeDtypeStruct((rows, width), BF16),
            jax.ShapeDtypeStruct((2, chain, width), BF16),
            jax.ShapeDtypeStruct((2, big_chain, width), BF16),
            jax.ShapeDtypeStruct(norms.shape, F32),
        ),
        in_specs=[vmem] * 8 + [hbm] * 7,
        out_specs=[vmem] * 4,
        scratch_shapes=[
            pltpu.VMEM(totals.shape, F32),
            pltpu.VMEM(dh_slots.shape, BF16),
            pltpu.VMEM((heads, tokens, LANES), BF16),
            along,
            along,
            along,
            pltpu.VMEM(x_slots.shape, BF16),
            pltpu.VMEM((heads * HEAD_DIM, tokens), BF16),
            pltpu.VMEM((heads, tokens, LANES), BF16),
            pltpu.VMEM((heads, HEAD_DIM, tokens), F32),
            pltpu.VMEM((heads, HEAD_DIM, rows), F32),
            pltpu.VMEM((heads, HEAD_DIM, rows), F32),
            pltpu.VMEM((shards, cols, rows), BF16),
            pltpu.VMEM((2, chain, width), F32),
            pltpu.VMEM((2, sent, width), BF16),
            pltpu.VMEM((2, sent, width), BF16),
            pltpu.VMEM((2, cols, rows), BF16),
            pltpu.VMEM((rows, width), BF16),
            pltpu.VMEM((rows, width), BF16),
            pltpu.VMEM((rows, width), F32),
            pltpu.VMEM((2 + stages,) + norms.shape, F32),
            *ring_scratch(size, big_chain, width, ring_steps),
            dma((2, 2, 2, spots - 1)),
            dma((7,)),
            dma((2, 2)),
            dma((2,)),
            dma((2, 2, steps)),
            dma((2, 2 + stages)),
        ],
        compiler_params=pltpu.CompilerParams(
            collective_id=1, has_side_effects=True, vmem_limit_bytes=WIDE_LIMIT
        ),
        cost_estimate=pl.CostEstimate(
            flops=5 * heads * tokens * tokens * LANES, bytes_accessed=60 * rows * width, transcendentals=0
        ),
        name="back",
    )(att, w_out, cosine, sine, norms, w_turned, w_near, dh, totals, dh_slots, q_rows, q, k, v, x_slots)


def emit_kernel(big_ref, small_ref, out_ref, dx_ref, gate_up_hbm, down_ref, qkv_ref, w_out_ref, out_copy_ref, dx_copy_ref, wide, sems):
    step, steps = pl.program_id(0), pl.num_programs(0)
    rows = down_ref.shape[0]

    def copies(which):
        return [
            pltpu.make_async_copy(wide.at[which, n], gate_up_hbm.at[span(which, rows), n, :], sems.at[which, n])
            for n in range(2)
        ]

    for n in range(2):
        wide[step, n] = big_ref[0, n].astype(F32)
    for copy in copies(step):
        copy.start()
    down_ref[...] = big_ref[0, 2].astype(F32)
    out_copy_ref[...] = out_ref[...]
    dx_copy_ref[...] = dx_ref[...]
    qkv_steps = steps * 3 // 4

    @pl.when(step < qkv_steps)
    def _():
        qkv_ref[...] = small_ref[0].astype(F32)

    @pl.when(step >= qkv_steps)
    def _():
        w_out_ref[...] = small_ref[0].astype(F32)

    @pl.when(step == steps - 1)
    def _():
        for which in range(steps):
            for copy in copies(which):
                copy.wait()


def emit(big, small, output, d_tokens):
    _, chain, width = small.shape
    steps = 8
    per, rows = steps // 2, width // steps
    qkv_steps = steps * 3 // 4
    tokens = output.shape[0] // steps
    shape = lambda *dims: jax.ShapeDtypeStruct(dims, F32)
    low = jax.ShapeDtypeStruct(output.shape, BF16)
    few = pl.BlockSpec((tokens, width), lambda i: (i, 0))
    return pl.pallas_call(
        emit_kernel,
        out_shape=(
            shape(width, 2, width),
            shape(width, width),
            shape(qkv_steps * rows, width),
            shape((steps - qkv_steps) * rows, width),
            low,
            low,
        ),
        grid=(steps,),
        in_specs=[
            pl.BlockSpec((1, 3, rows, width), lambda i: (i // per, 0, i % per, 0)),
            pl.BlockSpec((1, rows, width), lambda i: (i // per, i % per, 0)),
            few,
            few,
        ],
        out_specs=[
            pl.BlockSpec(memory_space=pl.ANY),
            pl.BlockSpec((rows, width), lambda i: (i, 0)),
            pl.BlockSpec((rows, width), lambda i: (jnp.minimum(i, qkv_steps - 1), 0)),
            pl.BlockSpec((rows, width), lambda i: (jnp.maximum(i - qkv_steps, 0), 0)),
            few,
            few,
        ],
        scratch_shapes=[pltpu.VMEM((steps, 2, rows, width), F32), pltpu.SemaphoreType.DMA((steps, 2))],
        compiler_params=pltpu.CompilerParams(vmem_limit_bytes=VMEM_LIMIT),
        cost_estimate=pl.CostEstimate(flops=0, bytes_accessed=24 * width * width, transcendentals=0),
        name="emit",
    )(big.reshape(2, 3, chain, width), small, output, d_tokens)


def body(
    tokens, lengths, w_qkv, w_out, w_gate_up, w_down, ln1_scale, ln1_shift, ln2_scale, ln2_shift, cotangent
):
    rows, width = tokens.shape
    shards = lax.axis_size("mp")
    local_cols = w_out.shape[0]
    hidden_cols = w_down.shape[0]
    m = lax.axis_index("mp")
    qkv_turned = w_qkv.transpose(1, 2, 0).reshape(3 * local_cols, width)
    qkv_near = lax.ppermute(qkv_turned, "mp", [(i, i ^ 1) for i in range(shards)])
    norms = jnp.concatenate([jnp.stack([ln1_scale, ln1_shift, ln2_scale, ln2_shift]), jnp.zeros((4, width), F32)])
    output, dh, dh_slots, norms, totals, x_slots, q, k, v, q_rows, att, cosine, sine = first(
        lengths, tokens, cotangent, norms, qkv_turned, w_out, w_gate_up, w_down
    )
    d_tokens, small, big, norms = back(
        att, w_out, cosine, sine, norms, qkv_turned, qkv_near, dh, totals, dh_slots, q_rows, q, k, v, x_slots
    )
    grad_gate_up, grad_down, grad_qkv, grad_out, output, d_tokens = emit(big, small, output, d_tokens)
    grad_qkv = grad_qkv.reshape(3, local_cols, width).transpose(2, 0, 1)
    norms = lax.dynamic_slice_in_dim(norms, m * local_cols, local_cols, 1)
    return (
        output,
        d_tokens,
        grad_qkv,
        grad_out,
        grad_gate_up,
        grad_down,
        norms[0],
        norms[1],
        norms[2],
        norms[3],
    )


def solution(mesh):
    return jax.shard_map(
        body,
        mesh=mesh,
        in_specs=(
            P(("dp", "mp"), None),
            P("dp", None),
            P(None, None, "mp"),
            P("mp", None),
            P(None, None, "mp"),
            P("mp", None),
            P(),
            P(),
            P(),
            P(),
            P(("dp", "mp"), None),
        ),
        out_specs=(
            P(("dp", "mp"), None),
            P(("dp", "mp"), None),
            P(None, None, "mp"),
            P("mp", None),
            P(None, None, "mp"),
            P("mp", None),
            P("mp"),
            P("mp"),
            P("mp"),
            P("mp"),
        ),
        check_vma=False,
    )
```

```python
import functools
import math

import jax
import jax.numpy as jnp
from jax import lax
from jax.experimental import pallas as pl
from jax.experimental.pallas import tpu as pltpu
from jax.sharding import PartitionSpec as P

F32 = jnp.float32
BF16 = jnp.bfloat16
HEAD_DIM = 64
LANES = 128
EPSILON = 1e-05
FAR = -(2.0**100)
LOG2E = math.log2(math.e)
NT = (((1,), (1,)), ((), ()))
TN = (((0,), (0,)), ((), ()))
NN = (((1,), (0,)), ((), ()))
VMEM_LIMIT = 58 << 20
WIDE_LIMIT = 62 << 20
MESH = pl.DeviceIdType.MESH


def mm(a, b, dims=NN):
    return lax.dot_general(a, b, dims, preferred_element_type=F32)


def thirds(row):
    high = row.astype(BF16).astype(F32)
    mid = (row - high).astype(BF16).astype(F32)
    low = row - high - mid
    return jnp.concatenate([high, mid, low, jnp.zeros((13, row.shape[1]), F32)], axis=0)


def span(index, size):
    if isinstance(index, int):
        return pl.ds(index * size, size)
    return pl.ds(pl.multiple_of(index * size, size), size)


def dp_orders(size):
    bits = list(range(size.bit_length() - 1))
    return [bits, bits[1::-1] + bits[2:]]


def halvings(size):
    return min(3, size.bit_length() - 1)


def peer_of(index, bit):
    mine = (index // (1 << bit)) % 2
    return index + (1 - 2 * mine) * (1 << bit), mine


def send(source, target, send_sem, recv_sem, partner):
    copy = pltpu.make_async_remote_copy(
        source, target, send_sem, recv_sem, device_id=partner, device_id_type=MESH
    )
    copy.start()
    return copy


def greet(partners):
    barrier = pltpu.get_barrier_semaphore()
    for partner in partners:
        pl.semaphore_signal(barrier, inc=1, device_id=partner, device_id_type=MESH)
    pl.semaphore_wait(barrier, len(partners))


RING_PIECES = 8
RING_EARLY = 2


class Ring:
    def __init__(self, size, me, total, give, take, result, scatter_sems, gather_sems):
        self.n = n = min(RING_PIECES, size)
        self.me, self.size = me, size
        self.total, self.give, self.take, self.result = total, give, take, result
        self.scatter_sems, self.gather_sems = scatter_sems, gather_sems
        self.rows, self.cols = total.shape[1] // n, total.shape[2] // 2
        low = me % n
        across, along = low % 2, low // 2
        self.spot = (1 - across) * along + across * (n - 1 - along)
        self.peers = [self.index_at((self.spot + step) % n) for step in (1, n - 1)]

    def index_at(self, spot):
        across = spot // (self.n // 2)
        along = (1 - across) * spot + across * (self.n - 1 - spot)
        return self.me - self.me % self.n + 2 * along + across

    def piece(self, chain, step):
        shift = self.n * 4 - step if chain == 0 else step
        return pl.ds(pl.multiple_of((self.spot + shift) % self.n * self.rows, 16), self.rows)

    def half(self, sub):
        return span(sub, self.cols)

    def scatter(self, chain, sub, step):
        return pltpu.make_async_remote_copy(
            self.give.at[chain, sub],
            self.take.at[chain, sub, step],
            self.scatter_sems.at[0, chain, sub, step],
            self.scatter_sems.at[1, chain, sub, step],
            device_id={"dp": self.peers[chain]},
            device_id_type=MESH,
        )

    def gather(self, chain, sub, step):
        part = self.result.at[chain, self.piece(chain, step + self.n - 1), self.half(sub)]
        return pltpu.make_async_remote_copy(
            part,
            part,
            self.gather_sems.at[0, chain, sub, step],
            self.gather_sems.at[1, chain, sub, step],
            device_id={"dp": self.peers[chain]},
            device_id_type=MESH,
        )

    def begin(self, step, chain):
        for sub in range(2):
            self.give[chain, sub] = self.total[chain, self.piece(chain, step), self.half(sub)].astype(BF16)
            self.scatter(chain, sub, step).start()

    def arrived(self, step, chain, sub):
        self.scatter(chain, sub, step).wait()
        mine = self.total[chain, self.piece(chain, step + 1), self.half(sub)]
        return mine + self.take[chain, sub, step].astype(F32)

    def keep(self, step):
        for chain in range(2):
            for sub in range(2):
                value = self.arrived(step, chain, sub)
                self.total[chain, self.piece(chain, step + 1), self.half(sub)] = value

    def pass_on(self, step, sub):
        for chain in range(2):
            self.give[chain, sub] = self.arrived(step, chain, sub).astype(BF16)
            self.scatter(chain, sub, step + 1).start()

    def turn(self, step, sub):
        for chain in range(2):
            value = self.arrived(step, chain, sub).astype(BF16)
            self.give[chain, sub] = value
        for stage in range((self.size // self.n).bit_length() - 1):
            copies = []
            for chain in range(2):
                peer = self.me // self.n
                mine = (peer // (1 << stage)) % 2
                copies.append(
                    pltpu.make_async_remote_copy(
                        self.give.at[chain, sub],
                        self.take.at[chain, sub, self.n - 1 + stage],
                        self.scatter_sems.at[0, chain, sub, self.n - 1 + stage],
                        self.scatter_sems.at[1, chain, sub, self.n - 1 + stage],
                        device_id={"dp": self.me + (1 - 2 * mine) * (self.n << stage)},
                        device_id_type=MESH,
                    )
                )
                copies[-1].start()
            for chain in range(2):
                copies[chain].wait()
                value = self.give[chain, sub].astype(F32) + self.take[chain, sub, self.n - 1 + stage].astype(F32)
                self.give[chain, sub] = value.astype(BF16)
        for chain in range(2):
            self.result[chain, self.piece(chain, self.n - 1), self.half(sub)] = self.give[chain, sub]
            self.gather(chain, sub, 0).start()

    def event(self, number):
        step, sub, n = number // 2, number % 2, self.n

        @pl.when(step < n - 2)
        def _():
            self.pass_on(step, sub)

        @pl.when(step == n - 2)
        def _():
            self.turn(n - 2, sub)

        @pl.when(step >= n - 1)
        def _():
            for chain in range(2):
                self.gather(chain, sub, step - (n - 1)).wait()

            @pl.when(step < 2 * n - 3)
            def _():
                for chain in range(2):
                    self.gather(chain, sub, step - (n - 2)).start()


def ring_scratch(size, rows, cols, steps):
    piece = (rows // min(RING_PIECES, size), cols // 2)
    return [
        pltpu.VMEM((2, 2) + piece, BF16),
        pltpu.VMEM((2, 2, steps) + piece, BF16),
        pltpu.SemaphoreType.DMA((2, 2, 2, steps)),
    ]


X_FAR, X_NEAR, X_LAST, W_IN, W_DOWN, W_OUT, ATT_NEAR, ATT_LAST = range(8)
BRANCH, NORMED, OUT, DOUT, DNORMED, DH, DH_NEAR, DH_LAST, GRAD_NEAR = range(8, 17)
KINDS = 17


def first_kernel(
    size, lengths, tok_ref, cot_ref, w_ref, wo_ref, win_hbm, wdn_hbm, scale_one_hbm, shift_one_hbm, scale_two_hbm, shift_two_hbm,
    out_ref, dh_ref, slots_ref, norms_ref, total_hbm, x_hbm, q_hbm, k_hbm, v_hbm, q_rows_hbm, att_hbm, cos_hbm, sin_hbm,
    x_ref, win, wdn, wo_near_ref, att, near, outbox, inbox, low, hat, res, own, r1, dlow, give, take, sums,
    ring_give, ring_take, ln_ref, ring_sems, sems, loads, stores,
):
    rows, width = tok_ref.shape
    hidden = wdn.shape[0] // 2
    cols = wo_ref.shape[0]
    heads = cols // HEAD_DIM
    shards = x_ref.shape[0]
    tokens = shards * rows
    half = width // 2
    chunk = rows // 2
    chunks = [slice(c * chunk, (c + 1) * chunk) for c in range(2)]
    m, me = lax.axis_index("mp"), lax.axis_index("dp")
    core, far = {"mp": peer_of(m, 0)[0]}, {"mp": peer_of(m, 1)[0]}
    ring_peers = Ring(size, me, give, None, None, None, None, None).peers
    greet([core, far] + [{"dp": peer} for peer in ring_peers])

    def link(kind, c, source, target, partner):
        return pltpu.make_async_remote_copy(
            source, target, sems.at[0, kind, c], sems.at[1, kind, c], device_id=partner, device_id_type=MESH
        )

    def post(kind, c, source, target, partner):
        copy = link(kind, c, source, target, partner)
        copy.start()
        return copy

    far_copies = [post(X_FAR, c, tok_ref.at[where], x_ref.at[2, where], far) for c, where in enumerate(chunks)]
    near_copy = post(X_NEAR, 0, tok_ref, x_ref.at[1], core)
    weight_copies = [
        post(W_OUT, 0, wo_ref, wo_near_ref, core),
        post(W_DOWN, 0, wdn_hbm, wdn.at[pl.ds(hidden, hidden)], core),
    ]
    fetches = []
    moves = [(wdn_hbm, wdn.at[pl.ds(0, hidden)])]
    for n, source in enumerate((scale_one_hbm, shift_one_hbm, scale_two_hbm, shift_two_hbm)):
        moves.append((source, ln_ref.at[n]))
    for n, (source, target) in enumerate(moves):
        fetches.append(pltpu.make_async_copy(source, target, loads.at[n]))
        fetches[-1].start()
    x_ref[0] = tok_ref[...]
    sums[...] = jnp.zeros_like(sums)
    for fetch in fetches[1:]:
        fetch.wait()
    scale_one, shift_one, scale_two, shift_two = (ln_ref[i : i + 1, :] for i in range(4))

    def branch(slot, other, where):
        return mm(att[slot, :, where], wo_ref[...], TN) + mm(near[other, :, where], wo_near_ref[...], TN)

    def by_parts(c, part):
        step = 64

        def run(i, carry):
            part(pl.ds(pl.multiple_of(c * chunk + i * step, step), step))
            return carry

        lax.fori_loop(0, chunk // step, run, 0)

    def mean(values):
        return jnp.sum(values, axis=-1, keepdims=True) * (1.0 / width)

    def add_up(index, values):
        sums[index] += jnp.sum(values.reshape(values.shape[0] // 8, 8, width), axis=0)

    def norm_one(where):
        h = hat[where, :] + inbox[where, :].astype(F32)
        h = h - mean(h)
        r = lax.rsqrt(mean(h * h) + EPSILON)
        h = h * r
        hat[where, :] = h
        r1[where, :] = jnp.broadcast_to(r, (r.shape[0], LANES))
        h = h * scale_one + shift_one
        res[where, :] = h
        low[0, where, :] = h.astype(BF16)

    def attention(raw, q_ref, k_ref, v_ref, k_rows_ref, q_rows_ref, cos_ref, sin_ref, top_ref, acc_ref):
        fetch = pltpu.make_async_copy(win_hbm, raw, loads.at[5])
        fetch.start()
        half_head = HEAD_DIM // 2
        starts, ends, end = [], [], 0
        for d in range(lengths.shape[1]):
            starts.append(end)
            end = end + lengths[0, d]
            ends.append(end)
        doc = lax.broadcasted_iota(jnp.int32, (16, rows), 0)
        first, last = jnp.zeros((16, rows), jnp.int32), jnp.zeros((16, rows), jnp.int32)
        for d in range(lengths.shape[1]):
            first, last = jnp.where(doc == d, starts[d], first), jnp.where(doc == d, ends[d], last)
        exponent = lax.broadcasted_iota(jnp.int32, (half_head, rows), 0).astype(F32)
        rate = jnp.exp(exponent * (-2.0 * math.log(1000.0) / HEAD_DIM))
        row = lax.broadcasted_iota(jnp.int32, (48, rows), 0)
        ones = jnp.where(row < 3, 1.0, 0.0)
        v_tail = jnp.concatenate([ones, jnp.zeros((16, rows), F32)], axis=0)
        top_ref[...] = jnp.full_like(top_ref, FAR)
        acc_ref[...] = jnp.zeros_like(acc_ref)

        def tables(slot, carry):
            where = span(slot, rows)
            shard = 2 * ((slot // 2 + m // 2) % 2) + (slot + m) % 2
            token = lax.broadcasted_iota(jnp.int32, (16, rows), 1) + shard * rows
            inside = (token >= first) & (token < last)
            begin = jnp.max(jnp.where(inside, first, 0), axis=0, keepdims=True)
            angles = rate * (token[0:1] - begin).astype(F32)
            cos_ref[:, where], sin_ref[:, where] = jnp.cos(angles), jnp.sin(angles)
            for h in range(heads):
                q_ref[h, HEAD_DIM:, where] = jnp.concatenate(
                    [jnp.where(inside, 0.0, FAR), jnp.zeros((48, rows), F32)], axis=0
                ).astype(BF16)
                k_ref[h, HEAD_DIM:, where] = jnp.concatenate([jnp.where(inside, 1.0, 0.0), ones], axis=0).astype(BF16)
                v_ref[h, HEAD_DIM:, where] = v_tail.astype(BF16)
            return carry

        def project(part, carry):
            where = span(part, chunk)
            projected = mm(w_ref[...], x_ref[part // 2, span(part % 2, chunk), :], NT)
            cosine, sine = cos_ref[:, where], sin_ref[:, where]

            def rotated(start, scale):
                one, two = projected[start : start + half_head], projected[start + half_head : start + HEAD_DIM]
                turned = jnp.concatenate([one * cosine - two * sine, two * cosine + one * sine], axis=0)
                return turned * scale

            for h in range(heads):
                q_ref[h, :HEAD_DIM, where] = rotated(h * HEAD_DIM, LOG2E / math.sqrt(HEAD_DIM)).astype(BF16)
                k = rotated(cols + h * HEAD_DIM, 1.0)
                k_ref[h, :HEAD_DIM, where] = k.astype(BF16)
                tail = k_ref[h, HEAD_DIM:, where].astype(F32)
                k_rows_ref[h, where, :] = jnp.concatenate([k, tail], axis=0).T.astype(BF16)
                start = 2 * cols + h * HEAD_DIM
                v_ref[h, :HEAD_DIM, where] = projected[start : start + HEAD_DIM].astype(BF16)
            return carry

        def pairs(count, pair):
            def run(n, carry):
                qs, group = pair(n)
                queries, keys = span(qs, chunk), span(group, 2 * rows)
                scores, olds, tops = [], [], []
                for h in range(heads):
                    s = mm(k_rows_ref[h, keys, :], q_ref[h, :, queries])
                    olds.append(top_ref[qs, h, 0:1, :])
                    tops.append(jnp.maximum(olds[h], jnp.max(s, axis=0, keepdims=True)))
                    scores.append(s)
                for h in range(heads):
                    probs = jnp.exp2(scores[h] - tops[h]).astype(BF16)
                    top_ref[qs, h, 0:1, :] = tops[h]
                    acc_ref[qs, h] = acc_ref[qs, h] * jnp.exp2(olds[h] - tops[h]) + mm(v_ref[h, :80, keys], probs)
                return carry

            lax.fori_loop(0, count, run, 0)

        writes = []

        def write(source, target):
            writes.append(pltpu.make_async_copy(source, target, stores.at[len(writes)]))
            writes[-1].start()

        def settle(slot, c):
            part = 2 * slot + c
            for h in range(heads):
                total = acc_ref[part, h, HEAD_DIM : HEAD_DIM + 1, :]
                out = acc_ref[part, h, :HEAD_DIM, :] / total
                att[slot, h * HEAD_DIM : (h + 1) * HEAD_DIM, chunks[c]] = out.astype(BF16)
                top_ref[part, h, 1:2, :] = top_ref[part, h, 0:1, :] + jnp.log2(total)

        def turn(part, carry):
            where = span(part, chunk)
            for h in range(heads):
                query = q_ref[h, :, where].astype(F32)
                wide = jnp.concatenate([query[:80], thirds(-top_ref[part, h, 1:2, :]), query[96:]], axis=0)
                q_rows_ref[h, where, :] = wide.T.astype(BF16)
            return carry

        lax.fori_loop(0, shards, tables, 0)
        fetch.wait()

        def untangle(i, carry):
            where = span(i, 32)
            for n in range(2):
                win[0, where, n * hidden : (n + 1) * hidden] = raw[where, n, :]
            return carry

        lax.fori_loop(0, width // 32, untangle, 0)
        post(W_IN, 0, win.at[0], win.at[1], core)
        last_copies = []

        def hand_on(c):
            far_copies[c].wait()
            last_copies.append(post(X_LAST, c, x_ref.at[2, chunks[c]], x_ref.at[3, chunks[c]], core))

        near_copy.wait()
        lax.fori_loop(0, 4, project, 0)
        hand_on(0)
        pairs(4, lambda n: (n, 0))
        last_copies[0].wait()
        lax.fori_loop(0, 2, lambda n, carry: project(4 + 2 * n, carry), 0)
        hand_on(1)
        project(5, 0)
        last_copies[1].wait()
        project(7, 0)
        for source, target in [
            (x_ref, x_hbm), (q_ref, q_hbm), (k_ref, k_hbm), (v_ref, v_hbm), (cos_ref, cos_hbm), (sin_ref, sin_hbm)
        ]:
            write(source, target)
        weight_copies[0].wait()
        branch_copies = []
        for c, where in enumerate(chunks):
            pairs(2, lambda n: (6 + c, n))
            settle(3, c)
            last_att = post(ATT_LAST, c, att.at[3, :, where], near.at[1, :, where], core)
            pairs(2, lambda n: (4 + c, n))
            settle(2, c)
            last_att.wait()
            outbox[where, :] = branch(2, 1, where).astype(BF16)
            branch_copies.append(post(BRANCH, c, outbox.at[where], inbox.at[where], far))
        pairs(4, lambda n: (3 - n, 1))
        for c in range(2):
            settle(1, c)
        near_att = post(ATT_NEAR, 0, att.at[1], near.at[0], core)
        for c in range(2):
            settle(0, c)
        write(att, att_hbm)
        near_att.wait()
        for where in chunks:
            hat[where, :] = tok_ref[where, :].astype(F32) + branch(0, 0, where)
        for c, where in enumerate(chunks):
            branch_copies[c].wait()
            by_parts(c, norm_one)
            post(NORMED, c, low.at[0, where], low.at[1, where], far)
        lax.fori_loop(0, 2 * shards, turn, 0)
        write(q_rows_ref, q_rows_hbm)
        for copy in writes:
            copy.wait()

    along = pltpu.VMEM((heads, LANES, tokens), BF16)
    down = pltpu.VMEM((heads, tokens, LANES), BF16)
    table = pltpu.VMEM((HEAD_DIM // 2, tokens), F32)
    pl.run_scoped(
        attention, pltpu.VMEM((width, 2, hidden), BF16), along, along, along, down, down, table, table,
        pltpu.VMEM((2 * shards, heads, 8, chunk), F32), pltpu.VMEM((2 * shards, heads, 80, chunk), F32),
    )
    normed_copies = [link(NORMED, c, low.at[0, where], low.at[1, where], far) for c, where in enumerate(chunks)]
    for copy in fetches[:1] + weight_copies[1:] + [link(W_IN, 0, win.at[0], win.at[1], core)]:
        copy.wait()

    def feed_forward(gu, hid, total):
        ring = Ring(size, me, total, ring_give, ring_take, None, ring_sems, None)
        tile = hidden // 2

        def mlp(side, where):
            def columns(t, carry):
                k, at = t // 2, (t % 2) * tile
                x = low[side, where, :]
                gate_at = pl.ds(pl.multiple_of(at, LANES), tile)
                up_at = pl.ds(pl.multiple_of(hidden + at, LANES), tile)
                gate, up = mm(x, win[k, :, gate_at]), mm(x, win[k, :, up_at])
                gu[side, k, where, gate_at] = gate.astype(BF16)
                gu[side, k, where, up_at] = up.astype(BF16)
                value = gate * jax.nn.sigmoid(gate) * up
                hid[side, where, pl.ds(pl.multiple_of(k * hidden + at, LANES), tile)] = value.astype(BF16)
                return carry

            lax.fori_loop(0, 4, columns, 0)
            return mm(hid[side, where, :], wdn[...])

        def both_sides(copies_in, kind, compute):
            copies = []
            for c, where in enumerate(chunks):
                own[where, :] = compute(0, where)
                copies_in[c].wait()
                outbox[where, :] = compute(1, where).astype(BF16)
                copies.append(post(kind, c, outbox.at[where], inbox.at[where], far))
            return copies

        out_copies = both_sides(normed_copies, OUT, mlp)

        def norm_two(where):
            z = res[where, :] + own[where, :] + inbox[where, :].astype(F32)
            z = z - mean(z)
            r = lax.rsqrt(mean(z * z) + EPSILON)
            z = z * r
            out_ref[where, :] = (z * scale_two + shift_two).astype(BF16)
            g = cot_ref[where, :].astype(F32)
            add_up(2, g * z)
            add_up(3, g)
            e = g * scale_two
            dz = r * (e - mean(e) - z * mean(e * z))
            res[where, :] = dz
            dlow[0, where, :] = dz.astype(BF16)

        dout_copies = []
        for c, where in enumerate(chunks):
            out_copies[c].wait()
            by_parts(c, norm_two)
            dout_copies.append(post(DOUT, c, dlow.at[0, where], dlow.at[1, where], far))

        def mlp_back(side, where):
            def columns(t, carry):
                k, at = t // 2, (t % 2) * tile
                d_hidden = mm(
                    dlow[side, where, :], wdn[pl.ds(pl.multiple_of(k * hidden + at, LANES), tile), :], NT
                )
                gate_at = pl.ds(pl.multiple_of(at, LANES), tile)
                up_at = pl.ds(pl.multiple_of(hidden + at, LANES), tile)
                gate, up = gu[side, k, where, gate_at].astype(F32), gu[side, k, where, up_at].astype(F32)
                s = jax.nn.sigmoid(gate)
                gu[side, k, where, gate_at] = (d_hidden * up * s * (1.0 + gate * (1.0 - s))).astype(BF16)
                gu[side, k, where, up_at] = (d_hidden * gate * s).astype(BF16)
                return carry

            lax.fori_loop(0, 4, columns, 0)
            return mm(gu[side, 0, where, :], win[0], NT) + mm(gu[side, 1, where, :], win[1], NT)

        dnormed_copies = both_sides(dout_copies, DNORMED, mlp_back)

        def weight_grads(k, target, then=lambda r: None):
            def chain(r, carry):
                at = pl.ds(pl.multiple_of(r * half, LANES), half)
                for n, place in enumerate((slice(0, hidden), slice(hidden, 2 * hidden))):
                    piece = mm(low[0, :, at], gu[0, k, :, place], TN) + mm(low[1, :, at], gu[1, k, :, place], TN)
                    target[r, n * half : (n + 1) * half, :] = piece.astype(target.dtype)
                at = pl.ds(pl.multiple_of(k * hidden + r * half, LANES), half)
                piece = mm(hid[0, :, at], dlow[0], TN) + mm(hid[1, :, at], dlow[1], TN)
                target[r, 2 * half : 3 * half, :] = piece.astype(target.dtype)
                then(r)
                return carry

            lax.fori_loop(0, 2, chain, 0)

        def grad_copy(r):
            return link(GRAD_NEAR, r, give.at[r], take.at[r], core)

        weight_grads(1, give, lambda r: grad_copy(r).start())

        def norm_one_back(where):
            d = res[where, :] + own[where, :] + inbox[where, :].astype(F32)
            h = hat[where, :]
            add_up(0, d * h)
            add_up(1, d)
            e = d * scale_one
            dh = r1[where, 0:1] * (e - mean(e) - h * mean(e * h))
            dh_ref[where, :] = dh
            slots_ref[0, where, :] = dh.astype(BF16)

        dh_copies, last_copies = [], []

        def dh_chunk(c):
            where = chunks[c]
            dnormed_copies[c].wait()
            by_parts(c, norm_one_back)
            mine = slots_ref.at[0, where]
            dh_copies.append(post(DH, c, mine, slots_ref.at[2, where], far))
            last_copies.append(post(DH_NEAR, c, mine, slots_ref.at[1, where], core))

        dh_chunk(0)
        weight_grads(0, total)
        dh_chunk(1)
        for r in range(2):
            grad_copy(r).wait()
            total[r] += take[r].astype(F32)
            ring.begin(0, r)

        def hand_on(c):
            dh_copies[c].wait()
            where = chunks[c]
            last_copies.append(post(DH_LAST, c, slots_ref.at[2, where], slots_ref.at[3, where], core))

        for i in range(4):
            norms_ref[i : i + 1, :] = jnp.sum(sums[i], axis=0, keepdims=True)
        norms_ref[4:8, :] = jnp.zeros((4, width), F32)
        for step in range(RING_EARLY - 1):
            for sub in range(2):
                ring.pass_on(step, sub)
            if step < 2:
                hand_on(step)
        for step in range(RING_EARLY - 1, 2):
            hand_on(step)
        ring.keep(RING_EARLY - 1)
        write = pltpu.make_async_copy(total, total_hbm, loads.at[0])
        write.start()
        for copy in last_copies:
            copy.wait()
        write.wait()

    pl.run_scoped(
        feed_forward,
        pltpu.VMEM((2, 2, rows, 2 * hidden), BF16),
        pltpu.VMEM((2, rows, 2 * hidden), BF16),
        pltpu.VMEM((2, 3 * half, width), F32),
    )


def first(lengths, tokens, cotangent, norms, w_turned, w_out, w_in, w_down):
    size, shards = lax.axis_size("dp"), lax.axis_size("mp")
    rows, width = tokens.shape
    cols, hidden = w_out.shape[0], w_down.shape[0]
    heads, length = cols // HEAD_DIM, rows * shards
    chain = 3 * width // 2
    vmem = pl.BlockSpec(memory_space=pltpu.VMEM)
    hbm = pl.BlockSpec(memory_space=pl.ANY)
    dma = pltpu.SemaphoreType.DMA
    shape = jax.ShapeDtypeStruct
    along, table = shape((heads, LANES, length), BF16), shape((HEAD_DIM // 2, length), F32)
    wide = lambda dtype, *lead: pltpu.VMEM(lead + (rows, width), dtype)
    return pl.pallas_call(
        functools.partial(first_kernel, size),
        out_shape=(
            shape((rows, width), BF16),
            shape((rows, width), F32),
            shape((shards, rows, width), BF16),
            shape((8, width), F32),
            shape((2, chain, width), F32),
            shape((shards, rows, width), BF16),
            along,
            along,
            along,
            shape((heads, length, LANES), BF16),
            shape((shards, cols, rows), BF16),
            table,
            table,
        ),
        in_specs=[pl.BlockSpec(memory_space=pltpu.SMEM)] + [vmem] * 4 + [hbm] * 6,
        out_specs=[vmem] * 4 + [hbm] * 9,
        scratch_shapes=[
            wide(BF16, shards),
            pltpu.VMEM((2, width, 2 * hidden), BF16),
            pltpu.VMEM((2 * hidden, width), BF16),
            pltpu.VMEM((cols, width), BF16),
            pltpu.VMEM((shards, cols, rows), BF16),
            pltpu.VMEM((2, cols, rows), BF16),
            wide(BF16),
            wide(BF16),
            wide(BF16, 2),
            wide(F32),
            wide(F32),
            wide(F32),
            pltpu.VMEM((rows, LANES), F32),
            wide(BF16, 2),
            pltpu.VMEM((2, chain, width), BF16),
            pltpu.VMEM((2, chain, width), BF16),
            pltpu.VMEM((4, 8, width), F32),
            *ring_scratch(size, chain, width, RING_EARLY)[:2],
            pltpu.VMEM((8, width), F32),
            *ring_scratch(size, chain, width, RING_EARLY)[2:],
            dma((2, KINDS, 2)),
            dma((6,)),
            dma((8,)),
        ],
        compiler_params=pltpu.CompilerParams(
            collective_id=0, has_side_effects=True, vmem_limit_bytes=WIDE_LIMIT
        ),
        cost_estimate=pl.CostEstimate(
            flops=36 * rows * width * hidden, bytes_accessed=40 * rows * width, transcendentals=0
        ),
        name="first",
    )(lengths, tokens, cotangent, w_turned, w_out, w_in, w_down, *norms)


class Sum:
    def __init__(self, size, me, first, total, give, take, result, sems):
        orders = dp_orders(size)
        self.total, self.give, self.take, self.result, self.sems = total, give, take, result, sems
        halving, stages = halvings(size), size.bit_length() - 1
        count = 1 << (halving - first)
        self.rows = total.shape[1] // count
        base, low, peers = [], [0, 0], []
        for chain in range(2):
            peers.append([peer_of(me, bit) for bit in orders[chain]])
            base.append(sum(peers[chain][done][1] * (1 << (halving - 1 - done)) for done in range(first)))
        self.steps, spot = [], 0
        for stage in range(first, stages):
            halve = stage < halving
            part = count // 2 if halve else count
            step = dict(kind="halve" if halve else "swap", part=part, spot=spot, chains=[], last=stage + 1 == stages)
            for chain in range(2):
                peer, mine = peers[chain][stage]
                away = low[chain] + (1 - mine) * part if halve else low[chain]
                low[chain] = low[chain] + mine * part if halve else low[chain]
                step["chains"].append(dict(peer=peer, away=away, keep=low[chain], final=base[chain] + low[chain]))
            self.steps.append(step)
            spot, count = spot + part, part
        low = [base[chain] + low[chain] for chain in range(2)]
        for stage in reversed(range(halving)):
            step = dict(kind="gather", part=count, chains=[])
            for chain in range(2):
                peer, mine = peers[chain][stage]
                step["chains"].append(dict(peer=peer, away=low[chain]))
                low[chain] = low[chain] - mine * count
            self.steps.append(step)
            count *= 2

    def block(self, low, count):
        return pl.ds(pl.multiple_of(low * self.rows, 16), count * self.rows)

    def copy(self, index, chain):
        step = self.steps[index]
        one = step["chains"][chain]
        if step["kind"] == "gather":
            source = target = self.result.at[chain, self.block(one["away"], step["part"])]
        else:
            spot = pl.ds(step["spot"] * self.rows, step["part"] * self.rows)
            source, target = self.give.at[chain, spot], self.take.at[chain, spot]
        return pltpu.make_async_remote_copy(
            source,
            target,
            self.sems.at[0, chain, index],
            self.sems.at[1, chain, index],
            device_id={"dp": one["peer"]},
            device_id_type=MESH,
        )

    def start(self, index, chains=(0, 1)):
        step = self.steps[index]
        for chain in chains:
            if step["kind"] != "gather":
                spot = pl.ds(step["spot"] * self.rows, step["part"] * self.rows)
                away = self.block(step["chains"][chain]["away"], step["part"])
                self.give[chain, spot, :] = self.total[chain, away, :].astype(BF16)
            self.copy(index, chain).start()

    def finish(self, index):
        step = self.steps[index]
        for chain in range(2):
            self.copy(index, chain).wait()
            if step["kind"] == "gather":
                continue
            one = step["chains"][chain]
            spot = pl.ds(step["spot"] * self.rows, step["part"] * self.rows)
            keep = self.block(one["keep"], step["part"])
            mine = self.total[chain, keep, :] if step["kind"] == "halve" else self.give[chain, spot, :].astype(F32)
            value = mine + self.take[chain, spot, :].astype(F32)
            if step["last"]:
                self.result[chain, self.block(one["final"], 1), :] = value.astype(BF16)
            else:
                self.total[chain, keep, :] = value

    def advance(self, index):
        self.finish(index)
        if index + 1 < len(self.steps):
            self.start(index + 1)


def pieces_sent(size, first):
    halving = halvings(size)
    return (1 << (halving - first)) - 1 + size.bit_length() - 1 - halving


def back_kernel(
    size, att_ref, w_out_ref, cos_ref, sin_ref, norms_ref, w_ref, w_near_ref, dh_ref,
    total_hbm, slots_hbm, q_rows_hbm, q_hbm, k_hbm, v_hbm, x_hbm,
    dx_ref, grad_ref, big_ref, sums_ref,
    big, slots, q_rows_ref, q_ref, k_ref, v_ref, x_ref,
    do_ref, do_rows_ref, dq_ref, dk_ref, dv_ref, d_qkv,
    total, give, take, near, far_out, far_in, own, norm_in,
    ring_give, ring_take, ring_sems, gather_sems, loads, near_sem, far_sem, sum_sems, norm_sem,
):
    heads, _, tokens = k_ref.shape
    shards, rows, width = slots.shape
    cols = heads * HEAD_DIM
    half = HEAD_DIM // 2
    m, me = lax.axis_index("mp"), lax.axis_index("dp")
    stages = size.bit_length() - 1
    core, far = {"mp": peer_of(m, 0)[0]}, {"mp": peer_of(m, 1)[0]}
    partners = [core, far] + [{"dp": peer_of(me, bit)[0]} for bit in range(stages)]
    sources = [total_hbm, slots_hbm, q_rows_hbm, q_hbm, k_hbm, v_hbm, x_hbm]
    targets = [big, slots, q_rows_ref, q_ref, k_ref, v_ref, x_ref]
    fetches = [
        pltpu.make_async_copy(source, target, loads.at[n])
        for n, (source, target) in enumerate(zip(sources, targets))
    ]
    for fetch in fetches:
        fetch.start()
    ring = Ring(size, me, big, ring_give, ring_take, big_ref, ring_sems, gather_sems)
    greet(partners + [{"dp": peer} for peer in ring.peers])
    sums_ref[...] = norms_ref[...]
    small = Sum(size, me, 0, total, give, take, grad_ref, sum_sems)
    fetches[0].wait()
    for chain in range(2):
        ring.begin(RING_EARLY, chain)
    fetches[1].wait()
    events = 2 * (2 * ring.n - 2)
    first_event = 2 * RING_EARLY

    def prepare(i, carry):
        d_att = mm(w_out_ref[...], slots[i], NT).astype(BF16)
        do_ref[:, span(i, rows)] = d_att
        products = d_att.astype(F32) * att_ref[i].astype(F32)
        for h in range(heads):
            mine = slice(h * HEAD_DIM, (h + 1) * HEAD_DIM)
            dot = jnp.sum(products[mine], axis=0, keepdims=True)
            wide = [d_att[mine].astype(F32), thirds(-dot), jnp.zeros((LANES - HEAD_DIM - 16, rows), F32)]
            do_rows_ref[h, span(i, rows), :] = jnp.concatenate(wide, axis=0).T.astype(BF16)
        return carry

    lax.fori_loop(0, shards, prepare, 0)
    dq_ref[...] = jnp.zeros_like(dq_ref)
    for fetch in fetches[2:]:
        fetch.wait()

    def rotated_back(values, cosine, sine):
        first, second = values[:half], values[half:]
        return [first * cosine + second * sine, second * cosine - first * sine]

    def over_keys(j, carry):
        keys = span(j, rows)
        dk_ref[...] = jnp.zeros_like(dk_ref)
        dv_ref[...] = jnp.zeros_like(dv_ref)

        def over_queries(i, carry):
            queries = span(i, rows)
            for h in range(heads):
                k = k_ref[h, :, keys]
                probs = jnp.exp2(mm(q_rows_ref[h, queries, :], k))
                d_scores = (probs * mm(do_rows_ref[h, queries, :], v_ref[h, :, keys])).astype(BF16)
                dv_ref[h] += mm(do_ref[h * HEAD_DIM : (h + 1) * HEAD_DIM, queries], probs.astype(BF16))
                dk_ref[h] += mm(q_ref[h, :HEAD_DIM, queries], d_scores)
                dq_ref[h, :, queries] += mm(k[:HEAD_DIM], d_scores, NT)
            number = first_event + j * shards + i
            pl.when(number < events)(lambda: ring.event(number))
            return carry

        lax.fori_loop(0, shards, over_queries, 0)
        cosine, sine = cos_ref[:, keys] * (1.0 / LOG2E), sin_ref[:, keys] * (1.0 / LOG2E)
        pieces = []
        for h in range(heads):
            pieces += rotated_back(dk_ref[h], cosine, sine)
        pieces += [dv_ref[h] for h in range(heads)]
        d_qkv[j, cols:, :] = jnp.concatenate(pieces, axis=0).astype(BF16)
        return carry

    lax.fori_loop(0, shards, over_keys, 0)
    first_event = min(first_event + shards * shards, events)
    for i in range(shards):
        scale = 1.0 / math.sqrt(HEAD_DIM)
        cosine, sine = cos_ref[:, span(i, rows)] * scale, sin_ref[:, span(i, rows)] * scale
        pieces = []
        for h in range(heads):
            pieces += rotated_back(dq_ref[h, :, span(i, rows)], cosine, sine)
        d_qkv[i, :cols, :] = jnp.concatenate(pieces, axis=0).astype(BF16)
    near_copies = [send(d_qkv.at[2 * i + 1], near.at[i], near_sem.at[0, i], near_sem.at[1, i], core) for i in range(2)]

    def product(first, count):
        piece = mm(d_qkv[0, first : first + count, :], x_ref[0])
        for slot in range(1, shards):
            piece += mm(d_qkv[slot, first : first + count, :], x_ref[slot])
        return piece

    chain_rows = total.shape[1]
    total[0] = product(0, chain_rows)
    total[1, :cols, :] = product(chain_rows, cols)
    piece = mm(att_ref[0], slots[0])
    for slot in range(1, shards):
        piece += mm(att_ref[slot], slots[slot])
    total[1, cols:, :] = piece
    small.start(0)

    def norm_exchange(stage):
        return send(sums_ref, norm_in.at[stage], norm_sem.at[0, stage], norm_sem.at[1, stage], partners[stage])

    norm_copy, norm_done = norm_exchange(0), 0
    for copy in near_copies:
        copy.wait()

    def d_tokens(index):
        return mm(d_qkv[2 * index], w_ref[...], TN) + mm(near[index], w_near_ref[...], TN)

    far_out[...] = d_tokens(1).astype(BF16)
    far_copy = send(far_out, far_in, far_sem.at[0], far_sem.at[1], far)
    own[...] = dh_ref[...] + d_tokens(0)

    left, share = first_event, -(-(events - first_event) // len(small.steps))
    small_done = 0
    while small_done < len(small.steps) or norm_done < len(partners):
        if small_done < len(small.steps):
            small.advance(small_done)
            small_done += 1
            for number in range(left, min(left + share, events)):
                ring.event(number)
            left = min(left + share, events)
        if norm_done < len(partners):
            norm_copy.wait()
            sums_ref[...] += norm_in[norm_done]
            norm_done += 1
            if norm_done < len(partners):
                norm_copy = norm_exchange(norm_done)
    far_copy.wait()
    dx_ref[...] = (own[...] + far_in[...].astype(F32)).astype(BF16)


def back(att, w_out, cosine, sine, norms, w_turned, w_near, dh, totals, dh_slots, q_rows, q, k, v, x_slots):
    size = lax.axis_size("dp")
    stages = size.bit_length() - 1
    heads, _, tokens = q.shape
    shards, rows, width = x_slots.shape
    cols = w_turned.shape[0]
    chain, big_chain = width // 2, totals.shape[1]
    sent = pieces_sent(size, 0) * (chain >> halvings(size))
    spots = min(RING_PIECES, size)
    ring_steps = spots - 1 + (size // spots).bit_length() - 1
    steps = stages + halvings(size)
    vmem = pl.BlockSpec(memory_space=pltpu.VMEM)
    hbm = pl.BlockSpec(memory_space=pl.ANY)
    dma = pltpu.SemaphoreType.DMA
    along = pltpu.VMEM((heads, LANES, tokens), BF16)
    return pl.pallas_call(
        functools.partial(back_kernel, size),
        out_shape=(
            jax.ShapeDtypeStruct((rows, width), BF16),
            jax.ShapeDtypeStruct((2, chain, width), BF16),
            jax.ShapeDtypeStruct((2, big_chain, width), BF16),
            jax.ShapeDtypeStruct(norms.shape, F32),
        ),
        in_specs=[vmem] * 8 + [hbm] * 7,
        out_specs=[vmem] * 4,
        scratch_shapes=[
            pltpu.VMEM(totals.shape, F32),
            pltpu.VMEM(dh_slots.shape, BF16),
            pltpu.VMEM((heads, tokens, LANES), BF16),
            along,
            along,
            along,
            pltpu.VMEM(x_slots.shape, BF16),
            pltpu.VMEM((heads * HEAD_DIM, tokens), BF16),
            pltpu.VMEM((heads, tokens, LANES), BF16),
            pltpu.VMEM((heads, HEAD_DIM, tokens), F32),
            pltpu.VMEM((heads, HEAD_DIM, rows), F32),
            pltpu.VMEM((heads, HEAD_DIM, rows), F32),
            pltpu.VMEM((shards, cols, rows), BF16),
            pltpu.VMEM((2, chain, width), F32),
            pltpu.VMEM((2, sent, width), BF16),
            pltpu.VMEM((2, sent, width), BF16),
            pltpu.VMEM((2, cols, rows), BF16),
            pltpu.VMEM((rows, width), BF16),
            pltpu.VMEM((rows, width), BF16),
            pltpu.VMEM((rows, width), F32),
            pltpu.VMEM((2 + stages,) + norms.shape, F32),
            *ring_scratch(size, big_chain, width, ring_steps),
            dma((2, 2, 2, spots - 1)),
            dma((7,)),
            dma((2, 2)),
            dma((2,)),
            dma((2, 2, steps)),
            dma((2, 2 + stages)),
        ],
        compiler_params=pltpu.CompilerParams(
            collective_id=1, has_side_effects=True, vmem_limit_bytes=WIDE_LIMIT
        ),
        cost_estimate=pl.CostEstimate(
            flops=5 * heads * tokens * tokens * LANES, bytes_accessed=60 * rows * width, transcendentals=0
        ),
        name="back",
    )(att, w_out, cosine, sine, norms, w_turned, w_near, dh, totals, dh_slots, q_rows, q, k, v, x_slots)


def emit_kernel(big_ref, small_ref, out_ref, dx_ref, gate_up_hbm, down_ref, qkv_ref, w_out_ref, out_copy_ref, dx_copy_ref, wide, sems):
    step, steps = pl.program_id(0), pl.num_programs(0)
    rows = down_ref.shape[0]

    def copies(which):
        return [
            pltpu.make_async_copy(wide.at[which, n], gate_up_hbm.at[span(which, rows), n, :], sems.at[which, n])
            for n in range(2)
        ]

    for n in range(2):
        wide[step, n] = big_ref[0, n].astype(F32)
    for copy in copies(step):
        copy.start()
    down_ref[...] = big_ref[0, 2].astype(F32)
    out_copy_ref[...] = out_ref[...]
    dx_copy_ref[...] = dx_ref[...]
    qkv_steps = steps * 3 // 4

    @pl.when(step < qkv_steps)
    def _():
        qkv_ref[...] = small_ref[0].astype(F32)

    @pl.when(step >= qkv_steps)
    def _():
        w_out_ref[...] = small_ref[0].astype(F32)

    @pl.when(step == steps - 1)
    def _():
        for which in range(steps):
            for copy in copies(which):
                copy.wait()


def emit(big, small, output, d_tokens):
    _, chain, width = small.shape
    steps = 8
    per, rows = steps // 2, width // steps
    qkv_steps = steps * 3 // 4
    tokens = output.shape[0] // steps
    shape = lambda *dims: jax.ShapeDtypeStruct(dims, F32)
    low = jax.ShapeDtypeStruct(output.shape, BF16)
    few = pl.BlockSpec((tokens, width), lambda i: (i, 0))
    return pl.pallas_call(
        emit_kernel,
        out_shape=(
            shape(width, 2, width),
            shape(width, width),
            shape(qkv_steps * rows, width),
            shape((steps - qkv_steps) * rows, width),
            low,
            low,
        ),
        grid=(steps,),
        in_specs=[
            pl.BlockSpec((1, 3, rows, width), lambda i: (i // per, 0, i % per, 0)),
            pl.BlockSpec((1, rows, width), lambda i: (i // per, i % per, 0)),
            few,
            few,
        ],
        out_specs=[
            pl.BlockSpec(memory_space=pl.ANY),
            pl.BlockSpec((rows, width), lambda i: (i, 0)),
            pl.BlockSpec((rows, width), lambda i: (jnp.minimum(i, qkv_steps - 1), 0)),
            pl.BlockSpec((rows, width), lambda i: (jnp.maximum(i - qkv_steps, 0), 0)),
            few,
            few,
        ],
        scratch_shapes=[pltpu.VMEM((steps, 2, rows, width), F32), pltpu.SemaphoreType.DMA((steps, 2))],
        compiler_params=pltpu.CompilerParams(vmem_limit_bytes=VMEM_LIMIT),
        cost_estimate=pl.CostEstimate(flops=0, bytes_accessed=24 * width * width, transcendentals=0),
        name="emit",
    )(big.reshape(2, 3, chain, width), small, output, d_tokens)


def body(
    tokens, lengths, w_qkv, w_out, w_gate_up, w_down, ln1_scale, ln1_shift, ln2_scale, ln2_shift, cotangent
):
    rows, width = tokens.shape
    shards = lax.axis_size("mp")
    local_cols = w_out.shape[0]
    hidden_cols = w_down.shape[0]
    m = lax.axis_index("mp")
    qkv_turned = w_qkv.transpose(1, 2, 0).reshape(3 * local_cols, width)
    qkv_near = lax.ppermute(qkv_turned, "mp", [(i, i ^ 1) for i in range(shards)])
    norms = (ln1_scale, ln1_shift, ln2_scale, ln2_shift)
    output, dh, dh_slots, norms, totals, x_slots, q, k, v, q_rows, att, cosine, sine = first(
        lengths, tokens, cotangent, norms, qkv_turned, w_out, w_gate_up, w_down
    )
    d_tokens, small, big, norms = back(
        att, w_out, cosine, sine, norms, qkv_turned, qkv_near, dh, totals, dh_slots, q_rows, q, k, v, x_slots
    )
    grad_gate_up, grad_down, grad_qkv, grad_out, output, d_tokens = emit(big, small, output, d_tokens)
    grad_qkv = grad_qkv.reshape(3, local_cols, width).transpose(2, 0, 1)
    norms = lax.dynamic_slice_in_dim(norms, m * local_cols, local_cols, 1)
    return (
        output,
        d_tokens,
        grad_qkv,
        grad_out,
        grad_gate_up,
        grad_down,
        norms[0],
        norms[1],
        norms[2],
        norms[3],
    )


def solution(mesh):
    return jax.shard_map(
        body,
        mesh=mesh,
        in_specs=(
            P(("dp", "mp"), None),
            P("dp", None),
            P(None, None, "mp"),
            P("mp", None),
            P(None, None, "mp"),
            P("mp", None),
            P(),
            P(),
            P(),
            P(),
            P(("dp", "mp"), None),
        ),
        out_specs=(
            P(("dp", "mp"), None),
            P(("dp", "mp"), None),
            P(None, None, "mp"),
            P("mp", None),
            P(None, None, "mp"),
            P("mp", None),
            P("mp"),
            P("mp"),
            P("mp"),
            P("mp"),
        ),
        check_vma=False,
    )
```

```python
import functools
import math

import jax
import jax.numpy as jnp
from jax import lax
from jax.experimental import pallas as pl
from jax.experimental.pallas import tpu as pltpu
from jax.sharding import PartitionSpec as P

F32 = jnp.float32
BF16 = jnp.bfloat16
HEAD_DIM = 64
LANES = 128
EPSILON = 1e-05
FAR = -(2.0**100)
LOG2E = math.log2(math.e)
NT = (((1,), (1,)), ((), ()))
TN = (((0,), (0,)), ((), ()))
NN = (((1,), (0,)), ((), ()))
VMEM_LIMIT = 58 << 20
WIDE_LIMIT = 62 << 20
MESH = pl.DeviceIdType.MESH


def mm(a, b, dims=NN):
    return lax.dot_general(a, b, dims, preferred_element_type=F32)


def thirds(row):
    high = row.astype(BF16).astype(F32)
    mid = (row - high).astype(BF16).astype(F32)
    low = row - high - mid
    return jnp.concatenate([high, mid, low, jnp.zeros((13, row.shape[1]), F32)], axis=0)


def span(index, size):
    if isinstance(index, int):
        return pl.ds(index * size, size)
    return pl.ds(pl.multiple_of(index * size, size), size)


def dp_orders(size):
    bits = list(range(size.bit_length() - 1))
    return [bits, bits[1::-1] + bits[2:]]


def halvings(size):
    return min(3, size.bit_length() - 1)


def peer_of(index, bit):
    mine = (index // (1 << bit)) % 2
    return index + (1 - 2 * mine) * (1 << bit), mine


def send(source, target, send_sem, recv_sem, partner):
    copy = pltpu.make_async_remote_copy(
        source, target, send_sem, recv_sem, device_id=partner, device_id_type=MESH
    )
    copy.start()
    return copy


def greet(partners):
    barrier = pltpu.get_barrier_semaphore()
    for partner in partners:
        pl.semaphore_signal(barrier, inc=1, device_id=partner, device_id_type=MESH)
    pl.semaphore_wait(barrier, len(partners))


RING_PIECES = 8
RING_EARLY = 2


class Ring:
    def __init__(self, size, me, total, give, take, result, scatter_sems, gather_sems):
        self.n = n = min(RING_PIECES, size)
        self.me, self.size = me, size
        self.total, self.give, self.take, self.result = total, give, take, result
        self.scatter_sems, self.gather_sems = scatter_sems, gather_sems
        self.rows, self.cols = total.shape[1] // n, total.shape[2] // 2
        low = me % n
        across, along = low % 2, low // 2
        self.spot = (1 - across) * along + across * (n - 1 - along)
        self.peers = [self.index_at((self.spot + step) % n) for step in (1, n - 1)]

    def index_at(self, spot):
        across = spot // (self.n // 2)
        along = (1 - across) * spot + across * (self.n - 1 - spot)
        return self.me - self.me % self.n + 2 * along + across

    def piece(self, chain, step):
        shift = self.n * 4 - step if chain == 0 else step
        return pl.ds(pl.multiple_of((self.spot + shift) % self.n * self.rows, 16), self.rows)

    def half(self, sub):
        return span(sub, self.cols)

    def scatter(self, chain, sub, step):
        return pltpu.make_async_remote_copy(
            self.give.at[chain, sub],
            self.take.at[chain, sub, step],
            self.scatter_sems.at[0, chain, sub, step],
            self.scatter_sems.at[1, chain, sub, step],
            device_id={"dp": self.peers[chain]},
            device_id_type=MESH,
        )

    def gather(self, chain, sub, step):
        part = self.result.at[chain, self.piece(chain, step + self.n - 1), self.half(sub)]
        return pltpu.make_async_remote_copy(
            part,
            part,
            self.gather_sems.at[0, chain, sub, step],
            self.gather_sems.at[1, chain, sub, step],
            device_id={"dp": self.peers[chain]},
            device_id_type=MESH,
        )

    def begin(self, step, chain):
        for sub in range(2):
            self.give[chain, sub] = self.total[chain, self.piece(chain, step), self.half(sub)].astype(BF16)
            self.scatter(chain, sub, step).start()

    def arrived(self, step, chain, sub):
        self.scatter(chain, sub, step).wait()
        mine = self.total[chain, self.piece(chain, step + 1), self.half(sub)]
        return mine + self.take[chain, sub, step].astype(F32)

    def keep(self, step):
        for chain in range(2):
            for sub in range(2):
                value = self.arrived(step, chain, sub)
                self.total[chain, self.piece(chain, step + 1), self.half(sub)] = value

    def pass_on(self, step, sub):
        for chain in range(2):
            self.give[chain, sub] = self.arrived(step, chain, sub).astype(BF16)
            self.scatter(chain, sub, step + 1).start()

    def turn(self, step, sub):
        for chain in range(2):
            value = self.arrived(step, chain, sub).astype(BF16)
            self.give[chain, sub] = value
        for stage in range((self.size // self.n).bit_length() - 1):
            copies = []
            for chain in range(2):
                peer = self.me // self.n
                mine = (peer // (1 << stage)) % 2
                copies.append(
                    pltpu.make_async_remote_copy(
                        self.give.at[chain, sub],
                        self.take.at[chain, sub, self.n - 1 + stage],
                        self.scatter_sems.at[0, chain, sub, self.n - 1 + stage],
                        self.scatter_sems.at[1, chain, sub, self.n - 1 + stage],
                        device_id={"dp": self.me + (1 - 2 * mine) * (self.n << stage)},
                        device_id_type=MESH,
                    )
                )
                copies[-1].start()
            for chain in range(2):
                copies[chain].wait()
                value = self.give[chain, sub].astype(F32) + self.take[chain, sub, self.n - 1 + stage].astype(F32)
                self.give[chain, sub] = value.astype(BF16)
        for chain in range(2):
            self.result[chain, self.piece(chain, self.n - 1), self.half(sub)] = self.give[chain, sub]
            self.gather(chain, sub, 0).start()

    def event(self, number):
        step, sub, n = number // 2, number % 2, self.n

        @pl.when(step < n - 2)
        def _():
            self.pass_on(step, sub)

        @pl.when(step == n - 2)
        def _():
            self.turn(n - 2, sub)

        @pl.when(step >= n - 1)
        def _():
            for chain in range(2):
                self.gather(chain, sub, step - (n - 1)).wait()

            @pl.when(step < 2 * n - 3)
            def _():
                for chain in range(2):
                    self.gather(chain, sub, step - (n - 2)).start()


def ring_scratch(size, rows, cols, steps):
    piece = (rows // min(RING_PIECES, size), cols // 2)
    return [
        pltpu.VMEM((2, 2) + piece, BF16),
        pltpu.VMEM((2, 2, steps) + piece, BF16),
        pltpu.SemaphoreType.DMA((2, 2, 2, steps)),
    ]


X_FAR, X_NEAR, X_LAST, W_IN, W_DOWN, W_OUT, ATT_NEAR, ATT_LAST = range(8)
BRANCH, NORMED, OUT, DOUT, DNORMED, DH, DH_NEAR, DH_LAST, GRAD_NEAR = range(8, 17)
KINDS = 17


def first_kernel(
    size, lengths, tok_ref, cot_ref, w_ref, wo_ref, win_hbm, wdn_hbm, scale_one_hbm, shift_one_hbm, scale_two_hbm, shift_two_hbm,
    out_ref, dh_ref, slots_ref, norms_ref, total_hbm, x_hbm, q_hbm, k_hbm, v_hbm, q_rows_hbm, att_hbm, cos_hbm, sin_hbm,
    x_ref, win, wdn, wo_near_ref, att, near, outbox, inbox, low, hat, res, own, r1, dlow, give, take, sums,
    ring_give, ring_take, ln_ref, ring_sems, sems, loads, stores,
):
    rows, width = tok_ref.shape
    hidden = wdn.shape[0] // 2
    cols = wo_ref.shape[0]
    heads = cols // HEAD_DIM
    shards = x_ref.shape[0]
    tokens = shards * rows
    half = width // 2
    chunk = rows // 2
    chunks = [slice(c * chunk, (c + 1) * chunk) for c in range(2)]
    m, me = lax.axis_index("mp"), lax.axis_index("dp")
    core, far = {"mp": peer_of(m, 0)[0]}, {"mp": peer_of(m, 1)[0]}
    ring_peers = Ring(size, me, give, None, None, None, None, None).peers
    greet([core, far] + [{"dp": peer} for peer in ring_peers])

    def link(kind, c, source, target, partner):
        return pltpu.make_async_remote_copy(
            source, target, sems.at[0, kind, c], sems.at[1, kind, c], device_id=partner, device_id_type=MESH
        )

    def post(kind, c, source, target, partner):
        copy = link(kind, c, source, target, partner)
        copy.start()
        return copy

    far_copies = [post(X_FAR, c, tok_ref.at[where], x_ref.at[2, where], far) for c, where in enumerate(chunks)]
    near_copy = post(X_NEAR, 0, tok_ref, x_ref.at[1], core)
    weight_copies = [
        post(W_OUT, 0, wo_ref, wo_near_ref, core),
        post(W_DOWN, 0, wdn_hbm, wdn.at[pl.ds(hidden, hidden)], core),
    ]
    fetches = []
    moves = [(wdn_hbm, wdn.at[pl.ds(0, hidden)])]
    for n, source in enumerate((scale_one_hbm, shift_one_hbm, scale_two_hbm, shift_two_hbm)):
        moves.append((source, ln_ref.at[n]))
    for n, (source, target) in enumerate(moves):
        fetches.append(pltpu.make_async_copy(source, target, loads.at[n]))
        fetches[-1].start()
    x_ref[0] = tok_ref[...]
    sums[...] = jnp.zeros_like(sums)
    for fetch in fetches[1:]:
        fetch.wait()
    scale_one, shift_one, scale_two, shift_two = (ln_ref[i : i + 1, :] for i in range(4))

    def branch(slot, other, where):
        return mm(att[slot, :, where], wo_ref[...], TN) + mm(near[other, :, where], wo_near_ref[...], TN)

    def by_parts(c, part):
        step = 64

        def run(i, carry):
            part(pl.ds(pl.multiple_of(c * chunk + i * step, step), step))
            return carry

        lax.fori_loop(0, chunk // step, run, 0)

    def mean(values):
        return jnp.sum(values, axis=-1, keepdims=True) * (1.0 / width)

    def add_up(index, values):
        sums[index] += jnp.sum(values.reshape(values.shape[0] // 8, 8, width), axis=0)

    def norm_one(where):
        h = hat[where, :] + inbox[where, :].astype(F32)
        h = h - mean(h)
        r = lax.rsqrt(mean(h * h) + EPSILON)
        h = h * r
        hat[where, :] = h
        r1[where, :] = jnp.broadcast_to(r, (r.shape[0], LANES))
        h = h * scale_one + shift_one
        res[where, :] = h
        low[0, where, :] = h.astype(BF16)

    def attention(raw, q_ref, k_ref, v_ref, k_rows_ref, q_rows_ref, cos_ref, sin_ref, top_ref, acc_ref):
        fetch = pltpu.make_async_copy(win_hbm, raw, loads.at[5])
        fetch.start()
        half_head = HEAD_DIM // 2
        starts, ends, end = [], [], 0
        for d in range(lengths.shape[1]):
            starts.append(end)
            end = end + lengths[0, d]
            ends.append(end)
        doc = lax.broadcasted_iota(jnp.int32, (16, rows), 0)
        first, last = jnp.zeros((16, rows), jnp.int32), jnp.zeros((16, rows), jnp.int32)
        for d in range(lengths.shape[1]):
            first, last = jnp.where(doc == d, starts[d], first), jnp.where(doc == d, ends[d], last)
        exponent = lax.broadcasted_iota(jnp.int32, (half_head, rows), 0).astype(F32)
        rate = jnp.exp(exponent * (-2.0 * math.log(1000.0) / HEAD_DIM))
        row = lax.broadcasted_iota(jnp.int32, (48, rows), 0)
        ones = jnp.where(row < 3, 1.0, 0.0)
        v_tail = jnp.concatenate([ones, jnp.zeros((16, rows), F32)], axis=0)
        top_ref[...] = jnp.full_like(top_ref, FAR)
        acc_ref[...] = jnp.zeros_like(acc_ref)

        def tables(slot, carry):
            where = span(slot, rows)
            shard = 2 * ((slot // 2 + m // 2) % 2) + (slot + m) % 2
            token = lax.broadcasted_iota(jnp.int32, (16, rows), 1) + shard * rows
            inside = (token >= first) & (token < last)
            begin = jnp.max(jnp.where(inside, first, 0), axis=0, keepdims=True)
            angles = rate * (token[0:1] - begin).astype(F32)
            cos_ref[:, where], sin_ref[:, where] = jnp.cos(angles), jnp.sin(angles)
            for h in range(heads):
                q_ref[h, HEAD_DIM:, where] = jnp.concatenate(
                    [jnp.where(inside, 0.0, FAR), jnp.zeros((48, rows), F32)], axis=0
                ).astype(BF16)
                k_ref[h, HEAD_DIM:, where] = jnp.concatenate([jnp.where(inside, 1.0, 0.0), ones], axis=0).astype(BF16)
                v_ref[h, HEAD_DIM:, where] = v_tail.astype(BF16)
            return carry

        def project(part, carry):
            where = span(part, chunk)
            projected = mm(w_ref[...], x_ref[part // 2, span(part % 2, chunk), :], NT)
            cosine, sine = cos_ref[:, where], sin_ref[:, where]

            def rotated(start, scale):
                one, two = projected[start : start + half_head], projected[start + half_head : start + HEAD_DIM]
                turned = jnp.concatenate([one * cosine - two * sine, two * cosine + one * sine], axis=0)
                return turned * scale

            for h in range(heads):
                q_ref[h, :HEAD_DIM, where] = rotated(h * HEAD_DIM, LOG2E / math.sqrt(HEAD_DIM)).astype(BF16)
                k = rotated(cols + h * HEAD_DIM, 1.0)
                k_ref[h, :HEAD_DIM, where] = k.astype(BF16)
                tail = k_ref[h, HEAD_DIM:, where].astype(F32)
                k_rows_ref[h, where, :] = jnp.concatenate([k, tail], axis=0).T.astype(BF16)
                start = 2 * cols + h * HEAD_DIM
                v_ref[h, :HEAD_DIM, where] = projected[start : start + HEAD_DIM].astype(BF16)
            return carry

        def pairs(count, pair):
            def run(n, carry):
                qs, group = pair(n)
                queries, keys = span(qs, chunk), span(group, 2 * rows)
                scores, olds, tops = [], [], []
                for h in range(heads):
                    s = mm(k_rows_ref[h, keys, :], q_ref[h, :, queries])
                    olds.append(top_ref[qs, h, 0:1, :])
                    tops.append(jnp.maximum(olds[h], jnp.max(s, axis=0, keepdims=True)))
                    scores.append(s)
                for h in range(heads):
                    probs = jnp.exp2(scores[h] - tops[h]).astype(BF16)
                    top_ref[qs, h, 0:1, :] = tops[h]
                    acc_ref[qs, h] = acc_ref[qs, h] * jnp.exp2(olds[h] - tops[h]) + mm(v_ref[h, :80, keys], probs)
                return carry

            lax.fori_loop(0, count, run, 0)

        writes = []

        def write(source, target):
            writes.append(pltpu.make_async_copy(source, target, stores.at[len(writes)]))
            writes[-1].start()

        def settle(slot, c):
            part = 2 * slot + c
            for h in range(heads):
                total = acc_ref[part, h, HEAD_DIM : HEAD_DIM + 1, :]
                out = acc_ref[part, h, :HEAD_DIM, :] / total
                att[slot, h * HEAD_DIM : (h + 1) * HEAD_DIM, chunks[c]] = out.astype(BF16)
                top_ref[part, h, 1:2, :] = top_ref[part, h, 0:1, :] + jnp.log2(total)

        def turn(part, carry):
            where = span(part, chunk)
            for h in range(heads):
                query = q_ref[h, :, where].astype(F32)
                wide = jnp.concatenate([query[:80], thirds(-top_ref[part, h, 1:2, :]), query[96:]], axis=0)
                q_rows_ref[h, where, :] = wide.T.astype(BF16)
            return carry

        lax.fori_loop(0, shards, tables, 0)
        fetch.wait()

        def untangle(i, carry):
            where = span(i, 32)
            for n in range(2):
                win[0, where, n * hidden : (n + 1) * hidden] = raw[where, n, :]
            return carry

        lax.fori_loop(0, width // 32, untangle, 0)
        post(W_IN, 0, win.at[0], win.at[1], core)
        last_copies = []

        def hand_on(c):
            far_copies[c].wait()
            last_copies.append(post(X_LAST, c, x_ref.at[2, chunks[c]], x_ref.at[3, chunks[c]], core))

        near_copy.wait()
        lax.fori_loop(0, 4, project, 0)
        hand_on(0)
        pairs(4, lambda n: (n, 0))
        last_copies[0].wait()
        lax.fori_loop(0, 2, lambda n, carry: project(4 + 2 * n, carry), 0)
        hand_on(1)
        project(5, 0)
        last_copies[1].wait()
        project(7, 0)
        for source, target in [
            (x_ref, x_hbm), (q_ref, q_hbm), (k_ref, k_hbm), (v_ref, v_hbm), (cos_ref, cos_hbm), (sin_ref, sin_hbm)
        ]:
            write(source, target)
        weight_copies[0].wait()
        branch_copies = []
        for c, where in enumerate(chunks):
            pairs(2, lambda n: (6 + c, n))
            settle(3, c)
            last_att = post(ATT_LAST, c, att.at[3, :, where], near.at[1, :, where], core)
            pairs(2, lambda n: (4 + c, n))
            settle(2, c)
            last_att.wait()
            outbox[where, :] = branch(2, 1, where).astype(BF16)
            branch_copies.append(post(BRANCH, c, outbox.at[where], inbox.at[where], far))
        pairs(4, lambda n: (3 - n, 1))
        for c in range(2):
            settle(1, c)
        near_att = post(ATT_NEAR, 0, att.at[1], near.at[0], core)
        for c in range(2):
            settle(0, c)
        write(att, att_hbm)
        near_att.wait()
        for where in chunks:
            hat[where, :] = tok_ref[where, :].astype(F32) + branch(0, 0, where)
        for c, where in enumerate(chunks):
            branch_copies[c].wait()
            by_parts(c, norm_one)
            post(NORMED, c, low.at[0, where], low.at[1, where], far)
        lax.fori_loop(0, 2 * shards, turn, 0)
        write(q_rows_ref, q_rows_hbm)
        for copy in writes:
            copy.wait()

    along = pltpu.VMEM((heads, LANES, tokens), BF16)
    down = pltpu.VMEM((heads, tokens, LANES), BF16)
    table = pltpu.VMEM((HEAD_DIM // 2, tokens), F32)
    pl.run_scoped(
        attention, pltpu.VMEM((width, 2, hidden), BF16), along, along, along, down, down, table, table,
        pltpu.VMEM((2 * shards, heads, 8, chunk), F32), pltpu.VMEM((2 * shards, heads, 80, chunk), F32),
    )
    normed_copies = [link(NORMED, c, low.at[0, where], low.at[1, where], far) for c, where in enumerate(chunks)]
    for copy in fetches[:1] + weight_copies[1:] + [link(W_IN, 0, win.at[0], win.at[1], core)]:
        copy.wait()

    def feed_forward(gu, hid, total):
        ring = Ring(size, me, total, ring_give, ring_take, None, ring_sems, None)
        tile = hidden // 2

        def mlp(side, where):
            def columns(t, carry):
                k, at = t // 2, (t % 2) * tile
                x = low[side, where, :]
                gate_at = pl.ds(pl.multiple_of(at, LANES), tile)
                up_at = pl.ds(pl.multiple_of(hidden + at, LANES), tile)
                gate, up = mm(x, win[k, :, gate_at]), mm(x, win[k, :, up_at])
                gu[side, k, where, gate_at] = gate.astype(BF16)
                gu[side, k, where, up_at] = up.astype(BF16)
                value = gate * jax.nn.sigmoid(gate) * up
                hid[side, where, pl.ds(pl.multiple_of(k * hidden + at, LANES), tile)] = value.astype(BF16)
                return carry

            lax.fori_loop(0, 4, columns, 0)
            return mm(hid[side, where, :], wdn[...])

        def both_sides(copies_in, kind, compute):
            copies = []
            for c, where in enumerate(chunks):
                own[where, :] = compute(0, where)
                copies_in[c].wait()
                outbox[where, :] = compute(1, where).astype(BF16)
                copies.append(post(kind, c, outbox.at[where], inbox.at[where], far))
            return copies

        out_copies = both_sides(normed_copies, OUT, mlp)

        def norm_two(where):
            z = res[where, :] + own[where, :] + inbox[where, :].astype(F32)
            z = z - mean(z)
            r = lax.rsqrt(mean(z * z) + EPSILON)
            z = z * r
            out_ref[where, :] = (z * scale_two + shift_two).astype(BF16)
            g = cot_ref[where, :].astype(F32)
            add_up(2, g * z)
            add_up(3, g)
            e = g * scale_two
            dz = r * (e - mean(e) - z * mean(e * z))
            res[where, :] = dz
            dlow[0, where, :] = dz.astype(BF16)

        dout_copies = []
        for c, where in enumerate(chunks):
            out_copies[c].wait()
            by_parts(c, norm_two)
            dout_copies.append(post(DOUT, c, dlow.at[0, where], dlow.at[1, where], far))

        def mlp_back(side, where):
            def columns(t, carry):
                k, at = t // 2, (t % 2) * tile
                d_hidden = mm(
                    dlow[side, where, :], wdn[pl.ds(pl.multiple_of(k * hidden + at, LANES), tile), :], NT
                )
                gate_at = pl.ds(pl.multiple_of(at, LANES), tile)
                up_at = pl.ds(pl.multiple_of(hidden + at, LANES), tile)
                gate, up = gu[side, k, where, gate_at].astype(F32), gu[side, k, where, up_at].astype(F32)
                s = jax.nn.sigmoid(gate)
                gu[side, k, where, gate_at] = (d_hidden * up * s * (1.0 + gate * (1.0 - s))).astype(BF16)
                gu[side, k, where, up_at] = (d_hidden * gate * s).astype(BF16)
                return carry

            lax.fori_loop(0, 4, columns, 0)
            return mm(gu[side, 0, where, :], win[0], NT) + mm(gu[side, 1, where, :], win[1], NT)

        dnormed_copies = both_sides(dout_copies, DNORMED, mlp_back)

        def weight_grads(k, target, then=lambda r: None):
            def chain(r, carry):
                at = pl.ds(pl.multiple_of(r * half, LANES), half)
                for n, place in enumerate((slice(0, hidden), slice(hidden, 2 * hidden))):
                    piece = mm(low[0, :, at], gu[0, k, :, place], TN) + mm(low[1, :, at], gu[1, k, :, place], TN)
                    target[r, n * half : (n + 1) * half, :] = piece.astype(target.dtype)
                at = pl.ds(pl.multiple_of(k * hidden + r * half, LANES), half)
                piece = mm(hid[0, :, at], dlow[0], TN) + mm(hid[1, :, at], dlow[1], TN)
                target[r, 2 * half : 3 * half, :] = piece.astype(target.dtype)
                then(r)
                return carry

            lax.fori_loop(0, 2, chain, 0)

        def grad_copy(r):
            return link(GRAD_NEAR, r, give.at[r], take.at[r], core)

        weight_grads(1, give, lambda r: grad_copy(r).start())

        def norm_one_back(where):
            d = res[where, :] + own[where, :] + inbox[where, :].astype(F32)
            h = hat[where, :]
            add_up(0, d * h)
            add_up(1, d)
            e = d * scale_one
            dh = r1[where, 0:1] * (e - mean(e) - h * mean(e * h))
            dh_ref[where, :] = dh
            slots_ref[0, where, :] = dh.astype(BF16)

        dh_copies, last_copies = [], []

        def dh_chunk(c):
            where = chunks[c]
            dnormed_copies[c].wait()
            by_parts(c, norm_one_back)
            mine = slots_ref.at[0, where]
            dh_copies.append(post(DH, c, mine, slots_ref.at[2, where], far))
            last_copies.append(post(DH_NEAR, c, mine, slots_ref.at[1, where], core))

        dh_chunk(0)
        weight_grads(0, total)
        dh_chunk(1)
        for r in range(2):
            grad_copy(r).wait()
            total[r] += take[r].astype(F32)
            ring.begin(0, r)

        def hand_on(c):
            dh_copies[c].wait()
            where = chunks[c]
            last_copies.append(post(DH_LAST, c, slots_ref.at[2, where], slots_ref.at[3, where], core))

        for i in range(4):
            norms_ref[i : i + 1, :] = jnp.sum(sums[i], axis=0, keepdims=True)
        norms_ref[4:8, :] = jnp.zeros((4, width), F32)
        for step in range(RING_EARLY - 1):
            for sub in range(2):
                ring.pass_on(step, sub)
            if step < 2:
                hand_on(step)
        for step in range(RING_EARLY - 1, 2):
            hand_on(step)
        ring.keep(RING_EARLY - 1)
        write = pltpu.make_async_copy(total, total_hbm, loads.at[0])
        write.start()
        for copy in last_copies:
            copy.wait()
        write.wait()

    pl.run_scoped(
        feed_forward,
        pltpu.VMEM((2, 2, rows, 2 * hidden), BF16),
        pltpu.VMEM((2, rows, 2 * hidden), BF16),
        pltpu.VMEM((2, 3 * half, width), F32),
    )


def first(lengths, tokens, cotangent, norms, w_turned, w_out, w_in, w_down):
    size, shards = lax.axis_size("dp"), lax.axis_size("mp")
    rows, width = tokens.shape
    cols, hidden = w_out.shape[0], w_down.shape[0]
    heads, length = cols // HEAD_DIM, rows * shards
    chain = 3 * width // 2
    vmem = pl.BlockSpec(memory_space=pltpu.VMEM)
    hbm = pl.BlockSpec(memory_space=pl.ANY)
    dma = pltpu.SemaphoreType.DMA
    shape = jax.ShapeDtypeStruct
    along, table = shape((heads, LANES, length), BF16), shape((HEAD_DIM // 2, length), F32)
    wide = lambda dtype, *lead: pltpu.VMEM(lead + (rows, width), dtype)
    return pl.pallas_call(
        functools.partial(first_kernel, size),
        out_shape=(
            shape((rows, width), BF16),
            shape((rows, width), F32),
            shape((shards, rows, width), BF16),
            shape((8, width), F32),
            shape((2, chain, width), F32),
            shape((shards, rows, width), BF16),
            along,
            along,
            along,
            shape((heads, length, LANES), BF16),
            shape((shards, cols, rows), BF16),
            table,
            table,
        ),
        in_specs=[pl.BlockSpec(memory_space=pltpu.SMEM)] + [vmem] * 4 + [hbm] * 6,
        out_specs=[vmem] * 4 + [hbm] * 9,
        scratch_shapes=[
            wide(BF16, shards),
            pltpu.VMEM((2, width, 2 * hidden), BF16),
            pltpu.VMEM((2 * hidden, width), BF16),
            pltpu.VMEM((cols, width), BF16),
            pltpu.VMEM((shards, cols, rows), BF16),
            pltpu.VMEM((2, cols, rows), BF16),
            wide(BF16),
            wide(BF16),
            wide(BF16, 2),
            wide(F32),
            wide(F32),
            wide(F32),
            pltpu.VMEM((rows, LANES), F32),
            wide(BF16, 2),
            pltpu.VMEM((2, chain, width), BF16),
            pltpu.VMEM((2, chain, width), BF16),
            pltpu.VMEM((4, 8, width), F32),
            *ring_scratch(size, chain, width, RING_EARLY)[:2],
            pltpu.VMEM((8, width), F32),
            *ring_scratch(size, chain, width, RING_EARLY)[2:],
            dma((2, KINDS, 2)),
            dma((6,)),
            dma((8,)),
        ],
        compiler_params=pltpu.CompilerParams(
            collective_id=0, has_side_effects=True, vmem_limit_bytes=WIDE_LIMIT
        ),
        cost_estimate=pl.CostEstimate(
            flops=36 * rows * width * hidden, bytes_accessed=40 * rows * width, transcendentals=0
        ),
        name="first",
    )(lengths, tokens, cotangent, w_turned, w_out, w_in, w_down, *norms)


class Sum:
    def __init__(self, size, me, first, total, give, take, result, sems):
        orders = dp_orders(size)
        self.total, self.give, self.take, self.result, self.sems = total, give, take, result, sems
        halving, stages = halvings(size), size.bit_length() - 1
        count = 1 << (halving - first)
        self.rows = total.shape[1] // count
        base, low, peers = [], [0, 0], []
        for chain in range(2):
            peers.append([peer_of(me, bit) for bit in orders[chain]])
            base.append(sum(peers[chain][done][1] * (1 << (halving - 1 - done)) for done in range(first)))
        self.steps, spot = [], 0
        for stage in range(first, stages):
            halve = stage < halving
            part = count // 2 if halve else count
            step = dict(kind="halve" if halve else "swap", part=part, spot=spot, chains=[], last=stage + 1 == stages)
            for chain in range(2):
                peer, mine = peers[chain][stage]
                away = low[chain] + (1 - mine) * part if halve else low[chain]
                low[chain] = low[chain] + mine * part if halve else low[chain]
                step["chains"].append(dict(peer=peer, away=away, keep=low[chain], final=base[chain] + low[chain]))
            self.steps.append(step)
            spot, count = spot + part, part
        low = [base[chain] + low[chain] for chain in range(2)]
        for stage in reversed(range(halving)):
            step = dict(kind="gather", part=count, chains=[])
            for chain in range(2):
                peer, mine = peers[chain][stage]
                step["chains"].append(dict(peer=peer, away=low[chain]))
                low[chain] = low[chain] - mine * count
            self.steps.append(step)
            count *= 2

    def block(self, low, count):
        return pl.ds(pl.multiple_of(low * self.rows, 16), count * self.rows)

    def copy(self, index, chain):
        step = self.steps[index]
        one = step["chains"][chain]
        if step["kind"] == "gather":
            source = target = self.result.at[chain, self.block(one["away"], step["part"])]
        else:
            spot = pl.ds(step["spot"] * self.rows, step["part"] * self.rows)
            source, target = self.give.at[chain, spot], self.take.at[chain, spot]
        return pltpu.make_async_remote_copy(
            source,
            target,
            self.sems.at[0, chain, index],
            self.sems.at[1, chain, index],
            device_id={"dp": one["peer"]},
            device_id_type=MESH,
        )

    def start(self, index, chains=(0, 1)):
        step = self.steps[index]
        for chain in chains:
            if step["kind"] != "gather":
                spot = pl.ds(step["spot"] * self.rows, step["part"] * self.rows)
                away = self.block(step["chains"][chain]["away"], step["part"])
                self.give[chain, spot, :] = self.total[chain, away, :].astype(BF16)
            self.copy(index, chain).start()

    def finish(self, index):
        step = self.steps[index]
        for chain in range(2):
            self.copy(index, chain).wait()
            if step["kind"] == "gather":
                continue
            one = step["chains"][chain]
            spot = pl.ds(step["spot"] * self.rows, step["part"] * self.rows)
            keep = self.block(one["keep"], step["part"])
            mine = self.total[chain, keep, :] if step["kind"] == "halve" else self.give[chain, spot, :].astype(F32)
            value = mine + self.take[chain, spot, :].astype(F32)
            if step["last"]:
                self.result[chain, self.block(one["final"], 1), :] = value.astype(BF16)
            else:
                self.total[chain, keep, :] = value

    def advance(self, index):
        self.finish(index)
        if index + 1 < len(self.steps):
            self.start(index + 1)


def pieces_sent(size, first):
    halving = halvings(size)
    return (1 << (halving - first)) - 1 + size.bit_length() - 1 - halving


def back_kernel(
    size, att_ref, w_out_ref, cos_ref, sin_ref, norms_ref, w_ref, w_near_ref, dh_ref,
    total_hbm, slots_hbm, q_rows_hbm, q_hbm, k_hbm, v_hbm, x_hbm,
    dx_ref, grad_ref, big_ref, sums_ref,
    big, slots, q_rows_ref, q_ref, k_ref, v_ref, x_ref,
    do_ref, do_rows_ref, dq_ref, dk_ref, dv_ref, d_qkv,
    total, give, take, near, far_out, far_in, own, norm_in,
    ring_give, ring_take, ring_sems, gather_sems, loads, near_sem, far_sem, sum_sems, norm_sem,
):
    heads, _, tokens = k_ref.shape
    shards, rows, width = slots.shape
    cols = heads * HEAD_DIM
    half = HEAD_DIM // 2
    m, me = lax.axis_index("mp"), lax.axis_index("dp")
    stages = size.bit_length() - 1
    core, far = {"mp": peer_of(m, 0)[0]}, {"mp": peer_of(m, 1)[0]}
    partners = [core, far] + [{"dp": peer_of(me, bit)[0]} for bit in range(stages)]
    sources = [total_hbm, slots_hbm, q_rows_hbm, q_hbm, k_hbm, v_hbm, x_hbm]
    targets = [big, slots, q_rows_ref, q_ref, k_ref, v_ref, x_ref]
    fetches = [
        pltpu.make_async_copy(source, target, loads.at[n])
        for n, (source, target) in enumerate(zip(sources, targets))
    ]
    for fetch in fetches:
        fetch.start()
    ring = Ring(size, me, big, ring_give, ring_take, big_ref, ring_sems, gather_sems)
    greet(partners + [{"dp": peer} for peer in ring.peers])
    sums_ref[...] = norms_ref[...]
    small = Sum(size, me, 0, total, give, take, grad_ref, sum_sems)
    fetches[0].wait()
    for chain in range(2):
        ring.begin(RING_EARLY, chain)
    fetches[1].wait()
    events = 2 * (2 * ring.n - 2)
    first_event = 2 * RING_EARLY

    def prepare(i, carry):
        d_att = mm(w_out_ref[...], slots[i], NT).astype(BF16)
        do_ref[:, span(i, rows)] = d_att
        products = d_att.astype(F32) * att_ref[i].astype(F32)
        for h in range(heads):
            mine = slice(h * HEAD_DIM, (h + 1) * HEAD_DIM)
            dot = jnp.sum(products[mine], axis=0, keepdims=True)
            wide = [d_att[mine].astype(F32), thirds(-dot), jnp.zeros((LANES - HEAD_DIM - 16, rows), F32)]
            do_rows_ref[h, span(i, rows), :] = jnp.concatenate(wide, axis=0).T.astype(BF16)
        return carry

    lax.fori_loop(0, shards, prepare, 0)
    dq_ref[...] = jnp.zeros_like(dq_ref)
    for fetch in fetches[2:]:
        fetch.wait()

    def rotated_back(values, cosine, sine):
        first, second = values[:half], values[half:]
        return [first * cosine + second * sine, second * cosine - first * sine]

    def over_keys(j, carry):
        keys = span(j, rows)
        dk_ref[...] = jnp.zeros_like(dk_ref)
        dv_ref[...] = jnp.zeros_like(dv_ref)

        def over_queries(i, carry):
            queries = span(i, rows)
            for h in range(heads):
                k = k_ref[h, :, keys]
                probs = jnp.exp2(mm(q_rows_ref[h, queries, :], k))
                d_scores = (probs * mm(do_rows_ref[h, queries, :], v_ref[h, :, keys])).astype(BF16)
                dv_ref[h] += mm(do_ref[h * HEAD_DIM : (h + 1) * HEAD_DIM, queries], probs.astype(BF16))
                dk_ref[h] += mm(q_ref[h, :HEAD_DIM, queries], d_scores)
                dq_ref[h, :, queries] += mm(k[:HEAD_DIM], d_scores, NT)
            number = first_event + j * shards + i
            pl.when(number < events)(lambda: ring.event(number))
            return carry

        lax.fori_loop(0, shards, over_queries, 0)
        cosine, sine = cos_ref[:, keys] * (1.0 / LOG2E), sin_ref[:, keys] * (1.0 / LOG2E)
        pieces = []
        for h in range(heads):
            pieces += rotated_back(dk_ref[h], cosine, sine)
        pieces += [dv_ref[h] for h in range(heads)]
        d_qkv[j, cols:, :] = jnp.concatenate(pieces, axis=0).astype(BF16)
        return carry

    lax.fori_loop(0, shards, over_keys, 0)
    first_event = min(first_event + shards * shards, events)
    for i in range(shards):
        scale = 1.0 / math.sqrt(HEAD_DIM)
        cosine, sine = cos_ref[:, span(i, rows)] * scale, sin_ref[:, span(i, rows)] * scale
        pieces = []
        for h in range(heads):
            pieces += rotated_back(dq_ref[h, :, span(i, rows)], cosine, sine)
        d_qkv[i, :cols, :] = jnp.concatenate(pieces, axis=0).astype(BF16)
    near_copies = [send(d_qkv.at[2 * i + 1], near.at[i], near_sem.at[0, i], near_sem.at[1, i], core) for i in range(2)]

    def product(first, count):
        piece = mm(d_qkv[0, first : first + count, :], x_ref[0])
        for slot in range(1, shards):
            piece += mm(d_qkv[slot, first : first + count, :], x_ref[slot])
        return piece

    chain_rows = total.shape[1]
    total[0] = product(0, chain_rows)
    total[1, :cols, :] = product(chain_rows, cols)
    piece = mm(att_ref[0], slots[0])
    for slot in range(1, shards):
        piece += mm(att_ref[slot], slots[slot])
    total[1, cols:, :] = piece
    small.start(0)

    def norm_exchange(stage):
        return send(sums_ref, norm_in.at[stage], norm_sem.at[0, stage], norm_sem.at[1, stage], partners[stage])

    norm_copy, norm_done = norm_exchange(0), 0
    for copy in near_copies:
        copy.wait()

    def d_tokens(index):
        return mm(d_qkv[2 * index], w_ref[...], TN) + mm(near[index], w_near_ref[...], TN)

    far_out[...] = d_tokens(1).astype(BF16)
    far_copy = send(far_out, far_in, far_sem.at[0], far_sem.at[1], far)
    own[...] = dh_ref[...] + d_tokens(0)

    left, share = first_event, -(-(events - first_event) // len(small.steps))
    small_done = 0
    while small_done < len(small.steps) or norm_done < len(partners):
        if small_done < len(small.steps):
            small.advance(small_done)
            small_done += 1
            for number in range(left, min(left + share, events)):
                ring.event(number)
            left = min(left + share, events)
        if norm_done < len(partners):
            norm_copy.wait()
            sums_ref[...] += norm_in[norm_done]
            norm_done += 1
            if norm_done < len(partners):
                norm_copy = norm_exchange(norm_done)
    far_copy.wait()
    dx_ref[...] = (own[...] + far_in[...].astype(F32)).astype(BF16)


def back(att, w_out, cosine, sine, norms, w_turned, w_near, dh, totals, dh_slots, q_rows, q, k, v, x_slots):
    size = lax.axis_size("dp")
    stages = size.bit_length() - 1
    heads, _, tokens = q.shape
    shards, rows, width = x_slots.shape
    cols = w_turned.shape[0]
    chain, big_chain = width // 2, totals.shape[1]
    sent = pieces_sent(size, 0) * (chain >> halvings(size))
    spots = min(RING_PIECES, size)
    ring_steps = spots - 1 + (size // spots).bit_length() - 1
    steps = stages + halvings(size)
    vmem = pl.BlockSpec(memory_space=pltpu.VMEM)
    hbm = pl.BlockSpec(memory_space=pl.ANY)
    dma = pltpu.SemaphoreType.DMA
    along = pltpu.VMEM((heads, LANES, tokens), BF16)
    return pl.pallas_call(
        functools.partial(back_kernel, size),
        out_shape=(
            jax.ShapeDtypeStruct((rows, width), BF16),
            jax.ShapeDtypeStruct((2, chain, width), BF16),
            jax.ShapeDtypeStruct((2, big_chain, width), BF16),
            jax.ShapeDtypeStruct(norms.shape, F32),
        ),
        in_specs=[vmem] * 8 + [hbm] * 7,
        out_specs=[vmem] * 4,
        scratch_shapes=[
            pltpu.VMEM(totals.shape, F32),
            pltpu.VMEM(dh_slots.shape, BF16),
            pltpu.VMEM((heads, tokens, LANES), BF16),
            along,
            along,
            along,
            pltpu.VMEM(x_slots.shape, BF16),
            pltpu.VMEM((heads * HEAD_DIM, tokens), BF16),
            pltpu.VMEM((heads, tokens, LANES), BF16),
            pltpu.VMEM((heads, HEAD_DIM, tokens), F32),
            pltpu.VMEM((heads, HEAD_DIM, rows), F32),
            pltpu.VMEM((heads, HEAD_DIM, rows), F32),
            pltpu.VMEM((shards, cols, rows), BF16),
            pltpu.VMEM((2, chain, width), F32),
            pltpu.VMEM((2, sent, width), BF16),
            pltpu.VMEM((2, sent, width), BF16),
            pltpu.VMEM((2, cols, rows), BF16),
            pltpu.VMEM((rows, width), BF16),
            pltpu.VMEM((rows, width), BF16),
            pltpu.VMEM((rows, width), F32),
            pltpu.VMEM((2 + stages,) + norms.shape, F32),
            *ring_scratch(size, big_chain, width, ring_steps),
            dma((2, 2, 2, spots - 1)),
            dma((7,)),
            dma((2, 2)),
            dma((2,)),
            dma((2, 2, steps)),
            dma((2, 2 + stages)),
        ],
        compiler_params=pltpu.CompilerParams(
            collective_id=1, has_side_effects=True, vmem_limit_bytes=WIDE_LIMIT
        ),
        cost_estimate=pl.CostEstimate(
            flops=5 * heads * tokens * tokens * LANES, bytes_accessed=60 * rows * width, transcendentals=0
        ),
        name="back",
    )(att, w_out, cosine, sine, norms, w_turned, w_near, dh, totals, dh_slots, q_rows, q, k, v, x_slots)


def emit_kernel(big_ref, small_ref, out_ref, dx_ref, gate_up_hbm, down_ref, qkv_ref, w_out_ref, out_copy_ref, dx_copy_ref, wide, sems):
    step, steps = pl.program_id(0), pl.num_programs(0)
    rows = down_ref.shape[0]

    def copies(which):
        return [
            pltpu.make_async_copy(wide.at[which, n], gate_up_hbm.at[span(which, rows), n, :], sems.at[which, n])
            for n in range(2)
        ]

    for n in range(2):
        wide[step, n] = big_ref[0, n].astype(F32)
    for copy in copies(step):
        copy.start()
    down_ref[...] = big_ref[0, 2].astype(F32)
    out_copy_ref[...] = out_ref[...]
    dx_copy_ref[...] = dx_ref[...]
    qkv_steps = steps * 3 // 4

    @pl.when(step < qkv_steps)
    def _():
        qkv_ref[...] = small_ref[0].astype(F32)

    @pl.when(step >= qkv_steps)
    def _():
        w_out_ref[...] = small_ref[0].astype(F32)

    @pl.when(step == steps - 1)
    def _():
        for which in range(steps):
            for copy in copies(which):
                copy.wait()


def emit(big, small, output, d_tokens):
    _, chain, width = small.shape
    steps = 4
    per, rows = steps // 2, width // steps
    qkv_steps = steps * 3 // 4
    tokens = output.shape[0] // steps
    shape = lambda *dims: jax.ShapeDtypeStruct(dims, F32)
    low = jax.ShapeDtypeStruct(output.shape, BF16)
    few = pl.BlockSpec((tokens, width), lambda i: (i, 0))
    return pl.pallas_call(
        emit_kernel,
        out_shape=(
            shape(width, 2, width),
            shape(width, width),
            shape(qkv_steps * rows, width),
            shape((steps - qkv_steps) * rows, width),
            low,
            low,
        ),
        grid=(steps,),
        in_specs=[
            pl.BlockSpec((1, 3, rows, width), lambda i: (i // per, 0, i % per, 0)),
            pl.BlockSpec((1, rows, width), lambda i: (i // per, i % per, 0)),
            few,
            few,
        ],
        out_specs=[
            pl.BlockSpec(memory_space=pl.ANY),
            pl.BlockSpec((rows, width), lambda i: (i, 0)),
            pl.BlockSpec((rows, width), lambda i: (jnp.minimum(i, qkv_steps - 1), 0)),
            pl.BlockSpec((rows, width), lambda i: (jnp.maximum(i - qkv_steps, 0), 0)),
            few,
            few,
        ],
        scratch_shapes=[pltpu.VMEM((steps, 2, rows, width), F32), pltpu.SemaphoreType.DMA((steps, 2))],
        compiler_params=pltpu.CompilerParams(vmem_limit_bytes=VMEM_LIMIT),
        cost_estimate=pl.CostEstimate(flops=0, bytes_accessed=24 * width * width, transcendentals=0),
        name="emit",
    )(big.reshape(2, 3, chain, width), small, output, d_tokens)


def body(
    tokens, lengths, w_qkv, w_out, w_gate_up, w_down, ln1_scale, ln1_shift, ln2_scale, ln2_shift, cotangent
):
    rows, width = tokens.shape
    shards = lax.axis_size("mp")
    local_cols = w_out.shape[0]
    hidden_cols = w_down.shape[0]
    m = lax.axis_index("mp")
    qkv_turned = w_qkv.transpose(1, 2, 0).reshape(3 * local_cols, width)
    qkv_near = lax.ppermute(qkv_turned, "mp", [(i, i ^ 1) for i in range(shards)])
    norms = (ln1_scale, ln1_shift, ln2_scale, ln2_shift)
    output, dh, dh_slots, norms, totals, x_slots, q, k, v, q_rows, att, cosine, sine = first(
        lengths, tokens, cotangent, norms, qkv_turned, w_out, w_gate_up, w_down
    )
    d_tokens, small, big, norms = back(
        att, w_out, cosine, sine, norms, qkv_turned, qkv_near, dh, totals, dh_slots, q_rows, q, k, v, x_slots
    )
    grad_gate_up, grad_down, grad_qkv, grad_out, output, d_tokens = emit(big, small, output, d_tokens)
    grad_qkv = grad_qkv.reshape(3, local_cols, width).transpose(2, 0, 1)
    norms = lax.dynamic_slice_in_dim(norms, m * local_cols, local_cols, 1)
    return (
        output,
        d_tokens,
        grad_qkv,
        grad_out,
        grad_gate_up,
        grad_down,
        norms[0],
        norms[1],
        norms[2],
        norms[3],
    )


def solution(mesh):
    return jax.shard_map(
        body,
        mesh=mesh,
        in_specs=(
            P(("dp", "mp"), None),
            P("dp", None),
            P(None, None, "mp"),
            P("mp", None),
            P(None, None, "mp"),
            P("mp", None),
            P(),
            P(),
            P(),
            P(),
            P(("dp", "mp"), None),
        ),
        out_specs=(
            P(("dp", "mp"), None),
            P(("dp", "mp"), None),
            P(None, None, "mp"),
            P("mp", None),
            P(None, None, "mp"),
            P("mp", None),
            P("mp"),
            P("mp"),
            P("mp"),
            P("mp"),
        ),
        check_vma=False,
    )
```
